128 devices in a mesh: req: 16 (over z, y), tp: 8 (over x, core).
Axes of the slice: x: 4, y: 4, z: 4, core: 2. Of those that a mesh axis runs over, the one named last changes fastest.
Arguments:
- hidden_in: bfloat16 [4096, 1024], P('req'), may hold values from -42 to 42
- prompt_kv: bfloat16 [2, 128, 512, 1024], P(None, 'req', None, 'tp'), may hold values from -9 to 9
- tail_kv: bfloat16 [2, 4096, 64, 1024], P(None, 'req', None, 'tp'), may hold values from -9 to 9
- group_of: int32 [4096], P('req'), may hold values from 0 to 7
- prompt_len: int32 [128], P('req'), may hold values from 64 to 512, as said below
- tail_len: int32 [4096], P('req'), may hold values from 0 to 63, as said below
- bucket_of: int32 [577], replicated, may hold values from 0 to 31, never falling along the last dimension, each value on 1 to 38 neighbouring positions
- bias_table: float32 [32, 16], P(None, 'tp'), may hold values from -6 to 302
- attn_gain: float32 [1024], replicated, may hold values from 0.1 to 1.9
- w_query: bfloat16 [1024, 1024], P(None, 'tp'), may hold values from -0.1875 to 0.1875
- w_key: bfloat16 [1024, 1024], P(None, 'tp'), may hold values from -0.1875 to 0.1875
- w_value: bfloat16 [1024, 1024], P(None, 'tp'), may hold values from -0.1875 to 0.1875
- w_out: bfloat16 [1024, 1024], P('tp'), may hold values from -0.75 to 0.75
- ffn_gain: float32 [1024], replicated, may hold values from 0.1 to 1.9
- router_weight: bfloat16 [1024, 16], replicated, may hold values from -0.1875 to 0.1875
- expert_ids: int32 [4096, 2], P('req'), may hold values from 0 to 15, all different within a row; in each aligned block of 256 rows (0 to 255, 256 to 511, ...) at most 40 rows name the same one
- w_gate: bfloat16 [16, 1024, 2816], P('req', None, 'tp'), may hold values from -0.1875 to 0.1875
- w_up: bfloat16 [16, 1024, 2816], P('req', None, 'tp'), may hold values from -0.1875 to 0.1875
- w_down: bfloat16 [16, 2816, 1024], P('req', 'tp'), may hold values from -0.109375 to 0.109375
- new_slot: int32 [4096], replicated, may hold values from 0 to 4095, as said below
Outputs:
- out_hidden: bfloat16 [4096, 1024], P('req')
- new_tail_kv: bfloat16 [2, 4096, 64, 1024], P(None, 'req', None, 'tp')
The draws below stay inside these ranges and needn't reach their ends.
Inputs may be any that keep to these rules, and one draw needn't show every extreme that they name: `expert_ids`: in each replica's aligned block of 256 tokens no expert is named by more than 40 of them, a bound that some block reaches. `new_slot`: A permutation. Exactly 4 requests of each replica are movers; all movers of one replica go to one replica (possibly itself), each taking a slot that a mover of that replica leaves; every other request keeps its slot. `prompt_len`: each replica has a group of 512 rows. `tail_len`: each replica has a request of 63 own rows and one of none.
All inputs are finite; a program needn't handle non-finite values.
Results may differ from the reference program's by a relative error of at most 0.013.
Values may be sent and summed in bfloat16 or wider, within the bound.
A program may use at most 128 MiB of HBM per device.

```python
import math
import jax
import jax.numpy as jnp
import numpy as np
from jax import lax

D = 1024
HEADS = 16
HD = 64
FF = 2816
BUCKETS = 32
TOP = 2
R_DEV = 256
G_DEV = 8
PRE = 512
TAIL = 64
MIG = 4
EXPERTS = 16
CAP = 40
REQS = 4096
GROUPS = 128
MAXDIST = 577
N_REQ = 16


def draw_hidden_in(key, part):
    k1, k2, k3 = jax.random.split(jax.random.fold_in(key, 5), 3)
    row_scale = jnp.exp(jax.random.uniform(k1, (REQS, 1), minval=math.log(0.4), maxval=math.log(4.0)))
    col_scale = jnp.exp(jax.random.uniform(k2, (1, D), minval=math.log(0.6), maxval=math.log(1.7)))
    base = jnp.clip(jax.random.normal(k3, (REQS, D)), -6.0, 6.0)
    return (base * row_scale * col_scale).astype(jnp.float32).astype(jnp.bfloat16)


def draw_prompt_len(key, part):
    k1, k2 = jax.random.split(jax.random.fold_in(key, 3))
    lens = jax.random.randint(k1, (N_REQ, G_DEV), PRE // 8, PRE + 1)
    order = jax.vmap(lambda k: jax.random.permutation(k, G_DEV))(jax.random.split(k2, N_REQ))
    cols = jnp.arange(G_DEV)[None, :]
    lens = jnp.where(cols == order[:, :1], PRE, lens)
    lens = jnp.where(cols == order[:, 1:2], PRE // 8, lens)
    return lens.reshape(-1).astype(jnp.int32)


def draw_tail_len(key, part):
    k1, k2 = jax.random.split(jax.random.fold_in(key, 4))
    lens = jax.random.randint(k1, (N_REQ, R_DEV), 0, TAIL)
    order = jax.vmap(lambda k: jax.random.permutation(k, R_DEV))(jax.random.split(k2, N_REQ))
    cols = jnp.arange(R_DEV)[None, :]
    lens = jnp.where(cols == order[:, :1], TAIL - 1, lens)
    lens = jnp.where(cols == order[:, 1:2], 0, lens)
    return lens.reshape(-1).astype(jnp.int32)


def draw_bias_table(key, part):
    k1 = jax.random.fold_in(jax.random.fold_in(key, 7), 0)
    return jnp.clip(1.5 * jax.random.normal(k1, (BUCKETS, HEADS)), -6.0, 6.0).astype(jnp.float32)


def draw_new_slot(key, part):
    k1, k2 = jax.random.split(jax.random.fold_in(key, 11))
    order = jax.vmap(lambda k: jax.random.permutation(k, R_DEV))(jax.random.split(k1, N_REQ))
    movers = order[:, :MIG].astype(jnp.int32)
    dest = jax.random.permutation(k2, N_REQ).astype(jnp.int32)
    base = jnp.arange(N_REQ, dtype=jnp.int32)[:, None] * R_DEV
    sources = (base + movers).reshape(-1)
    targets = (dest[:, None] * R_DEV + movers[dest]).reshape(-1)
    slots = jnp.arange(REQS, dtype=jnp.int32)
    return slots.at[sources].set(targets.astype(jnp.int32))


def set_ends(entries, stream_key, least, top_value):
    extent = entries.shape
    place = [jax.random.randint(jax.random.fold_in(stream_key, axis), (), 0, extent[axis]) for axis in range(len(extent))]
    entries = entries.at[tuple(place)].set(least)
    longest = extent.index(max(extent))
    place[longest] = (place[longest] + 1) % extent[longest]
    return entries.at[tuple(place)].set(top_value)


def shard_levels(own_key, extent, cuts, smallest, top_value):
    factor_of, own = 1.0, jax.random.fold_in(own_key, 6)
    for dim, parts in cuts:
        steps = jnp.exp(jax.random.uniform(jax.random.fold_in(own, dim), (parts,), jnp.float32, smallest / len(cuts), top_value / len(cuts)))
        factor_of = factor_of * jnp.repeat(steps, extent[dim] // parts).reshape([-1 if axis == dim else 1 for axis in range(len(extent))])
    return factor_of


def split_up(number_of, total, reach, lean):
    weights = [(1 << 20) // math.isqrt(rank ** lean) + 1 for rank in range(2, number_of + 1)]
    spare, counts = total - reach - (number_of - 1), [1] * (number_of - 1)
    while spare > 0:
        candidates = [i for i in range(number_of - 1) if counts[i] < reach]
        whole, budget = sum([weights[i] for i in candidates]), spare
        for i in candidates:
            extra = min(reach - counts[i], max(1, budget * weights[i] // whole), spare)
            counts[i] = counts[i] + extra
            spare = spare - extra
    return np.array([reach] + counts)


def ragged_sizes(rng, count, total, most, lean):
    if count == 2:
        one = jax.random.randint(rng, (), max(1, total - most), min(most, total - 1) + 1)
        return jnp.stack([one, total - one])
    lengths = jnp.asarray(split_up(count, total, most, lean), jnp.int32)
    twos = (count - 1) // 2
    donor, taker = lengths[1:1 + 2 * twos:2], lengths[2:2 + 2 * twos:2]
    slack = jnp.minimum(donor - 1, most - taker)
    moved = jax.random.randint(jax.random.fold_in(rng, 1), (twos,), 0, 1 << 20) % (slack + 1)
    lengths = lengths.at[1:1 + 2 * twos:2].set(donor - moved).at[2:2 + 2 * twos:2].set(taker + moved)
    return lengths[jax.random.permutation(jax.random.fold_in(rng, 2), count)]


def assign_block(own_key, own, number, rows, count, top, most, lean):
    order = jax.random.permutation(own_key, count)
    packed, ordinary = portions_of(count, rows * top, most, lean, True), portions_of(count, rows * top, most, lean, False)
    places = jnp.arange(count)

    def named(tallies, offset_by):
        used = int((tallies > 0).sum())
        fixed = max(1, used // 4)
        moved = fixed + (places - fixed + offset_by * (used - fixed)) % max(1, count - fixed)
        return jnp.zeros((count,), jnp.int32).at[order[jnp.where(places < fixed, places, moved)]].set(jnp.asarray(tallies, jnp.int32))

    tallies = jnp.where(number % 4 == 0, named(packed, number // 4), named(ordinary, number - number // 4 - 1))
    mixed = jax.random.permutation(jax.random.fold_in(own, 3), count)
    giver, receiver = mixed[0:count // 2 * 2:2], mixed[1:count // 2 * 2:2]
    margin = jnp.minimum(tallies[giver] - 1, most - tallies[receiver]) // 2
    margin = jnp.where((giver == order[0]) | (receiver == order[0]) | (tallies[receiver] == 0), 0, jnp.maximum(margin, 0))
    moved = jax.random.randint(jax.random.fold_in(own, 4), (count // 2,), 0, 1 << 20) % (margin + 1)
    tallies = tallies.at[giver].add(-moved).at[receiver].add(moved)
    labels = jnp.searchsorted(jnp.cumsum(tallies), jnp.arange(rows * top), side="right").astype(jnp.int32)
    grid = labels.reshape(top, rows).T
    grid = grid[jax.random.permutation(jax.random.fold_in(own, 1), rows)]
    offset_by = jax.random.randint(jax.random.fold_in(own, 2), (rows, 1), 0, top)
    return jnp.take_along_axis(grid, (jnp.arange(top)[None, :] + offset_by) % top, axis=1)


def portions_of(amount, total, reach, skew, full):
    weights = [(1 << 20) // math.isqrt(standing ** skew) + 1 for standing in range(1, amount + 1)]
    largest = reach if full else min(reach, max(-(-total // amount), total * weights[0] // sum(weights)))
    least = 1 if total - largest >= amount - 1 else 0
    holding, surplus = [largest] + [least] * (amount - 1), total - largest - least * (amount - 1)
    while surplus > 0:
        candidates = [i for i in range(1, amount) if holding[i] < largest] or [i for i in range(1, amount) if holding[i] < reach]
        pool, budget = sum([weights[i] for i in candidates]), surplus
        for i in candidates:
            addition = min(reach - holding[i], max(1, budget * weights[i] // pool), surplus)
            holding[i] = holding[i] + addition
            surplus = surplus - addition
    return np.array(holding)


def noise(stream_key, dims, deviation, limit, cuts=(), held_as=jnp.bfloat16):
    entries = jax.random.normal(stream_key, dims, jnp.float32) * deviation
    if len(cuts) > 0:
        entries = shard_levels(stream_key, dims, cuts, -0.22, 0.18) * entries
    return jnp.clip(entries, min=-limit, max=limit).astype(held_as)


def setup_inputs(seed: int = 0) -> dict:
    keys = jax.random.split(jax.random.key(seed), 21)
    hidden_in = draw_hidden_in(jax.random.fold_in(keys[20], 71), 0)
    prompt_kv = noise(keys[1], (2, GROUPS, PRE, HEADS * HD), 1.5, 9.0, ((1, 16), (3, 8)))
    tail_kv = noise(keys[2], (2, REQS, TAIL, HEADS * HD), 1.5, 9.0, ((1, 16), (3, 8)))
    group_of = set_ends(jax.random.randint(keys[3], (REQS,), 0, G_DEV), jax.random.fold_in(keys[3], 1), 0, G_DEV - 1).astype(jnp.int32)
    prompt_len = draw_prompt_len(jax.random.fold_in(keys[20], 71), 0)
    tail_len = draw_tail_len(jax.random.fold_in(keys[20], 71), 0)
    bucket_of = jnp.searchsorted(jnp.cumsum(ragged_sizes(keys[6], BUCKETS, MAXDIST, (PRE + TAIL + BUCKETS) // BUCKETS * 2, 2)), jnp.arange(MAXDIST), side="right").astype(jnp.int32)
    bias_table = draw_bias_table(jax.random.fold_in(keys[20], 71), 0)
    attn_gain = jnp.clip(1.0 + 0.18 * jax.random.normal(keys[8], (D,), jnp.float32), 0.1, 1.9)
    w_query = noise(keys[9], (D, HEADS * HD), D ** -0.5, 0.1875, ((1, 8),))
    w_key = noise(keys[10], (D, HEADS * HD), D ** -0.5, 0.1875, ((1, 8),))
    w_value = noise(keys[11], (D, HEADS * HD), D ** -0.5, 0.1875, ((1, 8),))
    w_out = noise(keys[12], (HEADS * HD, D), HD ** -0.5, 0.75, ((0, 8),))
    ffn_gain = jnp.clip(1.0 + 0.18 * jax.random.normal(keys[13], (D,), jnp.float32), 0.1, 1.9)
    router_weight = noise(keys[14], (D, EXPERTS), D ** -0.5, 0.1875)
    expert_ids_keys = jax.random.split(jax.random.fold_in(keys[15], 1), REQS // R_DEV)
    expert_ids_turns = jax.random.permutation(jax.random.fold_in(keys[15], 3), REQS // R_DEV)
    expert_ids = jax.vmap(lambda own, number: assign_block(jax.random.fold_in(keys[15], 2), own, number, R_DEV, EXPERTS, TOP, CAP, 2))(expert_ids_keys, expert_ids_turns).reshape((REQS, TOP))
    w_gate = noise(keys[16], (EXPERTS, D, FF), D ** -0.5, 0.1875, ((0, 16), (2, 8)))
    w_up = noise(keys[17], (EXPERTS, D, FF), D ** -0.5, 0.1875, ((0, 16), (2, 8)))
    w_down = noise(keys[18], (EXPERTS, FF, D), FF ** -0.5, 0.109375, ((0, 16), (1, 8)))
    new_slot = draw_new_slot(jax.random.fold_in(keys[20], 71), 0)
    return {"hidden_in": hidden_in, "prompt_kv": prompt_kv, "tail_kv": tail_kv, "group_of": group_of, "prompt_len": prompt_len, "tail_len": tail_len, "bucket_of": bucket_of, "bias_table": bias_table, "attn_gain": attn_gain, "w_query": w_query, "w_key": w_key, "w_value": w_value, "w_out": w_out, "ffn_gain": ffn_gain, "router_weight": router_weight, "expert_ids": expert_ids, "w_gate": w_gate, "w_up": w_up, "w_down": w_down, "new_slot": new_slot}


EPS = 1e-06

def rms_scale(values, gain):
    v = values.astype(jnp.float32)
    return (v * lax.rsqrt(lax.optimization_barrier(jnp.mean(v * v, axis=-1, keepdims=True)) + EPS) * gain).astype(jnp.bfloat16)

def round_keep(values):
    return lax.optimization_barrier(values.astype(jnp.bfloat16)).astype(jnp.float32)

def reference(hidden_in, prompt_kv, tail_kv, group_of, prompt_len, tail_len, bucket_of, bias_table, attn_gain, w_query, w_key, w_value, w_out, ffn_gain, router_weight, expert_ids, w_gate, w_up, w_down, new_slot):
    dist_bias = bias_table[bucket_of]
    scale = HD ** (-0.5)

    def one_replica(index):
        start_req = (index * R_DEV).astype(jnp.int32)
        start_grp = (index * G_DEV).astype(jnp.int32)
        rows_in = lax.dynamic_slice_in_dim(hidden_in, start_req, R_DEV, 0)
        prompts = lax.dynamic_slice_in_dim(prompt_kv, start_grp, G_DEV, 1)
        tails = lax.dynamic_slice_in_dim(tail_kv, start_req, R_DEV, 1)
        groups = lax.dynamic_slice_in_dim(group_of, start_req, R_DEV, 0)
        plens = lax.dynamic_slice_in_dim(prompt_len, start_grp, G_DEV, 0)
        tlens = lax.dynamic_slice_in_dim(tail_len, start_req, R_DEV, 0)
        normed = rms_scale(rows_in, attn_gain)
        query = jnp.dot(normed, w_query, preferred_element_type=jnp.float32).astype(jnp.bfloat16)
        key_new = jnp.dot(normed, w_key, preferred_element_type=jnp.float32).astype(jnp.bfloat16)
        value_new = jnp.dot(normed, w_value, preferred_element_type=jnp.float32).astype(jnp.bfloat16)
        q = query.astype(jnp.float32).reshape(R_DEV, HEADS, HD)
        pk = prompts[0].astype(jnp.float32).reshape(G_DEV, PRE, HEADS, HD)
        pv = prompts[1].astype(jnp.float32).reshape(G_DEV, PRE, HEADS, HD)
        tk = tails[0].astype(jnp.float32).reshape(R_DEV, TAIL, HEADS, HD)
        tv = tails[1].astype(jnp.float32).reshape(R_DEV, TAIL, HEADS, HD)
        kn = key_new.astype(jnp.float32).reshape(R_DEV, HEADS, HD)
        vn = value_new.astype(jnp.float32).reshape(R_DEV, HEADS, HD)
        own_len = plens[groups]
        pos = own_len + tlens
        jpos = jnp.arange(PRE, dtype=jnp.int32)
        pidx = jnp.clip(pos[:, None] - jpos[None, :], 0, MAXDIST - 1)
        pbias = jnp.transpose(dist_bias[pidx], (2, 0, 1))
        pmask = (jnp.arange(G_DEV, dtype=jnp.int32)[None, :, None] == groups[:, None, None]) & (jpos[None, None, :] < own_len[:, None, None])
        ps = jnp.einsum('rhd,gjhd->hrgj', q, pk) * scale + pbias[:, :, None, :]
        ps = jnp.where(pmask[None], ps, -jnp.inf)
        tpos = jnp.arange(TAIL, dtype=jnp.int32)
        tidx = jnp.clip(tlens[:, None] - tpos[None, :], 0, MAXDIST - 1)
        tbias = jnp.transpose(dist_bias[tidx], (2, 0, 1))
        tmask = tpos[None, :] < tlens[:, None]
        ts = jnp.einsum('rhd,rthd->hrt', q, tk) * scale + tbias
        ts = jnp.where(tmask[None], ts, -jnp.inf)
        ns = jnp.einsum('rhd,rhd->hr', q, kn) * scale + dist_bias[0][:, None]
        top = jnp.maximum(jnp.maximum(lax.optimization_barrier(jnp.max(ps, axis=(2, 3))), lax.optimization_barrier(jnp.max(ts, axis=2))), ns)
        pe = jnp.exp(ps - top[:, :, None, None])
        te = jnp.exp(ts - top[:, :, None])
        ne = jnp.exp(ns - top)
        total = lax.optimization_barrier(jnp.sum(pe, axis=(2, 3))) + lax.optimization_barrier(jnp.sum(te, axis=2)) + ne
        pw = round_keep(pe / total[:, :, None, None])
        tw = round_keep(te / total[:, :, None])
        nw = round_keep(ne / total)
        head = jnp.einsum('hrgj,gjhd->rhd', pw, pv) + jnp.einsum('hrt,rthd->rhd', tw, tv) + jnp.einsum('hr,rhd->rhd', nw, vn)
        head_out = head.reshape(R_DEV, HEADS * HD).astype(jnp.bfloat16)
        attn = jnp.dot(head_out, w_out, preferred_element_type=jnp.float32)
        resid = (rows_in.astype(jnp.float32) + attn).astype(jnp.bfloat16)
        return (resid, key_new, value_new)
    resid, key_new, value_new = lax.map(one_replica, jnp.arange(N_REQ, dtype=jnp.int32))
    resid = resid.reshape(REQS, D)
    key_new = key_new.reshape(REQS, HEADS * HD)
    value_new = value_new.reshape(REQS, HEADS * HD)
    normed2 = rms_scale(resid, ffn_gain)
    logits = jnp.dot(normed2, router_weight, preferred_element_type=jnp.float32)
    picked = jnp.take_along_axis(logits, expert_ids, axis=1)
    gate_first = jax.nn.sigmoid(picked[:, 0] - picked[:, 1])
    flat_e = expert_ids.reshape(-1)
    onehot = (flat_e[:, None] == jnp.arange(EXPERTS, dtype=jnp.int32)[None, :]).astype(jnp.int32)
    per = onehot.reshape(N_REQ, R_DEV * TOP, EXPERTS)
    pos = lax.optimization_barrier(jnp.sum((jnp.cumsum(per, axis=1) - 1) * per, axis=2)).reshape(-1)
    pair = jnp.arange(REQS * TOP, dtype=jnp.int32)
    slot = pair // (R_DEV * TOP) * CAP + pos
    tok_table = jnp.zeros((EXPERTS, N_REQ * CAP), jnp.int32).at[flat_e, slot].set(pair // TOP)
    used = jnp.zeros((EXPERTS, N_REQ * CAP), jnp.int32).at[flat_e, slot].set(1)

    def one_expert(items):
        wg, wu, wd, tok, live = items
        rows = jnp.where(live[:, None] > 0, normed2[tok], jnp.zeros((), jnp.bfloat16))
        gate_h = jnp.dot(rows, wg, preferred_element_type=jnp.float32)
        up_h = jnp.dot(rows, wu, preferred_element_type=jnp.float32)
        act = (jax.nn.gelu(gate_h, approximate=True) * up_h).astype(jnp.bfloat16)
        return jnp.dot(act, wd, preferred_element_type=jnp.float32).astype(jnp.bfloat16)
    outputs = lax.map(one_expert, (w_gate, w_up, w_down, tok_table, used))
    pair_out = outputs[flat_e, slot].astype(jnp.float32).reshape(REQS, TOP, D)
    mixed = (resid.astype(jnp.float32) + gate_first[:, None] * pair_out[:, 0] + (1.0 - gate_first)[:, None] * pair_out[:, 1]).astype(jnp.bfloat16)
    everyone = jnp.arange(REQS, dtype=jnp.int32)
    tail_new = tail_kv.at[0, everyone, tail_len].set(key_new).at[1, everyone, tail_len].set(value_new)
    out_hidden = jnp.zeros_like(mixed).at[new_slot].set(mixed)
    new_tail_kv = jnp.zeros_like(tail_new).at[:, new_slot].set(tail_new)
    return (out_hidden, new_tail_kv)
```

```python
import functools
import jax
import jax.numpy as jnp
from jax import lax
from jax.experimental import pallas as pl
from jax.experimental.pallas import tpu as pltpu
from jax.sharding import PartitionSpec as P

F32 = jnp.float32
BF16 = jnp.bfloat16
EPS = 1e-06
NEG = -1e30
RB = 32
TOP = 2
MIG = 4


def col_form(row):
    n = row.shape[1]
    return jnp.transpose(jnp.broadcast_to(row.astype(F32), (128, n)))


def attn_kernel(
    tl_s, st_s, tab_s, plen_s, send_s,
    hid_ref, gain_ref, wq_ref, wk_ref, wv_ref, grp_ref, tlr_ref, ids_ref, pkv_ref, tail_ref, tail_any,
    tail_out, head_ref, send_ref, slot_ref,
    q16, kvn, lhs, kcat, sco, prob, posb, plb, tlb, tbias, opart, mpart, lpart, sems,
):
    step = pl.program_id(0)
    nsteps = pl.num_programs(0)
    rows = hid_ref.shape[0]
    nb = rows // 8
    groups = pkv_ref.shape[1]
    pre = pkv_ref.shape[2]
    nbuck = st_s.shape[0]
    mig = send_ref.shape[0]

    @pl.when(step == 0)
    def _():
        for m in range(mig):
            for kv in range(2):
                pltpu.make_async_copy(
                    tail_any.at[kv, send_s[m]], send_ref.at[m, kv], sems.at[m, kv]
                ).start()
        h = hid_ref[...].astype(F32)
        ms = jnp.mean(h * h, axis=-1, keepdims=True)
        n1 = (h * lax.rsqrt(ms + EPS) * gain_ref[...]).astype(BF16)
        q = jnp.dot(n1, wq_ref[...], preferred_element_type=F32).astype(BF16).astype(F32)
        kvn[0] = jnp.dot(n1, wk_ref[...], preferred_element_type=F32).astype(BF16).astype(F32)
        kvn[1] = jnp.dot(n1, wv_ref[...], preferred_element_type=F32).astype(BF16).astype(F32)
        g = col_form(grp_ref[...])
        tl = col_form(tlr_ref[...])
        pln = jnp.zeros_like(g)
        for i in range(groups):
            pln = jnp.where(g == float(i), plen_s[i].astype(F32), pln)
        posb[...] = pln + tl
        plb[...] = pln
        tlb[...] = tl
        lane = lax.broadcasted_iota(jnp.int32, (nb, 2, 8, 128), 3)
        head = lax.broadcasted_iota(jnp.int32, (nb, 2, 8, 128), 1)
        qh = jnp.broadcast_to((q * 0.125).reshape(nb, 1, 8, 128), (nb, 2, 8, 128))
        qh = jnp.where((lane // 64) == head, qh, 0.0).reshape(2 * rows, 128)
        q16[...] = qh.astype(BF16)
        g2 = jnp.broadcast_to(g.reshape(nb, 1, 8, 128), (nb, 2, 8, 128)).reshape(2 * rows, 128)
        for i in range(groups):
            lhs[:, i * 128 : (i + 1) * 128] = jnp.where(g2 == float(i), qh, 0.0).astype(BF16)
            kcat[:, i * 128 : (i + 1) * 128] = pkv_ref[0, i]
        for c in range(2):
            sco[pl.ds(c * rows, rows), :] = lax.dot_general(
                lhs[pl.ds(c * rows, rows), :], kcat[...], (((1,), (1,)), ((), ())),
                preferred_element_type=F32,
            )

        @pl.loop(0, nb)
        def _(b):
            pos = posb[pl.ds(b * 8, 8), :]
            pb = plb[pl.ds(b * 8, 8), :]
            tb = tlb[pl.ds(b * 8, 8), :]
            ln = lax.broadcasted_iota(jnp.int32, (8, 128), 1)
            lnf = ln.astype(F32)
            nch = pre // 128
            idx = [pos - (lnf + float(c * 128)) for c in range(nch)]
            idx.append(tb - (ln % 64).astype(F32))
            acc = [[jnp.full((8, 128), tab_s[0, hh], F32) for _ in idx] for hh in range(2)]
            for k in range(1, nbuck):
                th = st_s[k].astype(F32)
                t0 = tab_s[k, 0]
                t1 = tab_s[k, 1]
                for c in range(len(idx)):
                    ge = idx[c] >= th
                    acc[0][c] = jnp.where(ge, t0, acc[0][c])
                    acc[1][c] = jnp.where(ge, t1, acc[1][c])
            sub = lax.broadcasted_iota(jnp.int32, (8, 128), 0)
            tvalid = (idx[nch] >= 0.0) & ((ln // 64) == (sub % 2))
            for hh in range(2):
                rs = pl.ds(b * 16 + hh * 8, 8)
                tbias[rs, :] = jnp.where(tvalid, acc[hh][nch], NEG)
                s = [
                    jnp.where(lnf + float(c * 128) < pb, sco[rs, c * 128 : (c + 1) * 128] + acc[hh][c], NEG)
                    for c in range(nch)
                ]
                mx = functools.reduce(jnp.maximum, s)
                mx = jnp.max(mx, axis=1, keepdims=True)
                e = [jnp.exp(x - mx) for x in s]
                tot = jnp.sum(functools.reduce(jnp.add, e), axis=1, keepdims=True)
                mpart[rs, :] = jnp.broadcast_to(mx, (8, 128))
                lpart[rs, :] = jnp.broadcast_to(tot, (8, 128))
                for c in range(nch):
                    sco[rs, c * 128 : (c + 1) * 128] = e[c]

        prob[...] = sco[...].astype(BF16)
        acc = jnp.zeros((2 * rows, 128), F32)
        for i in range(groups):
            o = jnp.dot(prob[...], pkv_ref[1, i], preferred_element_type=F32)
            acc = jnp.where(g2 == float(i), o, acc)
        opart[...] = acc

        ids = ids_ref[...]
        e0 = ids[:, 0:1]
        e1 = ids[:, 1:2]
        ln = lax.broadcasted_iota(jnp.int32, (rows, 128), 1)
        hit0 = ln == e0
        hit1 = ln == e1
        ri = lax.broadcasted_iota(jnp.int32, (rows, rows), 0)
        ci = lax.broadcasted_iota(jnp.int32, (rows, rows), 1)
        lower = (ci < ri).astype(F32).astype(BF16)
        o0 = hit0.astype(F32)
        o1 = hit1.astype(F32)
        cum0 = jnp.dot(lower, o0.astype(BF16), preferred_element_type=F32)
        cum1 = jnp.dot(lower, o1.astype(BF16), preferred_element_type=F32)
        tot0 = jnp.sum(o0, axis=0, keepdims=True)
        p0 = jnp.sum(jnp.where(hit0, cum0, 0.0), axis=1, keepdims=True)
        p1 = jnp.sum(jnp.where(hit1, cum1 + tot0, 0.0), axis=1, keepdims=True)
        cap = float(slot_stride(5 * rows * TOP // (4 * 16)))
        slot_ref[0] = jnp.broadcast_to(e0.astype(F32) * cap + p0, (rows, 128))
        slot_ref[1] = jnp.broadcast_to(e1.astype(F32) * cap + p1, (rows, 128))

    def put_row(ref, lead, r, kv, length):
        base = pl.multiple_of((length // 16) * 16, 16)
        w = ref[(*lead, pl.ds(base, 16), slice(None))].astype(F32)
        sub = lax.broadcasted_iota(jnp.int32, (16, 128), 0)
        row = kvn[kv, pl.ds(r, 1), :]
        ref[(*lead, pl.ds(base, 16), slice(None))] = jnp.where(sub == length - base, row, w).astype(BF16)

    tail_out[...] = tail_ref[...]
    for i in range(RB):
        r = step * RB + i
        length = tl_s[r]
        for kv in range(2):
            put_row(tail_out, (kv, i), r, kv, length)

    sub = lax.broadcasted_iota(jnp.int32, (2, 8, 128), 1).reshape(16, 128)
    pair = sub // 2
    for bb in range(RB // 8):
        b = step * (RB // 8) + bb
        rs = pl.ds(pl.multiple_of(b * 16, 16), 16)
        kb = tail_out[0, bb * 8 : (bb + 1) * 8].reshape(512, 128)
        vb = tail_out[1, bb * 8 : (bb + 1) * 8].reshape(512, 128)
        s4 = lax.dot_general(q16[rs, :], kb, (((1,), (1,)), ((), ())), preferred_element_type=F32)
        s = s4[:, 0:128]
        for c in range(1, 4):
            s = jnp.where(pair == c, s4[:, c * 128 : (c + 1) * 128], s)
        s = s + tbias[rs, :]
        mt = jnp.max(s, axis=1, keepdims=True)
        mp = mpart[rs, :]
        mx = jnp.maximum(mt, mp)
        e = jnp.exp(s - mx)
        ap = jnp.exp(mp - mx)
        tot = jnp.sum(e, axis=1, keepdims=True) + lpart[rs, :] * ap
        p4 = jnp.concatenate([jnp.where(pair == c, e, 0.0) for c in range(4)], axis=1).astype(BF16)
        o = jnp.dot(p4, vb, preferred_element_type=F32) + opart[rs, :] * ap
        o = (o / tot).reshape(2, 8, 128)
        lane8 = lax.broadcasted_iota(jnp.int32, (8, 128), 1)
        head_ref[pl.ds(pl.multiple_of(b * 8, 8), 8), :] = jnp.where(lane8 < 64, o[0], o[1])

    @pl.when(step == nsteps - 1)
    def _():
        for m in range(mig):
            for kv in range(2):
                pltpu.make_async_copy(
                    tail_any.at[kv, send_s[m]], send_ref.at[m, kv], sems.at[m, kv]
                ).wait()
        for m in range(mig):
            r = send_s[m]
            length = tl_s[r]
            for kv in range(2):
                put_row(send_ref, (m, kv), r, kv, length)


def attention_call(hidden_in, gain, wq, wk, wv, group_of, prompt_len, tail_len, starts, table, send_idx, expert_ids, prompt_kv, tail_kv):
    rows = hidden_in.shape[0]
    smem = pl.BlockSpec(memory_space=pltpu.SMEM)
    once = pl.Buffered(1)

    def whole(shape):
        return pl.BlockSpec(shape, lambda s: (0,) * len(shape), pipeline_mode=once)

    def wholeo(shape):
        return pl.BlockSpec(shape, lambda s: (0,) * len(shape))

    _, groups, pre, wd = prompt_kv.shape
    tail_rows = tail_kv.shape[2]
    tail_spec = pl.BlockSpec((2, RB, tail_rows, wd), lambda s: (0, s, 0, 0))
    return pl.pallas_call(
        attn_kernel,
        grid=(rows // RB,),
        out_shape=(
            jax.ShapeDtypeStruct(tail_kv.shape, BF16),
            jax.ShapeDtypeStruct((rows, wd), F32),
            jax.ShapeDtypeStruct((send_idx.shape[0], 2, tail_rows, wd), BF16),
            jax.ShapeDtypeStruct((2, rows, 128), F32),
        ),
        in_specs=[smem] * 5
        + [
            whole(hidden_in.shape), whole((1, hidden_in.shape[1])), whole(wq.shape), whole(wk.shape), whole(wv.shape),
            whole((1, rows)), whole((1, rows)), whole(expert_ids.shape), whole(prompt_kv.shape), tail_spec,
            pl.BlockSpec(memory_space=pl.ANY),
        ],
        out_specs=(
            tail_spec, wholeo((rows, wd)), wholeo((send_idx.shape[0], 2, tail_rows, wd)), wholeo((2, rows, 128)),
        ),
        scratch_shapes=[
            pltpu.VMEM((2 * rows, 128), BF16),
            pltpu.VMEM((2, rows, 128), F32),
            pltpu.VMEM((2 * rows, groups * 128), BF16),
            pltpu.VMEM((pre, groups * 128), BF16),
            pltpu.VMEM((2 * rows, pre), F32),
            pltpu.VMEM((2 * rows, pre), BF16),
            pltpu.VMEM((rows, 128), F32),
            pltpu.VMEM((rows, 128), F32),
            pltpu.VMEM((rows, 128), F32),
            pltpu.VMEM((2 * rows, 128), F32),
            pltpu.VMEM((2 * rows, 128), F32),
            pltpu.VMEM((2 * rows, 128), F32),
            pltpu.VMEM((2 * rows, 128), F32),
            pltpu.SemaphoreType.DMA((send_idx.shape[0], 2)),
        ],
        compiler_params=pltpu.CompilerParams(vmem_limit_bytes=60 << 20, dimension_semantics=("arbitrary",)),
        cost_estimate=pl.CostEstimate(flops=2_000_000_000, bytes_accessed=22_000_000, transcendentals=400_000),
        name="attention_tails",
    )(
        tail_len, starts, table, prompt_len, send_idx,
        hidden_in, gain.reshape(1, -1), wq, wk, wv, group_of.reshape(1, -1), tail_len.reshape(1, -1), expert_ids,
        prompt_kv, tail_kv, tail_kv,
    )


MESH = pl.DeviceIdType.MESH


def moe_kernel(
    src_s, send_s, vac_s,
    hid_ref, head_ref, wout_ref, gain_ref, router_ref, ids_ref, slot_ref, wg_ref, wu_ref, wd_ref, tail_ref,
    out_ref, got_ref,
    t1, t2, t2r, part, psib, psend, precv, stat, statr, dsend, drecv, xall, ypart, ysib, ysend, yrecv, rsend, rrecv, mvs, mvr, mix,
    s_t1, r_t1, s_t2, r_t2, s_psib, r_psib, s_px, r_px, s_st, r_st, s_d, r_d, s_gx, r_gx, s_gs, r_gs,
    s_ysib, r_ysib, s_yx, r_yx, s_r, r_r, s_mv, r_mv, s_ox, r_ox, s_os, r_os,
):
    r = lax.axis_index("req")
    t = lax.axis_index("tp")
    n_req = t1.shape[0]
    n_tp = mix.shape[0]
    n_x = n_tp // 2
    rows = hid_ref.shape[0]
    cap = xall.shape[1] // n_req
    capp = dsend.shape[0] // n_req
    c = lax.rem(t, 2)
    x = t // 2
    sib = x * 2 + 1 - c
    width = hid_ref.shape[1]

    def tp_copy(src, dst, ss, rs, peer):
        return pltpu.make_async_remote_copy(
            src_ref=src, dst_ref=dst, send_sem=ss, recv_sem=rs, device_id=(r, peer), device_id_type=MESH
        )

    def req_copy(src, dst, ss, rs, peer):
        return pltpu.make_async_remote_copy(
            src_ref=src, dst_ref=dst, send_sem=ss, recv_sem=rs, device_id=(peer, t), device_id_type=MESH
        )

    def xpeer(d):
        return lax.rem(x + d, n_x) * 2 + c

    def xfrom(d):
        return lax.rem(x + n_x - d, n_x) * 2 + c

    barrier = pltpu.get_barrier_semaphore()

    @pl.loop(1, n_tp)
    def _(d):
        pl.semaphore_signal(barrier, inc=1, device_id=(r, lax.rem(t + d, n_tp)), device_id_type=MESH)

    @pl.loop(1, n_req)
    def _(d):
        pl.semaphore_signal(barrier, inc=1, device_id=(lax.rem(r + d, n_req), t), device_id_type=MESH)

    head = head_ref[...].astype(BF16)
    for tt in range(n_tp):
        part[tt % 2, tt // 2] = jnp.dot(
            head, wout_ref[:, tt * 128 : (tt + 1) * 128], preferred_element_type=F32
        ).astype(BF16)

    pl.semaphore_wait(barrier, n_tp - 1 + n_req - 1)

    def rs_sib(d, buf, dst, ss, rs):
        xx = lax.rem(x + d, n_x)
        return tp_copy(buf.at[1 - c, xx], dst.at[xx], ss.at[d], rs.at[d], sib)

    def rs_x(d, buf, dst, ss, rs):
        return tp_copy(buf.at[d], dst.at[d], ss.at[d], rs.at[d], xpeer(d))

    def reduce_scatter(buf, bsib, bsend, brecv, ss1, rs1, ss2, rs2):
        for d in (1, 2, 3, 0):
            rs_sib(d, buf, bsib, ss1, rs1).start()
        for d in (1, 2, 3):
            xx = lax.rem(x + d, n_x)
            rs_sib(d, buf, bsib, ss1, rs1).wait_recv()
            bsend[d] = (buf[c, xx].astype(F32) + bsib[xx].astype(F32)).astype(BF16)
            rs_x(d, bsend, brecv, ss2, rs2).start()
        rs_sib(0, buf, bsib, ss1, rs1).wait_recv()
        for d in (1, 2, 3):
            rs_x(d, bsend, brecv, ss2, rs2).wait_recv()

    def rs_total(buf, bsib, brecv, sl):
        tot = buf[c, x, sl, :].astype(F32) + bsib[x, sl, :].astype(F32)
        for d in (1, 2, 3):
            tot = tot + brecv[d, sl, :].astype(F32)
        return tot

    def rs_finish(buf, bsib, bsend, brecv, ss1, rs1, ss2, rs2):
        for d in (0, 1, 2, 3):
            rs_sib(d, buf, bsib, ss1, rs1).wait_send()
        for d in (1, 2, 3):
            rs_x(d, bsend, brecv, ss2, rs2).wait_send()

    def ag_x(d, buf, ss, rs):
        return tp_copy(buf.at[t], buf.at[t], ss.at[d], rs.at[d], xpeer(d))

    def ag_s(d, buf, ss, rs):
        who = xfrom(d)
        return tp_copy(buf.at[who], buf.at[who], ss.at[d], rs.at[d], sib)

    def all_gather(buf, ss1, rs1, ss2, rs2):
        for d in (1, 2, 3):
            ag_x(d, buf, ss1, rs1).start()
        ag_s(0, buf, ss2, rs2).start()
        for d in (1, 3, 2):
            who = xfrom(d)
            tp_copy(buf.at[who], buf.at[who], ss1.at[d], rs1.at[d], xpeer(d)).wait_recv()
            ag_s(d, buf, ss2, rs2).start()
        for d in (0, 1, 3, 2):
            mine = xfrom(d)
            other = lax.rem(x + n_x - d, n_x) * 2 + 1 - c
            tp_copy(buf.at[mine], buf.at[other], ss2.at[d], rs2.at[d], sib).wait_recv()

    def ag_finish(buf, ss1, rs1, ss2, rs2):
        for d in (1, 2, 3):
            ag_x(d, buf, ss1, rs1).wait_send()
        for d in (0, 1, 2, 3):
            ag_s(d, buf, ss2, rs2).wait_send()

    reduce_scatter(part, psib, psend, precv, s_psib, r_psib, s_px, r_px)

    def t1_copy(d):
        j = lax.rem(r + d, n_req)
        return req_copy(tail_ref.at[j], t1.at[r], s_t1.at[d], r_t1.at[d], j)

    @pl.loop(1, n_req)
    def _(d):
        t1_copy(d).start()

    t1[r] = tail_ref[r]

    attn = rs_total(part, psib, precv, slice(None))
    lanes = pl.ds(pl.multiple_of(t * 128, 128), 128)
    resid = (hid_ref[:, lanes].astype(F32) + attn).astype(BF16).astype(F32)
    u = resid * gain_ref[:, lanes]
    lg = jnp.dot(
        u.astype(BF16), router_ref[pl.ds(pl.multiple_of(t * 128, 128), 128), :], preferred_element_type=F32
    )
    ex = lax.broadcasted_iota(jnp.int32, lg.shape, 1)
    diff = jnp.sum(
        jnp.where(ex == ids_ref[:, 0:1], lg, 0.0) - jnp.where(ex == ids_ref[:, 1:2], lg, 0.0), axis=1, keepdims=True
    )
    sq = jnp.sum(resid * resid, axis=1, keepdims=True)
    ln = lax.broadcasted_iota(jnp.int32, (rows, 128), 1)
    packed = jnp.where(ln == 0, sq, jnp.where(ln == 1, diff, 0.0))
    stat[...] = jnp.transpose(packed)[0:8]

    def st_copy(d):
        return tp_copy(stat, statr.at[d], s_st.at[d], r_st.at[d], lax.rem(t + d, n_tp))

    for d in range(1, n_tp):
        st_copy(d).start()
    tot = stat[...]
    for d in range(1, n_tp):
        st_copy(d).wait_recv()
        tot = tot + statr[d]
    tot = jnp.transpose(jnp.concatenate([tot, jnp.zeros((120, rows), F32)], axis=0))
    rs = lax.rsqrt(tot[:, 0:1] * (1.0 / width) + EPS)
    gate = jax.nn.sigmoid(tot[:, 1:2] * rs)
    n2 = (u * rs).astype(BF16)

    s0 = slot_ref[0]
    s1 = slot_ref[1]
    nsl = n_req * cap
    nslp = n_req * capp
    lnf = ln.astype(F32)
    for k in range(nslp // 128):
        pick = (s0 == lnf + float(k * 128)) | (s1 == lnf + float(k * 128))
        dsend[k * 128 : (k + 1) * 128, :] = lax.dot_general(
            pick.astype(F32).astype(BF16), n2, (((0,), (0,)), ((), ())), preferred_element_type=F32
        ).astype(BF16)

    def block(j):
        return pl.ds(pl.multiple_of(j * capp, 16), capp)

    def d_copy(d):
        j = lax.rem(r + d, n_req)
        return req_copy(dsend.at[block(j)], drecv.at[block(r)], s_d.at[d], r_d.at[d], j)

    @pl.loop(1, n_req)
    def _(d):
        d_copy(d).start()

    drecv[block(r), :] = dsend[block(r), :]

    @pl.loop(1, n_req)
    def _(d):
        t1_copy(d).wait_recv()

    @pl.loop(0, n_req)
    def _(j):
        t2[j] = t1[src_s[j]]

    def t2_copy(d):
        j = lax.rem(r + d, n_req)
        return req_copy(t2.at[j], t2r.at[r], s_t2.at[d], r_t2.at[d], j)

    @pl.loop(1, n_req)
    def _(d):
        d_copy(d).wait_recv()

    xall[t] = jnp.concatenate(
        [drecv[j * capp : (j + 1) * capp, :].astype(F32)[0:cap] for j in range(n_req)], axis=0
    ).astype(BF16)
    all_gather(xall, s_gx, r_gx, s_gs, r_gs)

    @pl.loop(1, n_req)
    def _(d):
        t2_copy(d).start()

    t2r[r] = t2[r]

    @pl.loop(0, nsl // 128)
    def _(m):
        sl = pl.ds(pl.multiple_of(m * 128, 128), 128)
        xm = jnp.concatenate([xall[tt, sl, :] for tt in range(n_tp)], axis=1)
        gh = jnp.dot(xm, wg_ref[...], preferred_element_type=F32)
        uh = jnp.dot(xm, wu_ref[...], preferred_element_type=F32)
        act = (jax.nn.gelu(gh, approximate=True) * uh).astype(BF16)
        y = jnp.dot(act, wd_ref[...], preferred_element_type=F32).astype(BF16)
        for tt in range(n_tp):
            ypart[tt % 2, tt // 2, sl, :] = y[:, tt * 128 : (tt + 1) * 128]

    reduce_scatter(ypart, ysib, ysend, yrecv, s_ysib, r_ysib, s_yx, r_yx)
    tot = rs_total(ypart, ysib, yrecv, slice(None))
    pad = jnp.zeros((capp - cap, 128), F32)
    for j in range(n_req):
        rsend[j * capp : (j + 1) * capp, :] = jnp.concatenate([tot[j * cap : (j + 1) * cap], pad], axis=0).astype(BF16)

    def r_copy(d):
        j = lax.rem(r + d, n_req)
        return req_copy(rsend.at[block(j)], rrecv.at[block(r)], s_r.at[d], r_r.at[d], j)

    @pl.loop(1, n_req)
    def _(d):
        r_copy(d).start()

    rrecv[block(r), :] = rsend[block(r), :]

    @pl.loop(1, n_req)
    def _(d):
        r_copy(d).wait_recv()

    p0 = jnp.zeros((rows, 128), F32)
    p1 = jnp.zeros((rows, 128), F32)
    for k in range(nslp // 128):
        got = rrecv[k * 128 : (k + 1) * 128, :]
        p0 = p0 + jnp.dot((s0 == lnf + float(k * 128)).astype(F32).astype(BF16), got, preferred_element_type=F32)
        p1 = p1 + jnp.dot((s1 == lnf + float(k * 128)).astype(F32).astype(BF16), got, preferred_element_type=F32)
    mixed = (resid + gate * p0 + (1.0 - gate) * p1).astype(BF16)

    n_mig = send_s.shape[0]
    kk = lax.broadcasted_iota(jnp.int32, (16, rows), 0)
    rr = lax.broadcasted_iota(jnp.int32, (16, rows), 1)
    pick = jnp.zeros((16, rows), F32)
    for k in range(n_mig):
        pick = jnp.where((kk == k) & (rr == send_s[k]), 1.0, pick)
    mvs[...] = jnp.dot(pick.astype(BF16), mixed, preferred_element_type=F32).astype(BF16)

    def mv_copy(d):
        j = lax.rem(r + d, n_req)
        return req_copy(mvs, mvr.at[r], s_mv.at[d], r_mv.at[d], j)

    @pl.loop(1, n_req)
    def _(d):
        mv_copy(d).start()

    mvr[r] = mvs[...]

    @pl.loop(1, n_req)
    def _(d):
        mv_copy(d).wait_recv()

    came = mvr[src_s[r]].astype(F32)
    ri = lax.broadcasted_iota(jnp.int32, (rows, 128), 0)
    new = mixed.astype(F32)
    for k in range(n_mig):
        new = jnp.where(ri == vac_s[k], came[k : k + 1, :], new)
    mix[t] = new.astype(BF16)
    all_gather(mix, s_ox, r_ox, s_os, r_os)
    for tt in range(n_tp):
        out_ref[:, tt * 128 : (tt + 1) * 128] = mix[tt]

    @pl.loop(1, n_req)
    def _(d):
        t2_copy(d).wait_recv()

    got_ref[...] = t2r[...]

    rs_finish(part, psib, psend, precv, s_psib, r_psib, s_px, r_px)
    rs_finish(ypart, ysib, ysend, yrecv, s_ysib, r_ysib, s_yx, r_yx)
    ag_finish(xall, s_gx, r_gx, s_gs, r_gs)
    ag_finish(mix, s_ox, r_ox, s_os, r_os)
    for d in range(1, n_tp):
        st_copy(d).wait_send()

    @pl.loop(1, n_req)
    def _(d):
        t1_copy(d).wait_send()
        d_copy(d).wait_send()
        t2_copy(d).wait_send()
        r_copy(d).wait_send()
        mv_copy(d).wait_send()


def slot_stride(cap):
    return -(-cap // 16) * 16


def moe_call(n_req, n_tp, src, send_idx, vac, hidden, head, w_out, gain, router, ids, slots, wg, wu, wd, send_tail):
    rows, width = hidden.shape
    cap = 5 * rows * TOP // (4 * n_req)
    nsl = n_req * cap
    nslp = n_req * slot_stride(cap)
    chunk = send_tail.shape[1]
    smem = pl.BlockSpec(memory_space=pltpu.SMEM)
    vmem = pl.BlockSpec(memory_space=pltpu.VMEM)
    dma = pltpu.SemaphoreType.DMA
    n_x = n_tp // 2

    def bf(*shape):
        return pltpu.VMEM(shape, BF16)

    return pl.pallas_call(
        moe_kernel,
        out_shape=(
            jax.ShapeDtypeStruct((rows, width), BF16),
            jax.ShapeDtypeStruct((n_req, chunk, 128), BF16),
        ),
        in_specs=[smem] * 3 + [vmem] * 11,
        out_specs=(vmem, vmem),
        scratch_shapes=[
            bf(n_req, chunk, 128), bf(n_req, chunk, 128), bf(n_req, chunk, 128),
            bf(2, n_x, rows, 128), bf(n_x, rows, 128), bf(n_x, rows, 128), bf(n_x, rows, 128),
            pltpu.VMEM((8, rows), F32), pltpu.VMEM((n_tp, 8, rows), F32),
            bf(nslp, 128), bf(nslp, 128), bf(n_tp, nsl, 128),
            bf(2, n_x, nsl, 128), bf(n_x, nsl, 128), bf(n_x, nsl, 128), bf(n_x, nsl, 128),
            bf(nslp, 128), bf(nslp, 128),
            bf(16, 128), bf(n_req, 16, 128), bf(n_tp, rows, 128),
        ]
        + [dma((n_req,))] * 4
        + [dma((n_x,))] * 4
        + [dma((n_tp,))] * 2
        + [dma((n_req,))] * 2
        + [dma((n_x,))] * 4
        + [dma((n_x,))] * 4
        + [dma((n_req,))] * 4
        + [dma((n_x,))] * 4,
        compiler_params=pltpu.CompilerParams(
            collective_id=0, has_side_effects=True, vmem_limit_bytes=56 << 20
        ),
        name="moe_exchange",
    )(src, send_idx, vac, hidden, head, w_out, gain.reshape(1, -1), router, ids, slots, wg, wu, wd, send_tail)


def place_kernel(vac_s, got_ref, tail_in, tail_out, sems):
    rows = tail_out.shape[1]
    n_mig = got_ref.shape[0]
    for k in range(n_mig):
        for kv in range(2):

            @pl.when(vac_s[k] < rows)
            def _():
                pltpu.make_async_copy(got_ref.at[k, kv], tail_out.at[kv, vac_s[k]], sems.at[k, kv]).start()

    for k in range(n_mig):
        for kv in range(2):

            @pl.when(vac_s[k] < rows)
            def _():
                pltpu.make_async_copy(got_ref.at[k, kv], tail_out.at[kv, vac_s[k]], sems.at[k, kv]).wait()


def place_call(vac, got, tail):
    return pl.pallas_call(
        place_kernel,
        out_shape=jax.ShapeDtypeStruct(tail.shape, tail.dtype),
        in_specs=[
            pl.BlockSpec(memory_space=pltpu.SMEM),
            pl.BlockSpec(memory_space=pltpu.VMEM),
            pl.BlockSpec(memory_space=pl.ANY),
        ],
        out_specs=pl.BlockSpec(memory_space=pl.ANY),
        scratch_shapes=[pltpu.SemaphoreType.DMA((got.shape[0], 2))],
        input_output_aliases={2: 0},
        name="place_tails",
    )(vac, got, tail)


def body(
    hidden_in, prompt_kv, tail_kv, group_of, prompt_len, tail_len, bucket_of, bias_table, attn_gain, w_query, w_key,
    w_value, w_out, ffn_gain, router_weight, expert_ids, w_gate, w_up, w_down, new_slot,
):
    rows = hidden_in.shape[0]
    n_req = lax.axis_size("req")
    n_tp = lax.axis_size("tp")
    me = lax.axis_index("req")
    buckets = bias_table.shape[0]
    starts = jnp.sum((bucket_of[:, None] < jnp.arange(buckets, dtype=jnp.int32)[None, :]).astype(jnp.int32), axis=0)
    local = jnp.arange(rows, dtype=jnp.int32)
    kth = jnp.arange(MIG, dtype=jnp.int32)
    slots2 = new_slot.reshape(n_req, rows)
    moved2 = slots2 != jnp.arange(n_req * rows, dtype=jnp.int32).reshape(n_req, rows)
    replica = jnp.arange(n_req, dtype=jnp.int32)
    goes = jnp.max(jnp.where(moved2, slots2 // rows, -1), axis=1)
    goes = jnp.where(goes < 0, replica, goes)
    src = jnp.sum(jnp.where(goes[None, :] == replica[:, None], replica[None, :], 0), axis=1)
    mine = lax.dynamic_slice_in_dim(new_slot, me * rows, rows, 0)
    moved = mine != me * rows + local
    order = jnp.sum((moved[None, :] & (mine[None, :] < mine[:, None])).astype(jnp.int32), axis=1)
    place = jnp.sum((moved[None, :] & (local[None, :] < local[:, None])).astype(jnp.int32), axis=1)
    is_kth = moved[None, :] & (order[None, :] == kth[:, None])
    send_idx = jnp.sum(jnp.where(is_kth, local[None, :], 0), axis=1)
    at_kth = moved[None, :] & (place[None, :] == kth[:, None])
    vac = jnp.min(jnp.where(at_kth, local[None, :], rows), axis=1)
    tail_new, head, send_tail, slots = attention_call(
        hidden_in, attn_gain, w_query, w_key, w_value, group_of, prompt_len, tail_len, starts, bias_table, send_idx,
        expert_ids, prompt_kv, tail_kv,
    )
    pieces = send_tail.reshape(n_req, -1, send_tail.shape[-1])
    out_hidden, got = moe_call(
        n_req, n_tp, src, send_idx, vac, hidden_in, head, w_out, ffn_gain, router_weight, expert_ids, slots,
        w_gate[0], w_up[0], w_down[0], pieces,
    )
    new_tail = place_call(vac, got.reshape(send_tail.shape), tail_new)
    return (out_hidden, new_tail)


def solution(mesh):
    return jax.shard_map(
        body,
        mesh=mesh,
        in_specs=(
            P("req", None), P(None, "req", None, "tp"), P(None, "req", None, "tp"), P("req"), P("req"), P("req"), P(),
            P(None, "tp"), P(), P(None, "tp"), P(None, "tp"), P(None, "tp"), P("tp", None), P(), P(), P("req", None),
            P("req", None, "tp"), P("req", None, "tp"), P("req", "tp", None), P(),
        ),
        out_specs=(P("req", None), P(None, "req", None, "tp")),
        check_vma=False,
    )
```

```python
import functools

import jax
import jax.numpy as jnp
from jax import lax
from jax.experimental import pallas as pl
from jax.experimental.pallas import tpu as pltpu
from jax.sharding import PartitionSpec as P

F32 = jnp.float32
BF16 = jnp.bfloat16
EPS = 1e-06
NEG = -1e30
RB = 32
TOP = 2
MIG = 4


def slot_stride(cap):
    return -(-cap // 16) * 16


def col_form(row):
    n = row.shape[1]
    return jnp.transpose(jnp.broadcast_to(row.astype(F32), (128, n)))


def attn_kernel(
    tl_s, tab_s, plen_s, idx_s,
    gain_ref, grp_ref, tlr_ref, ids_ref, bkt_ref, hid_any, wq_any, wk_any, wv_any, pkv_any, tail_any,
    tail_out, head_ref, send_ref, slot_ref,
    hid_v, wcat, pkv_v, buf, q16, kvn, lhs, kcat, sco, prob, posb, plb, tlb, bkt, dtab, tbias, opart, mpart, lpart,
    s_in, s_tin, s_tout,
):
    rows = hid_v.shape[0]
    nb = rows // 8
    groups = pkv_v.shape[1]
    pre = pkv_v.shape[2]
    nbuck = tab_s.shape[1]
    mig = send_ref.shape[0]
    span = bkt_ref.shape[1]
    nblk = rows // RB
    loads = [
        pltpu.make_async_copy(hid_any, hid_v, s_in.at[0]),
        pltpu.make_async_copy(wq_any, wcat.at[:, 0:128], s_in.at[1]),
        pltpu.make_async_copy(wk_any, wcat.at[:, 128:256], s_in.at[2]),
        pltpu.make_async_copy(wv_any, wcat.at[:, 256:384], s_in.at[3]),
        pltpu.make_async_copy(pkv_any.at[0], pkv_v.at[0], s_in.at[4]),
        pltpu.make_async_copy(pkv_any.at[1], pkv_v.at[1], s_in.at[5]),
    ]
    for cp in loads:
        cp.start()

    def t_in(s, kv):
        sl = pl.ds(s * RB, RB)
        return pltpu.make_async_copy(tail_any.at[kv, sl], buf.at[kv, sl], s_tin.at[s, kv])

    def t_out(s, kv):
        sl = pl.ds(s * RB, RB)
        return pltpu.make_async_copy(buf.at[kv, sl], tail_out.at[kv, sl], s_tout.at[s, kv])

    @pl.loop(0, nblk)
    def _(s):
        t_in(s, 0).start()
        t_in(s, 1).start()

    bkt[...] = jnp.zeros_like(bkt)
    bkt[:, 0:span] = jnp.broadcast_to(bkt_ref[...], (8, span))
    nd = bkt.shape[1] // 128
    for c in range(nd):
        bk = bkt[:, c * 128 : (c + 1) * 128]
        d0 = jnp.zeros((8, 128), F32)
        d1 = d0
        for k in range(nbuck):
            hit = bk == k
            d0 = jnp.where(hit, tab_s[0, k], d0)
            d1 = jnp.where(hit, tab_s[1, k], d1)
        dtab[0, :, c * 128 : (c + 1) * 128] = d0
        dtab[1, :, c * 128 : (c + 1) * 128] = d1

    g = col_form(grp_ref[...])
    tl = col_form(tlr_ref[...])
    pln = jnp.zeros_like(g)
    for i in range(groups):
        pln = jnp.where(g == float(i), plen_s[i].astype(F32), pln)
    posb[...] = (pln + tl).astype(jnp.int32)
    plb[...] = pln.astype(jnp.int32)
    tlb[...] = tl.astype(jnp.int32)
    g2 = jnp.broadcast_to(g.reshape(nb, 1, 8, 128), (nb, 2, 8, 128)).reshape(2 * rows, 128)

    e0 = col_form(ids_ref[0:1, :])
    e1 = col_form(ids_ref[1:2, :])
    ln = lax.broadcasted_iota(jnp.int32, (rows, 128), 1).astype(F32)
    hit0 = ln == e0
    hit1 = ln == e1
    ri = lax.broadcasted_iota(jnp.int32, (rows, rows), 0)
    ci = lax.broadcasted_iota(jnp.int32, (rows, rows), 1)
    lower = (ci < ri).astype(F32).astype(BF16)
    o0 = hit0.astype(F32)
    o1 = hit1.astype(F32)
    cum0 = jnp.dot(lower, o0.astype(BF16), preferred_element_type=F32)
    cum1 = jnp.dot(lower, o1.astype(BF16), preferred_element_type=F32)
    tot0 = jnp.sum(o0, axis=0, keepdims=True)
    p0 = jnp.sum(jnp.where(hit0, cum0, 0.0), axis=1, keepdims=True)
    p1 = jnp.sum(jnp.where(hit1, cum1 + tot0, 0.0), axis=1, keepdims=True)
    stride = float(slot_stride(5 * rows * TOP // (4 * 16)))
    slot_ref[0] = e0 * stride + p0
    slot_ref[1] = e1 * stride + p1

    for cp in loads[:4]:
        cp.wait()
    h = hid_v[...].astype(F32)
    ms = jnp.mean(h * h, axis=-1, keepdims=True)
    n1 = (h * lax.rsqrt(ms + EPS) * gain_ref[...]).astype(BF16)
    qkv = jnp.dot(n1, wcat[...], preferred_element_type=F32).astype(BF16).astype(F32)
    q = qkv[:, 0:128]
    kvn[0] = qkv[:, 128:256]
    kvn[1] = qkv[:, 256:384]
    lane = lax.broadcasted_iota(jnp.int32, (nb, 2, 8, 128), 3)
    head = lax.broadcasted_iota(jnp.int32, (nb, 2, 8, 128), 1)
    qh = jnp.broadcast_to((q * 0.125).reshape(nb, 1, 8, 128), (nb, 2, 8, 128))
    qh = jnp.where((lane // 64) == head, qh, 0.0).reshape(2 * rows, 128)
    q16[...] = qh.astype(BF16)
    loads[4].wait()
    for i in range(groups):
        lhs[:, i * 128 : (i + 1) * 128] = jnp.where(g2 == float(i), qh, 0.0).astype(BF16)
        kcat[:, i * 128 : (i + 1) * 128] = pkv_v[0, i]
    sco[...] = lax.dot_general(lhs[...], kcat[...], (((1,), (1,)), ((), ())), preferred_element_type=F32)

    def take(tab, i):
        return jnp.take_along_axis(tab, i, axis=1, mode="promise_in_bounds")

    nch = pre // 128

    def prompt_softmax(b):
        pos = posb[pl.ds(b * 8, 8), :]
        pb = plb[pl.ds(b * 8, 8), :]
        tb = tlb[pl.ds(b * 8, 8), :]
        ln = lax.broadcasted_iota(jnp.int32, (8, 128), 1)
        sub = lax.broadcasted_iota(jnp.int32, (8, 128), 0)
        low = pos & 127
        gi = (low - ln) & 127
        blk = (pos >> 7) - (ln > low).astype(jnp.int32)
        at = [blk == k for k in range(nd)]
        td = tb - (ln & 63)
        tvalid = (td >= 0) & ((ln >> 6) == (sub & 1))
        td = jnp.maximum(td, 0)
        es = [[], []]
        for hh in range(2):
            rs = pl.ds(b * 16 + hh * 8, 8)
            tbias[rs, :] = jnp.where(tvalid, take(dtab[hh, :, 0:128], td), NEG)
            gs = [take(dtab[hh, :, k * 128 : (k + 1) * 128], gi) for k in range(nd)]
            s = []
            for c in range(nch):
                bias = gs[0]
                for k in range(1, nd - c):
                    bias = jnp.where(at[k + c], gs[k], bias)
                s.append(jnp.where(ln + c * 128 < pb, sco[rs, c * 128 : (c + 1) * 128] + bias, NEG))
            mx = jnp.max(functools.reduce(jnp.maximum, s), axis=1, keepdims=True)
            e = [jnp.exp(v - mx) for v in s]
            tot = jnp.sum(functools.reduce(jnp.add, e), axis=1, keepdims=True)
            mpart[rs, :] = jnp.broadcast_to(mx, (8, 128))
            lpart[rs, :] = jnp.broadcast_to(tot, (8, 128))
            es[hh] = e
        for c in range(nch):
            prob[pl.ds(b * 16, 16), c * 128 : (c + 1) * 128] = jnp.concatenate(
                [es[0][c], es[1][c]], axis=0
            ).astype(BF16)

    @pl.loop(0, nb // 2)
    def _(i):
        prompt_softmax(pl.multiple_of(i * 2, 2))
        prompt_softmax(i * 2 + 1)

    loads[5].wait()
    acc = jnp.zeros((2 * rows, 128), F32)
    for i in range(0, groups, 2):
        rhs = jnp.concatenate([pkv_v[1, i], pkv_v[1, i + 1]], axis=1)
        o = jnp.dot(prob[...], rhs, preferred_element_type=F32)
        acc = jnp.where(g2 == float(i), o[:, 0:128], acc)
        acc = jnp.where(g2 == float(i + 1), o[:, 128:256], acc)
    opart[...] = acc

    sub16 = lax.broadcasted_iota(jnp.int32, (16, 128), 0)
    pair = lax.rem(sub16, 8) // 2
    lane8 = lax.broadcasted_iota(jnp.int32, (8, 128), 1)

    @pl.loop(0, nblk)
    def _(s):
        t_in(s, 0).wait()
        t_in(s, 1).wait()
        for i in range(RB):
            r = s * RB + i
            length = tl_s[r]
            base = pl.multiple_of((length >> 4) << 4, 16)
            for kv in range(2):
                w = buf[kv, r, pl.ds(base, 16), :].astype(F32)
                row = kvn[kv, pl.ds(r, 1), :]
                buf[kv, r, pl.ds(base, 16), :] = jnp.where(sub16 == length - base, row, w).astype(BF16)
        t_out(s, 0).start()
        t_out(s, 1).start()
        for bb in range(RB // 8):
            b = s * (RB // 8) + bb
            rs = pl.ds(pl.multiple_of(b * 16, 16), 16)
            own = pl.ds(b * 8, 8)
            kb = buf[0, own].reshape(512, 128)
            vb = buf[1, own].reshape(512, 128)
            s4 = lax.dot_general(q16[rs, :], kb, (((1,), (1,)), ((), ())), preferred_element_type=F32)
            sc = s4[:, 0:128]
            for c in range(1, 4):
                sc = jnp.where(pair == c, s4[:, c * 128 : (c + 1) * 128], sc)
            sc = sc + tbias[rs, :]
            mt = jnp.max(sc, axis=1, keepdims=True)
            mp = mpart[rs, :]
            mx = jnp.maximum(mt, mp)
            e = jnp.exp(sc - mx)
            ap = jnp.exp(mp - mx)
            tot = jnp.sum(e, axis=1, keepdims=True) + lpart[rs, :] * ap
            p4 = jnp.concatenate([jnp.where(pair == c, e, 0.0) for c in range(4)], axis=1).astype(BF16)
            o = jnp.dot(p4, vb, preferred_element_type=F32) + opart[rs, :] * ap
            o = (o / tot).reshape(2, 8, 128)
            head_ref[pl.ds(pl.multiple_of(b * 8, 8), 8), :] = jnp.where(lane8 < 64, o[0], o[1])

    for m in range(mig):
        for kv in range(2):
            send_ref[m, kv] = buf[kv, idx_s[m]]

    @pl.loop(0, nblk)
    def _(s):
        t_out(s, 0).wait()
        t_out(s, 1).wait()


def attention_call(
    hidden_in, gain, wq, wk, wv, group_of, prompt_len, tail_len, bucket_of, table_t, idx, ids_t, prompt_kv, tail_kv
):
    rows, width = hidden_in.shape
    smem = pl.BlockSpec(memory_space=pltpu.SMEM)
    vmem = pl.BlockSpec(memory_space=pltpu.VMEM)
    anym = pl.BlockSpec(memory_space=pl.ANY)
    _, groups, pre, wd = prompt_kv.shape
    tail_rows = tail_kv.shape[2]
    nd = -(-bucket_of.shape[0] // 128)
    nblk = rows // RB
    dma = pltpu.SemaphoreType.DMA
    return pl.pallas_call(
        attn_kernel,
        out_shape=(
            jax.ShapeDtypeStruct(tail_kv.shape, BF16),
            jax.ShapeDtypeStruct((rows, wd), F32),
            jax.ShapeDtypeStruct((MIG, 2, tail_rows, wd), BF16),
            jax.ShapeDtypeStruct((2, rows, 128), F32),
        ),
        in_specs=[smem] * 4 + [vmem] * 5 + [anym] * 6,
        out_specs=(anym, vmem, vmem, vmem),
        scratch_shapes=[
            pltpu.VMEM((rows, width), BF16),
            pltpu.VMEM((width, 3 * wd), BF16),
            pltpu.VMEM(prompt_kv.shape, BF16),
            pltpu.VMEM(tail_kv.shape, BF16),
            pltpu.VMEM((2 * rows, wd), BF16),
            pltpu.VMEM((2, rows, wd), F32),
            pltpu.VMEM((2 * rows, groups * wd), BF16),
            pltpu.VMEM((pre, groups * wd), BF16),
            pltpu.VMEM((2 * rows, pre), F32),
            pltpu.VMEM((2 * rows, pre), BF16),
            pltpu.VMEM((rows, 128), jnp.int32),
            pltpu.VMEM((rows, 128), jnp.int32),
            pltpu.VMEM((rows, 128), jnp.int32),
            pltpu.VMEM((8, nd * 128), jnp.int32),
            pltpu.VMEM((2, 8, nd * 128), F32),
            pltpu.VMEM((2 * rows, 128), F32),
            pltpu.VMEM((2 * rows, 128), F32),
            pltpu.VMEM((2 * rows, 128), F32),
            pltpu.VMEM((2 * rows, 128), F32),
            dma((6,)),
            dma((nblk, 2)),
            dma((nblk, 2)),
        ],
        compiler_params=pltpu.CompilerParams(vmem_limit_bytes=60 << 20),
        name="attention_tails",
    )(
        tail_len, table_t, prompt_len, idx,
        gain.reshape(1, -1), group_of.reshape(1, -1), tail_len.reshape(1, -1), ids_t, bucket_of.reshape(1, -1),
        hidden_in, wq, wk, wv, prompt_kv, tail_kv,
    )


MESH = pl.DeviceIdType.MESH
NCH = 2


def moe_kernel(
    src_s, idx_s,
    head_ref, gain_ref, router_ref, ids_ref, slot_ref, tail_ref, hid_any, wout_any, wg_any, wu_any, wd_any,
    mix, came, got,
    hid_v, wout_v, wg_v, wu_v, wd_v,
    t1, t2, part, psib, psend, precv, stat, statr, dsend, drecv, xall, ypart, ysib, ysend, yrecv, rsend, rrecv, mvs, mvr,
    s_in, s_t1, r_t1, s_t2, r_t2, s_ps, r_ps, s_px, r_px, s_st, r_st, s_d, r_d, s_gx, r_gx, s_gs, r_gs,
    s_ys, r_ys, s_yx, r_yx, s_r, r_r, s_mv, r_mv, s_ox, r_ox, s_os, r_os, s_cm, r_cm,
):
    r = lax.axis_index("req")
    t = lax.axis_index("tp")
    n_req = t1.shape[0]
    n_tp = mix.shape[0]
    n_x = n_tp // 2
    rows = hid_v.shape[0]
    width = wout_v.shape[1]
    crows = xall.shape[2]
    per = n_req // NCH
    cap = crows // per
    nslp = dsend.shape[0]
    capp = nslp // n_req
    c = lax.rem(t, 2)
    x = t // 2
    sib = x * 2 + 1 - c
    lanes = pl.ds(pl.multiple_of(t * 128, 128), 128)

    loads = [
        pltpu.make_async_copy(wout_any, wout_v, s_in.at[0]),
        pltpu.make_async_copy(hid_any.at[:, lanes], hid_v, s_in.at[1]),
        pltpu.make_async_copy(wg_any, wg_v, s_in.at[2]),
        pltpu.make_async_copy(wu_any, wu_v, s_in.at[3]),
        pltpu.make_async_copy(wd_any, wd_v, s_in.at[4]),
    ]
    for cp in loads:
        cp.start()

    def tp_copy(src, dst, ss, rs, peer):
        return pltpu.make_async_remote_copy(
            src_ref=src, dst_ref=dst, send_sem=ss, recv_sem=rs, device_id=(r, peer), device_id_type=MESH
        )

    def req_copy(src, dst, ss, rs, peer):
        return pltpu.make_async_remote_copy(
            src_ref=src, dst_ref=dst, send_sem=ss, recv_sem=rs, device_id=(peer, t), device_id_type=MESH
        )

    def xpeer(d):
        return lax.rem(x + d, n_x) * 2 + c

    def xfrom(d):
        return lax.rem(x + n_x - d, n_x) * 2 + c

    barrier = pltpu.get_barrier_semaphore()

    @pl.loop(1, n_tp)
    def _(d):
        pl.semaphore_signal(barrier, inc=1, device_id=(r, lax.rem(t + d, n_tp)), device_id_type=MESH)

    @pl.loop(1, n_req)
    def _(d):
        pl.semaphore_signal(barrier, inc=1, device_id=(lax.rem(r + d, n_req), t), device_id_type=MESH)

    head = head_ref[...].astype(BF16)
    loads[0].wait()
    for tt in range(n_tp):
        part[tt % 2, tt // 2] = jnp.dot(
            head, wout_v[:, tt * 128 : (tt + 1) * 128], preferred_element_type=F32
        ).astype(BF16)

    pl.semaphore_wait(barrier, n_tp - 1 + n_req - 1)

    def rs_sib(d, buf, dst, ss, rs):
        xx = lax.rem(x + d, n_x)
        return tp_copy(buf.at[1 - c, xx], dst.at[xx], ss.at[d], rs.at[d], sib)

    def rs_x(d, buf, dst, ss, rs):
        return tp_copy(buf.at[d], dst.at[d], ss.at[d], rs.at[d], xpeer(d))

    def rs_start(buf, bsib, ss1, rs1):
        for d in (2, 1, 3, 0):
            rs_sib(d, buf, bsib, ss1, rs1).start()

    def rs_send(buf, bsib, bsend, brecv, ss1, rs1, ss2, rs2):
        for d in (2, 1, 3):
            xx = lax.rem(x + d, n_x)
            rs_sib(d, buf, bsib, ss1, rs1).wait_recv()
            bsend[d] = (buf[c, xx].astype(F32) + bsib[xx].astype(F32)).astype(BF16)
            rs_x(d, bsend, brecv, ss2, rs2).start()

    def rs_total(buf, bsib, bsend, brecv, ss1, rs1, ss2, rs2):
        rs_sib(0, buf, bsib, ss1, rs1).wait_recv()
        tot = buf[c, x].astype(F32) + bsib[x].astype(F32)
        for d in (1, 3, 2):
            rs_x(d, bsend, brecv, ss2, rs2).wait_recv()
            tot = tot + brecv[d].astype(F32)
        return tot

    def rs_finish(buf, bsib, bsend, brecv, ss1, rs1, ss2, rs2):
        for d in (0, 1, 2, 3):
            rs_sib(d, buf, bsib, ss1, rs1).wait_send()
        for d in (1, 2, 3):
            rs_x(d, bsend, brecv, ss2, rs2).wait_send()

    def ag_x(d, buf, ss, rs):
        return tp_copy(buf.at[t], buf.at[t], ss.at[d], rs.at[d], xpeer(d))

    def ag_s(d, buf, ss, rs):
        who = xfrom(d)
        return tp_copy(buf.at[who], buf.at[who], ss.at[d], rs.at[d], sib)

    def ag_start(buf, ss1, rs1, ss2, rs2):
        for d in (2, 1, 3):
            ag_x(d, buf, ss1, rs1).start()
        ag_s(0, buf, ss2, rs2).start()

    def ag_pass(buf, ss1, rs1, ss2, rs2):
        for d in (1, 3, 2):
            who = xfrom(d)
            tp_copy(buf.at[who], buf.at[who], ss1.at[d], rs1.at[d], xpeer(d)).wait_recv()
            ag_s(d, buf, ss2, rs2).start()

    def ag_wait(buf, ss1, rs1, ss2, rs2):
        for d in (0, 1, 3, 2):
            mine = xfrom(d)
            other = lax.rem(x + n_x - d, n_x) * 2 + 1 - c
            tp_copy(buf.at[mine], buf.at[other], ss2.at[d], rs2.at[d], sib).wait_recv()

    def ag_finish(buf, ss1, rs1, ss2, rs2):
        for d in (1, 2, 3):
            ag_x(d, buf, ss1, rs1).wait_send()
        for d in (0, 1, 2, 3):
            ag_s(d, buf, ss2, rs2).wait_send()

    attn_rs = (part, psib, psend, precv, s_ps, r_ps, s_px, r_px)
    rs_start(part, psib, s_ps, r_ps)
    rs_send(*attn_rs)

    def t1_copy(d):
        j = lax.rem(r + d, n_req)
        return req_copy(tail_ref.at[j], t1.at[r], s_t1.at[d], r_t1.at[d], j)

    @pl.loop(1, n_req)
    def _(d):
        t1_copy(d).start()

    t1[r] = tail_ref[r]
    loads[1].wait()
    resid = (hid_v[...].astype(F32) + rs_total(*attn_rs)).astype(BF16)

    s0 = slot_ref[0]
    s1 = slot_ref[1]
    lnf = lax.broadcasted_iota(jnp.int32, (rows, 128), 1).astype(F32)
    for k in range(nslp // 128):
        pick = (s0 == lnf + float(k * 128)) | (s1 == lnf + float(k * 128))
        dsend[k * 128 : (k + 1) * 128, :] = lax.dot_general(
            pick.astype(F32).astype(BF16), resid, (((0,), (0,)), ((), ())), preferred_element_type=F32
        ).astype(BF16)

    def block(j):
        return pl.ds(pl.multiple_of(j * capp, 16), capp)

    def d_copy(d):
        j = lax.rem(r + d, n_req)
        return req_copy(dsend.at[block(j)], drecv.at[block(r)], s_d.at[d], r_d.at[d], j)

    @pl.loop(1, n_req)
    def _(d):
        d_copy(d).start()

    drecv[block(r), :] = dsend[block(r), :]

    rf = resid.astype(F32)
    u = rf * gain_ref[:, lanes]
    lg = lax.dot_general(
        u.astype(BF16), router_ref[:, lanes], (((1,), (1,)), ((), ())), preferred_element_type=F32
    )
    e0 = col_form(ids_ref[0:1, :])
    e1 = col_form(ids_ref[1:2, :])
    n_e = lg.shape[1]
    ex = lnf[:, 0:n_e]
    diff = jnp.sum(
        jnp.where(ex == e0[:, 0:n_e], lg, 0.0) - jnp.where(ex == e1[:, 0:n_e], lg, 0.0), axis=1, keepdims=True
    )
    sq = jnp.sum(rf * rf, axis=1, keepdims=True)
    stat[...] = jnp.transpose(jnp.where(lnf == 0.0, sq, jnp.where(lnf == 1.0, diff, 0.0)))[0:8]

    def st_copy(d):
        return tp_copy(stat, statr.at[d], s_st.at[d], r_st.at[d], lax.rem(t + d, n_tp))

    for d in range(1, n_tp):
        st_copy(d).start()

    @pl.loop(1, n_req)
    def _(d):
        d_copy(d).wait_recv()

    def x_ag(h):
        return (xall.at[h], s_gx.at[h], r_gx.at[h], s_gs.at[h], r_gs.at[h])

    for h in range(NCH):
        xall[h, t] = jnp.concatenate(
            [drecv[j * capp : (j + 1) * capp, :].astype(F32)[0:cap] for j in range(h * per, (h + 1) * per)], axis=0
        ).astype(BF16)
        ag_start(*x_ag(h))

    @pl.loop(1, n_req)
    def _(d):
        t1_copy(d).wait_recv()

    @pl.loop(0, n_req)
    def _(j):
        t2[j] = t1[src_s[j]]

    def t2_copy(d):
        j = lax.rem(r + d, n_req)
        return req_copy(t2.at[j], got.at[r], s_t2.at[d], r_t2.at[d], j)

    @pl.loop(1, n_req)
    def _(d):
        t2_copy(d).start()

    got[r] = t2[r]

    tot = stat[...]
    for d in range(1, n_tp):
        st_copy(d).wait_recv()
        tot = tot + statr[d]
    tot = jnp.transpose(jnp.concatenate([tot, jnp.zeros((120, rows), F32)], axis=0))
    gate = jax.nn.sigmoid(tot[:, 1:2] * lax.rsqrt(tot[:, 0:1] * (1.0 / width) + EPS))

    for cp in loads[2:]:
        cp.wait()

    def ffn(h):
        xm = jnp.concatenate([xall[h, tt] for tt in range(n_tp)], axis=1).astype(F32)
        ms = jnp.mean(xm * xm, axis=-1, keepdims=True)
        nm = (xm * lax.rsqrt(ms + EPS) * gain_ref[...]).astype(BF16)
        gh = lax.dot_general(nm, wg_v[...], (((1,), (1,)), ((), ())), preferred_element_type=F32)
        uh = lax.dot_general(nm, wu_v[...], (((1,), (1,)), ((), ())), preferred_element_type=F32)
        act = (jax.nn.gelu(gh, approximate=True) * uh).astype(BF16)
        y = jnp.dot(act, wd_v[...], preferred_element_type=F32).astype(BF16)
        for tt in range(n_tp):
            ypart[h, tt % 2, tt // 2] = y[:, tt * 128 : (tt + 1) * 128]

    def y_rs(h):
        return (
            ypart.at[h], ysib.at[h], ysend.at[h], yrecv.at[h], s_ys.at[h], r_ys.at[h], s_yx.at[h], r_yx.at[h]
        )

    ag_pass(*x_ag(0))
    for h in range(NCH):
        ag_wait(*x_ag(h))
        ffn(h)
        rs_start(ypart.at[h], ysib.at[h], s_ys.at[h], r_ys.at[h])
        if h + 1 < NCH:
            ag_pass(*x_ag(h + 1))
        rs_send(*y_rs(h))

    def r_copy(d):
        j = lax.rem(r + d, n_req)
        return req_copy(rsend.at[block(j)], rrecv.at[block(r)], s_r.at[d], r_r.at[d], j)

    pad = jnp.zeros((capp - cap, 128), F32)
    for h in range(NCH):
        tot = rs_total(*y_rs(h))
        for i in range(per):
            j = h * per + i
            rsend[j * capp : (j + 1) * capp, :] = jnp.concatenate(
                [tot[i * cap : (i + 1) * cap], pad], axis=0
            ).astype(BF16)

        @pl.loop(h * per, (h + 1) * per)
        def _(j):
            @pl.when(j != r)
            def _():
                r_copy(lax.rem(j + n_req - r, n_req)).start()

    rrecv[block(r), :] = rsend[block(r), :]

    @pl.loop(1, n_req)
    def _(d):
        r_copy(d).wait_recv()

    p0 = jnp.zeros((rows, 128), F32)
    p1 = jnp.zeros((rows, 128), F32)
    for k in range(nslp // 128):
        res = rrecv[k * 128 : (k + 1) * 128, :]
        p0 = p0 + jnp.dot((s0 == lnf + float(k * 128)).astype(F32).astype(BF16), res, preferred_element_type=F32)
        p1 = p1 + jnp.dot((s1 == lnf + float(k * 128)).astype(F32).astype(BF16), res, preferred_element_type=F32)
    mixed = (rf + gate * p0 + (1.0 - gate) * p1).astype(BF16)

    kk = lax.broadcasted_iota(jnp.int32, (16, rows), 0)
    rr = lax.broadcasted_iota(jnp.int32, (16, rows), 1)
    pick = jnp.zeros((16, rows), F32)
    for k in range(MIG):
        pick = jnp.where((kk == k) & (rr == idx_s[k]), 1.0, pick)
    mvs[...] = jnp.dot(pick.astype(BF16), mixed, preferred_element_type=F32).astype(BF16)

    def mv_copy(d):
        j = lax.rem(r + d, n_req)
        return req_copy(mvs, mvr.at[r], s_mv.at[d], r_mv.at[d], j)

    @pl.loop(1, n_req)
    def _(d):
        mv_copy(d).start()

    mvr[r] = mvs[...]
    mix[t] = mixed
    o_ag = (mix, s_ox, r_ox, s_os, r_os)
    ag_start(*o_ag)
    ag_pass(*o_ag)

    @pl.loop(1, n_req)
    def _(d):
        mv_copy(d).wait_recv()

    came[t] = mvr[src_s[r]]

    def cm_copy(d):
        return tp_copy(came.at[t], came.at[t], s_cm.at[d], r_cm.at[d], lax.rem(t + d, n_tp))

    for d in range(1, n_tp):
        cm_copy(d).start()

    ag_wait(*o_ag)
    for d in range(1, n_tp):
        who = lax.rem(t + n_tp - d, n_tp)
        tp_copy(came.at[who], came.at[who], s_cm.at[d], r_cm.at[d], who).wait_recv()

    @pl.loop(1, n_req)
    def _(d):
        t2_copy(d).wait_recv()

    rs_finish(*attn_rs)
    for h in range(NCH):
        rs_finish(*y_rs(h))
        ag_finish(*x_ag(h))
    ag_finish(*o_ag)
    for d in range(1, n_tp):
        st_copy(d).wait_send()
        cm_copy(d).wait_send()

    @pl.loop(1, n_req)
    def _(d):
        t1_copy(d).wait_send()
        d_copy(d).wait_send()
        t2_copy(d).wait_send()
        r_copy(d).wait_send()
        mv_copy(d).wait_send()


def moe_call(n_req, n_tp, src, idx, head, gain, router_t, ids_t, slots, send_tail, hidden, w_out, wg_t, wu_t, wd):
    rows, width = hidden.shape
    cap = 5 * rows * TOP // (4 * n_req)
    nsl = n_req * cap
    crows = nsl // NCH
    nslp = n_req * slot_stride(cap)
    chunk = send_tail.shape[1]
    smem = pl.BlockSpec(memory_space=pltpu.SMEM)
    vmem = pl.BlockSpec(memory_space=pltpu.VMEM)
    anym = pl.BlockSpec(memory_space=pl.ANY)
    dma = pltpu.SemaphoreType.DMA
    n_x = n_tp // 2

    def bf(*shape):
        return pltpu.VMEM(shape, BF16)

    return pl.pallas_call(
        moe_kernel,
        out_shape=(
            jax.ShapeDtypeStruct((n_tp, rows, 128), BF16),
            jax.ShapeDtypeStruct((n_tp, 16, 128), BF16),
            jax.ShapeDtypeStruct((n_req, chunk, 128), BF16),
        ),
        in_specs=[smem] * 2 + [vmem] * 6 + [anym] * 5,
        out_specs=(vmem, vmem, vmem),
        scratch_shapes=[
            bf(rows, 128), bf(*w_out.shape), bf(*wg_t.shape), bf(*wu_t.shape), bf(*wd.shape),
            bf(n_req, chunk, 128), bf(n_req, chunk, 128),
            bf(2, n_x, rows, 128), bf(n_x, rows, 128), bf(n_x, rows, 128), bf(n_x, rows, 128),
            pltpu.VMEM((8, rows), F32), pltpu.VMEM((n_tp, 8, rows), F32),
            bf(nslp, 128), bf(nslp, 128), bf(NCH, n_tp, crows, 128),
            bf(NCH, 2, n_x, crows, 128), bf(NCH, n_x, crows, 128), bf(NCH, n_x, crows, 128), bf(NCH, n_x, crows, 128),
            bf(nslp, 128), bf(nslp, 128),
            bf(16, 128), bf(n_req, 16, 128),
        ]
        + [dma((5,))]
        + [dma((n_req,))] * 4
        + [dma((n_x,))] * 4
        + [dma((n_tp,))] * 2
        + [dma((n_req,))] * 2
        + [dma((NCH, n_x))] * 8
        + [dma((n_req,))] * 4
        + [dma((n_x,))] * 4
        + [dma((n_tp,))] * 2,
        compiler_params=pltpu.CompilerParams(collective_id=0, has_side_effects=True, vmem_limit_bytes=56 << 20),
        name="moe_exchange",
    )(src, idx, head, gain.reshape(1, -1), router_t, ids_t, slots, send_tail, hidden, w_out, wg_t, wu_t, wd)


def place_kernel(idx_s, mix_ref, came_ref, got_ref, tail_in, out_ref, tail_out, sems):
    rows = tail_out.shape[1]

    def put(k, kv):
        return pltpu.make_async_copy(got_ref.at[k, kv], tail_out.at[kv, idx_s[MIG + k]], sems.at[k, kv])

    for k in range(MIG):
        for kv in range(2):

            @pl.when(idx_s[MIG + k] < rows)
            def _():
                put(k, kv).start()

    for tt in range(mix_ref.shape[0]):
        out_ref[:, tt * 128 : (tt + 1) * 128] = mix_ref[tt]
    sub = lax.broadcasted_iota(jnp.int32, (16, 128), 0)
    for k in range(MIG):
        slot = idx_s[MIG + k]

        @pl.when(slot < rows)
        def _():
            base = pl.multiple_of((slot >> 4) << 4, 16)
            for tt in range(mix_ref.shape[0]):
                cols = slice(tt * 128, (tt + 1) * 128)
                row = came_ref[tt].astype(F32)[k : k + 1, :]
                w = out_ref[pl.ds(base, 16), cols].astype(F32)
                out_ref[pl.ds(base, 16), cols] = jnp.where(sub == slot - base, row, w).astype(BF16)

    for k in range(MIG):
        for kv in range(2):

            @pl.when(idx_s[MIG + k] < rows)
            def _():
                put(k, kv).wait()


def place_call(idx, mix, came, got, tail):
    n_tp, rows, wd = mix.shape
    vmem = pl.BlockSpec(memory_space=pltpu.VMEM)
    return pl.pallas_call(
        place_kernel,
        out_shape=(
            jax.ShapeDtypeStruct((rows, n_tp * wd), BF16),
            jax.ShapeDtypeStruct(tail.shape, tail.dtype),
        ),
        in_specs=[pl.BlockSpec(memory_space=pltpu.SMEM), vmem, vmem, vmem, pl.BlockSpec(memory_space=pl.ANY)],
        out_specs=(vmem, pl.BlockSpec(memory_space=pl.ANY)),
        scratch_shapes=[pltpu.SemaphoreType.DMA((MIG, 2))],
        input_output_aliases={4: 1},
        name="place_rows",
    )(idx, mix, came, got, tail)


def body(
    hidden_in, prompt_kv, tail_kv, group_of, prompt_len, tail_len, bucket_of, bias_table, attn_gain, w_query, w_key,
    w_value, w_out, ffn_gain, router_weight, expert_ids, w_gate, w_up, w_down, new_slot,
):
    rows = hidden_in.shape[0]
    n_req = lax.axis_size("req")
    n_tp = lax.axis_size("tp")
    me = lax.axis_index("req")
    local = jnp.arange(rows, dtype=jnp.int32)
    kth = jnp.arange(MIG, dtype=jnp.int32)
    tiles = new_slot.reshape(n_req * rows // 128, 128)
    moved_t = tiles != jnp.arange(n_req * rows, dtype=jnp.int32).reshape(tiles.shape)
    goes = jnp.max(jnp.where(moved_t, tiles // rows, -1), axis=1).reshape(n_req, rows // 128)
    goes = jnp.max(goes, axis=1)
    replica = jnp.arange(n_req, dtype=jnp.int32)
    goes = jnp.where(goes < 0, replica, goes)
    src = jnp.sum(jnp.where(goes[None, :] == replica[:, None], replica[None, :], 0), axis=1)
    mine = lax.dynamic_slice_in_dim(new_slot, me * rows, rows, 0)
    moved = mine != me * rows + local
    key = jnp.concatenate([mine, local])
    both = jnp.concatenate([moved, moved])
    part = jnp.concatenate([jnp.zeros_like(local), jnp.ones_like(local)])
    rank = jnp.sum(
        (both[None, :] & (part[None, :] == part[:, None]) & (key[None, :] < key[:, None])).astype(jnp.int32), axis=1
    )
    want = jnp.arange(2 * MIG, dtype=jnp.int32)
    hit = both[None, :] & (rank + part * MIG == want[:, None])
    idx = jnp.min(jnp.where(hit, jnp.concatenate([local, local])[None, :], rows), axis=1)
    idx = jnp.where(want < MIG, jnp.minimum(idx, rows - 1), idx)
    ids_t = expert_ids.T
    tail_new, head, send_tail, slots = attention_call(
        hidden_in, attn_gain, w_query, w_key, w_value, group_of, prompt_len, tail_len, bucket_of, bias_table.T, idx,
        ids_t, prompt_kv, tail_kv,
    )
    pieces = send_tail.reshape(n_req, -1, send_tail.shape[-1])
    mix, came, got = moe_call(
        n_req, n_tp, src, idx, head, ffn_gain, router_weight.T, ids_t, slots, pieces, hidden_in, w_out,
        w_gate[0].T, w_up[0].T, w_down[0],
    )
    return place_call(idx, mix, came, got.reshape(send_tail.shape), tail_new)


def solution(mesh):
    return jax.shard_map(
        body,
        mesh=mesh,
        in_specs=(
            P("req", None), P(None, "req", None, "tp"), P(None, "req", None, "tp"), P("req"), P("req"), P("req"), P(),
            P(None, "tp"), P(), P(None, "tp"), P(None, "tp"), P(None, "tp"), P("tp", None), P(), P(), P("req", None),
            P("req", None, "tp"), P("req", None, "tp"), P("req", "tp", None), P(),
        ),
        out_specs=(P("req", None), P(None, "req", None, "tp")),
        check_vma=False,
    )
```

```python
import functools

import jax
import jax.numpy as jnp
from jax import lax
from jax.experimental import pallas as pl
from jax.experimental.pallas import tpu as pltpu
from jax.sharding import PartitionSpec as P

F32 = jnp.float32
BF16 = jnp.bfloat16
EPS = 1e-06
NEG = -1e30
RB = 32
TOP = 2
MIG = 4


def slot_stride(cap):
    return -(-cap // 16) * 16


def col_form(row):
    n = row.shape[1]
    return jnp.transpose(jnp.broadcast_to(row.astype(F32), (128, n)))


def migration_tables(ns_ref, meta_ref, rows):
    me = lax.axis_index("req")
    per = rows // 128
    tiles = ns_ref[...].astype(F32)
    shape = tiles.shape
    lane = lax.broadcasted_iota(jnp.int32, shape, 1).astype(F32)
    sub = lax.broadcasted_iota(jnp.int32, shape, 0)
    moved = tiles != sub.astype(F32) * 128.0 + lane
    where_to = jnp.floor(tiles * (1.0 / rows))
    goes = jnp.max(jnp.where(moved, where_to, -1.0), axis=1, keepdims=True)
    src = jnp.max(jnp.where(goes == lane, (sub // per).astype(F32), -1.0), axis=0, keepdims=True)
    src = jnp.where(src < 0.0, lane[0:1], src)

    mine = ns_ref[pl.ds(me * per, per), :].astype(F32)
    row = jnp.concatenate([mine[i : i + 1] for i in range(per)], axis=1)
    col = col_form(row)
    base = (me * rows).astype(F32)
    rid = lax.broadcasted_iota(jnp.int32, (rows, 128), 0).astype(F32)
    rlane = lax.broadcasted_iota(jnp.int32, (rows, 128), 1).astype(F32)
    moved_col = col != rid + base
    order = jnp.zeros((rows, 128), F32)
    place = jnp.zeros((rows, 128), F32)
    for i in range(per):
        part = row[:, i * 128 : (i + 1) * 128]
        other = rlane + float(i * 128)
        moved_row = part != other[0:1] + base
        order = order + jnp.where(moved_row & (part < col), 1.0, 0.0)
        place = place + jnp.where(moved_row & (other < rid), 1.0, 0.0)
    order = jnp.sum(order, axis=1, keepdims=True)
    place = jnp.sum(place, axis=1, keepdims=True)
    out = float(rows)
    send = jnp.min(jnp.where(moved_col & (order == rlane), rid, out), axis=0, keepdims=True)
    send = jnp.minimum(send, out - 1.0)
    vac = jnp.min(jnp.where(moved_col & (place + float(MIG) == rlane), rid, out), axis=0, keepdims=True)
    idx = jnp.where(rlane[0:1] < float(MIG), send, vac)
    s8 = lax.broadcasted_iota(jnp.int32, (8, 128), 0)
    meta_ref[...] = jnp.where(s8 == 0, idx, jnp.where(s8 == 1, src, 0.0)).astype(jnp.int32)


def attn_kernel(
    tl_s, tab_s, plen_s, bkt_s,
    gain_ref, grp_ref, tlr_ref, ids_ref, ns_ref, hid_any, wq_any, wk_any, wv_any, pkv_any, tail_any,
    tail_out, head_ref, send_ref, slot_ref, meta_ref,
    hid_v, wcat, pkv_v, buf, q16, kvn, lhs, kcat, sco, prob, posb, plb, tlb, dtab, tbias, opart, mpart, lpart,
    first_s, meta_s, s_in, s_tin, s_tout, s_meta,
):
    rows = hid_v.shape[0]
    nb = rows // 8
    groups = pkv_v.shape[1]
    pre = pkv_v.shape[2]
    nbuck = tab_s.shape[1]
    mig = send_ref.shape[0]
    span = bkt_s.shape[0]
    nblk = rows // RB
    loads = [
        pltpu.make_async_copy(hid_any, hid_v, s_in.at[0]),
        pltpu.make_async_copy(wq_any, wcat.at[:, 0:128], s_in.at[1]),
        pltpu.make_async_copy(wk_any, wcat.at[:, 128:256], s_in.at[2]),
        pltpu.make_async_copy(wv_any, wcat.at[:, 256:384], s_in.at[3]),
        pltpu.make_async_copy(pkv_any.at[0], pkv_v.at[0], s_in.at[4]),
        pltpu.make_async_copy(pkv_any.at[1], pkv_v.at[1], s_in.at[5]),
    ]
    for cp in loads:
        cp.start()

    def t_in(s, kv):
        sl = pl.ds(s * RB, RB)
        return pltpu.make_async_copy(tail_any.at[kv, sl], buf.at[kv, sl], s_tin.at[s, kv])

    def t_out(s, kv):
        sl = pl.ds(s * RB, RB)
        return pltpu.make_async_copy(buf.at[kv, sl], tail_out.at[kv, sl], s_tout.at[s, kv])

    @pl.loop(0, nblk)
    def _(s):
        t_in(s, 0).start()
        t_in(s, 1).start()

    for k in range(nbuck):
        first_s[k] = span

    @pl.loop(0, span, unroll=8)
    def _(i):
        d = span - 1 - i
        first_s[bkt_s[d]] = d

    nd = dtab.shape[2] // 128
    dist = [lax.broadcasted_iota(jnp.int32, (8, 128), 1) + c * 128 for c in range(nd)]
    d0 = [jnp.full((8, 128), tab_s[0, 0], F32) for _ in range(nd)]
    d1 = [jnp.full((8, 128), tab_s[1, 0], F32) for _ in range(nd)]
    for k in range(1, nbuck):
        for c in range(nd):
            ge = dist[c] >= first_s[k]
            d0[c] = jnp.where(ge, tab_s[0, k], d0[c])
            d1[c] = jnp.where(ge, tab_s[1, k], d1[c])
    for c in range(nd):
        dtab[0, :, c * 128 : (c + 1) * 128] = d0[c]
        dtab[1, :, c * 128 : (c + 1) * 128] = d1[c]

    migration_tables(ns_ref, meta_ref, rows)
    meta_copy = pltpu.make_async_copy(meta_ref, meta_s, s_meta)
    meta_copy.start()

    g = col_form(grp_ref[...])
    tl = col_form(tlr_ref[...])
    pln = jnp.zeros_like(g)
    for i in range(groups):
        pln = jnp.where(g == float(i), plen_s[i].astype(F32), pln)
    posb[...] = (pln + tl).astype(jnp.int32)
    plb[...] = pln.astype(jnp.int32)
    tlb[...] = tl.astype(jnp.int32)
    g2 = jnp.broadcast_to(g.reshape(nb, 1, 8, 128), (nb, 2, 8, 128)).reshape(2 * rows, 128)

    e0 = col_form(ids_ref[0:1, :])
    e1 = col_form(ids_ref[1:2, :])
    ln = lax.broadcasted_iota(jnp.int32, (rows, 128), 1).astype(F32)
    hit0 = ln == e0
    hit1 = ln == e1
    ri = lax.broadcasted_iota(jnp.int32, (rows, rows), 0)
    ci = lax.broadcasted_iota(jnp.int32, (rows, rows), 1)
    lower = (ci < ri).astype(F32).astype(BF16)
    o0 = hit0.astype(F32)
    o1 = hit1.astype(F32)
    cum0 = jnp.dot(lower, o0.astype(BF16), preferred_element_type=F32)
    cum1 = jnp.dot(lower, o1.astype(BF16), preferred_element_type=F32)
    tot0 = jnp.sum(o0, axis=0, keepdims=True)
    p0 = jnp.sum(jnp.where(hit0, cum0, 0.0), axis=1, keepdims=True)
    p1 = jnp.sum(jnp.where(hit1, cum1 + tot0, 0.0), axis=1, keepdims=True)
    stride = float(slot_stride(5 * rows * TOP // (4 * 16)))
    slot_ref[0] = e0 * stride + p0
    slot_ref[1] = e1 * stride + p1

    for cp in loads[:4]:
        cp.wait()
    h = hid_v[...].astype(F32)
    ms = jnp.mean(h * h, axis=-1, keepdims=True)
    n1 = (h * lax.rsqrt(ms + EPS) * gain_ref[...]).astype(BF16)
    qkv = jnp.dot(n1, wcat[...], preferred_element_type=F32).astype(BF16).astype(F32)
    q = qkv[:, 0:128]
    kvn[0] = qkv[:, 128:256]
    kvn[1] = qkv[:, 256:384]
    lane = lax.broadcasted_iota(jnp.int32, (nb, 2, 8, 128), 3)
    head = lax.broadcasted_iota(jnp.int32, (nb, 2, 8, 128), 1)
    qh = jnp.broadcast_to((q * 0.125).reshape(nb, 1, 8, 128), (nb, 2, 8, 128))
    qh = jnp.where((lane // 64) == head, qh, 0.0).reshape(2 * rows, 128)
    q16[...] = qh.astype(BF16)
    loads[4].wait()
    for i in range(groups):
        lhs[:, i * 128 : (i + 1) * 128] = jnp.where(g2 == float(i), qh, 0.0).astype(BF16)
        kcat[:, i * 128 : (i + 1) * 128] = pkv_v[0, i]
    sco[...] = lax.dot_general(lhs[...], kcat[...], (((1,), (1,)), ((), ())), preferred_element_type=F32)

    def take(tab, i):
        return jnp.take_along_axis(tab, i, axis=1, mode="promise_in_bounds")

    nch = pre // 128

    def prompt_softmax(b):
        pos = posb[pl.ds(b * 8, 8), :]
        pb = plb[pl.ds(b * 8, 8), :]
        tb = tlb[pl.ds(b * 8, 8), :]
        ln = lax.broadcasted_iota(jnp.int32, (8, 128), 1)
        sub = lax.broadcasted_iota(jnp.int32, (8, 128), 0)
        low = pos & 127
        gi = (low - ln) & 127
        blk = (pos >> 7) - (ln > low).astype(jnp.int32)
        at = [blk == k for k in range(nd)]
        td = tb - (ln & 63)
        tvalid = (td >= 0) & ((ln >> 6) == (sub & 1))
        td = jnp.maximum(td, 0)
        es = [[], []]
        for hh in range(2):
            rs = pl.ds(b * 16 + hh * 8, 8)
            tbias[rs, :] = jnp.where(tvalid, take(dtab[hh, :, 0:128], td), NEG)
            gs = [take(dtab[hh, :, k * 128 : (k + 1) * 128], gi) for k in range(nd)]
            s = []
            for c in range(nch):
                bias = gs[0]
                for k in range(1, nd - c):
                    bias = jnp.where(at[k + c], gs[k], bias)
                s.append(jnp.where(ln + c * 128 < pb, sco[rs, c * 128 : (c + 1) * 128] + bias, NEG))
            mx = jnp.max(functools.reduce(jnp.maximum, s), axis=1, keepdims=True)
            e = [jnp.exp(v - mx) for v in s]
            tot = jnp.sum(functools.reduce(jnp.add, e), axis=1, keepdims=True)
            mpart[rs, :] = jnp.broadcast_to(mx, (8, 128))
            lpart[rs, :] = jnp.broadcast_to(tot, (8, 128))
            es[hh] = e
        for c in range(nch):
            prob[pl.ds(b * 16, 16), c * 128 : (c + 1) * 128] = jnp.concatenate(
                [es[0][c], es[1][c]], axis=0
            ).astype(BF16)

    @pl.loop(0, nb // 2)
    def _(i):
        prompt_softmax(pl.multiple_of(i * 2, 2))
        prompt_softmax(i * 2 + 1)

    loads[5].wait()
    acc = jnp.zeros((2 * rows, 128), F32)
    for i in range(0, groups, 2):
        rhs = jnp.concatenate([pkv_v[1, i], pkv_v[1, i + 1]], axis=1)
        o = jnp.dot(prob[...], rhs, preferred_element_type=F32)
        acc = jnp.where(g2 == float(i), o[:, 0:128], acc)
        acc = jnp.where(g2 == float(i + 1), o[:, 128:256], acc)
    opart[...] = acc

    sub16 = lax.broadcasted_iota(jnp.int32, (16, 128), 0)
    pair = lax.rem(sub16, 8) // 2
    lane8 = lax.broadcasted_iota(jnp.int32, (8, 128), 1)

    @pl.loop(0, nblk)
    def _(s):
        t_in(s, 0).wait()
        t_in(s, 1).wait()
        for i in range(RB):
            r = s * RB + i
            length = tl_s[r]
            base = pl.multiple_of((length >> 4) << 4, 16)
            for kv in range(2):
                w = buf[kv, r, pl.ds(base, 16), :].astype(F32)
                row = kvn[kv, pl.ds(r, 1), :]
                buf[kv, r, pl.ds(base, 16), :] = jnp.where(sub16 == length - base, row, w).astype(BF16)
        t_out(s, 0).start()
        t_out(s, 1).start()
        for bb in range(RB // 8):
            b = s * (RB // 8) + bb
            rs = pl.ds(pl.multiple_of(b * 16, 16), 16)
            own = pl.ds(b * 8, 8)
            kb = buf[0, own].reshape(512, 128)
            vb = buf[1, own].reshape(512, 128)
            s4 = lax.dot_general(q16[rs, :], kb, (((1,), (1,)), ((), ())), preferred_element_type=F32)
            sc = s4[:, 0:128]
            for c in range(1, 4):
                sc = jnp.where(pair == c, s4[:, c * 128 : (c + 1) * 128], sc)
            sc = sc + tbias[rs, :]
            mt = jnp.max(sc, axis=1, keepdims=True)
            mp = mpart[rs, :]
            mx = jnp.maximum(mt, mp)
            e = jnp.exp(sc - mx)
            ap = jnp.exp(mp - mx)
            tot = jnp.sum(e, axis=1, keepdims=True) + lpart[rs, :] * ap
            p4 = jnp.concatenate([jnp.where(pair == c, e, 0.0) for c in range(4)], axis=1).astype(BF16)
            o = jnp.dot(p4, vb, preferred_element_type=F32) + opart[rs, :] * ap
            o = (o / tot).reshape(2, 8, 128)
            head_ref[pl.ds(pl.multiple_of(b * 8, 8), 8), :] = jnp.where(lane8 < 64, o[0], o[1])

    meta_copy.wait()
    for m in range(mig):
        for kv in range(2):
            send_ref[m, kv] = buf[kv, meta_s[0, m]]

    @pl.loop(0, nblk)
    def _(s):
        t_out(s, 0).wait()
        t_out(s, 1).wait()


def attention_call(
    hidden_in, gain, wq, wk, wv, group_of, prompt_len, tail_len, bucket_of, table_t, new_slot, ids_t, prompt_kv, tail_kv
):
    rows, width = hidden_in.shape
    smem = pl.BlockSpec(memory_space=pltpu.SMEM)
    vmem = pl.BlockSpec(memory_space=pltpu.VMEM)
    anym = pl.BlockSpec(memory_space=pl.ANY)
    _, groups, pre, wd = prompt_kv.shape
    tail_rows = tail_kv.shape[2]
    nd = -(-bucket_of.shape[0] // 128)
    nblk = rows // RB
    dma = pltpu.SemaphoreType.DMA
    return pl.pallas_call(
        attn_kernel,
        out_shape=(
            jax.ShapeDtypeStruct(tail_kv.shape, BF16),
            jax.ShapeDtypeStruct((rows, wd), F32),
            jax.ShapeDtypeStruct((MIG, 2, tail_rows, wd), BF16),
            jax.ShapeDtypeStruct((2, rows, 128), F32),
            jax.ShapeDtypeStruct((8, 128), jnp.int32),
        ),
        in_specs=[smem] * 4 + [vmem] * 5 + [anym] * 6,
        out_specs=(anym, vmem, vmem, vmem, vmem),
        scratch_shapes=[
            pltpu.VMEM((rows, width), BF16),
            pltpu.VMEM((width, 3 * wd), BF16),
            pltpu.VMEM(prompt_kv.shape, BF16),
            pltpu.VMEM(tail_kv.shape, BF16),
            pltpu.VMEM((2 * rows, wd), BF16),
            pltpu.VMEM((2, rows, wd), F32),
            pltpu.VMEM((2 * rows, groups * wd), BF16),
            pltpu.VMEM((pre, groups * wd), BF16),
            pltpu.VMEM((2 * rows, pre), F32),
            pltpu.VMEM((2 * rows, pre), BF16),
            pltpu.VMEM((rows, 128), jnp.int32),
            pltpu.VMEM((rows, 128), jnp.int32),
            pltpu.VMEM((rows, 128), jnp.int32),
            pltpu.VMEM((2, 8, nd * 128), F32),
            pltpu.VMEM((2 * rows, 128), F32),
            pltpu.VMEM((2 * rows, 128), F32),
            pltpu.VMEM((2 * rows, 128), F32),
            pltpu.VMEM((2 * rows, 128), F32),
            pltpu.SMEM((table_t.shape[1],), jnp.int32),
            pltpu.SMEM((8, 128), jnp.int32),
            dma((6,)),
            dma((nblk, 2)),
            dma((nblk, 2)),
            dma,
        ],
        compiler_params=pltpu.CompilerParams(vmem_limit_bytes=60 << 20),
        name="attention_tails",
    )(
        tail_len, table_t, prompt_len, bucket_of,
        gain.reshape(1, -1), group_of.reshape(1, -1), tail_len.reshape(1, -1), ids_t, new_slot.reshape(-1, 128),
        hidden_in, wq, wk, wv, prompt_kv, tail_kv,
    )


MESH = pl.DeviceIdType.MESH
NCH = 2


def moe_kernel(
    meta_s,
    head_ref, gain_ref, router_ref, ids_ref, slot_ref, tail_ref, hid_any, wout_any, wg_any, wu_any, wd_any,
    mix, came, got,
    hid_v, wout_v, wg_v, wu_v, wd_v,
    t1, t2, part, psib, psend, precv, stat, statr, dsend, drecv, xall, ypart, ysib, ysend, yrecv, rsend, rrecv, mvs, mvr,
    s_in, s_t1, r_t1, s_t2, r_t2, s_ps, r_ps, s_px, r_px, s_st, r_st, s_d, r_d, s_gx, r_gx, s_gs, r_gs,
    s_ys, r_ys, s_yx, r_yx, s_r, r_r, s_mv, r_mv, s_ox, r_ox, s_os, r_os, s_cm, r_cm,
):
    r = lax.axis_index("req")
    t = lax.axis_index("tp")
    n_req = t1.shape[0]
    n_tp = mix.shape[0]
    n_x = n_tp // 2
    rows = hid_v.shape[0]
    width = wout_v.shape[1]
    crows = xall.shape[2]
    per = n_req // NCH
    cap = crows // per
    nslp = dsend.shape[0]
    capp = nslp // n_req
    c = lax.rem(t, 2)
    x = t // 2
    sib = x * 2 + 1 - c
    lanes = pl.ds(pl.multiple_of(t * 128, 128), 128)

    loads = [
        pltpu.make_async_copy(wout_any, wout_v, s_in.at[0]),
        pltpu.make_async_copy(hid_any.at[:, lanes], hid_v, s_in.at[1]),
        pltpu.make_async_copy(wg_any, wg_v, s_in.at[2]),
        pltpu.make_async_copy(wu_any, wu_v, s_in.at[3]),
        pltpu.make_async_copy(wd_any, wd_v, s_in.at[4]),
    ]
    for cp in loads:
        cp.start()

    def tp_copy(src, dst, ss, rs, peer):
        return pltpu.make_async_remote_copy(
            src_ref=src, dst_ref=dst, send_sem=ss, recv_sem=rs, device_id=(r, peer), device_id_type=MESH
        )

    def req_copy(src, dst, ss, rs, peer):
        return pltpu.make_async_remote_copy(
            src_ref=src, dst_ref=dst, send_sem=ss, recv_sem=rs, device_id=(peer, t), device_id_type=MESH
        )

    def xpeer(d):
        return lax.rem(x + d, n_x) * 2 + c

    def xfrom(d):
        return lax.rem(x + n_x - d, n_x) * 2 + c

    barrier = pltpu.get_barrier_semaphore()

    @pl.loop(1, n_tp)
    def _(d):
        pl.semaphore_signal(barrier, inc=1, device_id=(r, lax.rem(t + d, n_tp)), device_id_type=MESH)

    @pl.loop(1, n_req)
    def _(d):
        pl.semaphore_signal(barrier, inc=1, device_id=(lax.rem(r + d, n_req), t), device_id_type=MESH)

    head = head_ref[...].astype(BF16)
    loads[0].wait()
    for tt in range(n_tp):
        part[tt % 2, tt // 2] = jnp.dot(
            head, wout_v[:, tt * 128 : (tt + 1) * 128], preferred_element_type=F32
        ).astype(BF16)

    pl.semaphore_wait(barrier, n_tp - 1 + n_req - 1)

    def rs_sib(d, buf, dst, ss, rs):
        xx = lax.rem(x + d, n_x)
        return tp_copy(buf.at[1 - c, xx], dst.at[xx], ss.at[d], rs.at[d], sib)

    def rs_x(d, buf, dst, ss, rs):
        return tp_copy(buf.at[d], dst.at[d], ss.at[d], rs.at[d], xpeer(d))

    def rs_start(buf, bsib, ss1, rs1):
        for d in (2, 1, 3, 0):
            rs_sib(d, buf, bsib, ss1, rs1).start()

    def rs_send(buf, bsib, bsend, brecv, ss1, rs1, ss2, rs2):
        for d in (2, 1, 3):
            xx = lax.rem(x + d, n_x)
            rs_sib(d, buf, bsib, ss1, rs1).wait_recv()
            bsend[d] = (buf[c, xx].astype(F32) + bsib[xx].astype(F32)).astype(BF16)
            rs_x(d, bsend, brecv, ss2, rs2).start()

    def rs_total(buf, bsib, bsend, brecv, ss1, rs1, ss2, rs2):
        rs_sib(0, buf, bsib, ss1, rs1).wait_recv()
        tot = buf[c, x].astype(F32) + bsib[x].astype(F32)
        for d in (1, 3, 2):
            rs_x(d, bsend, brecv, ss2, rs2).wait_recv()
            tot = tot + brecv[d].astype(F32)
        return tot

    def rs_finish(buf, bsib, bsend, brecv, ss1, rs1, ss2, rs2):
        for d in (0, 1, 2, 3):
            rs_sib(d, buf, bsib, ss1, rs1).wait_send()
        for d in (1, 2, 3):
            rs_x(d, bsend, brecv, ss2, rs2).wait_send()

    def ag_x(d, buf, ss, rs):
        return tp_copy(buf.at[t], buf.at[t], ss.at[d], rs.at[d], xpeer(d))

    def ag_s(d, buf, ss, rs):
        who = xfrom(d)
        return tp_copy(buf.at[who], buf.at[who], ss.at[d], rs.at[d], sib)

    def ag_start(buf, ss1, rs1, ss2, rs2):
        for d in (2, 1, 3):
            ag_x(d, buf, ss1, rs1).start()
        ag_s(0, buf, ss2, rs2).start()

    def ag_pass(buf, ss1, rs1, ss2, rs2):
        for d in (1, 3, 2):
            who = xfrom(d)
            tp_copy(buf.at[who], buf.at[who], ss1.at[d], rs1.at[d], xpeer(d)).wait_recv()
            ag_s(d, buf, ss2, rs2).start()

    def ag_wait(buf, ss1, rs1, ss2, rs2):
        for d in (0, 1, 3, 2):
            mine = xfrom(d)
            other = lax.rem(x + n_x - d, n_x) * 2 + 1 - c
            tp_copy(buf.at[mine], buf.at[other], ss2.at[d], rs2.at[d], sib).wait_recv()

    def ag_finish(buf, ss1, rs1, ss2, rs2):
        for d in (1, 2, 3):
            ag_x(d, buf, ss1, rs1).wait_send()
        for d in (0, 1, 2, 3):
            ag_s(d, buf, ss2, rs2).wait_send()

    attn_rs = (part, psib, psend, precv, s_ps, r_ps, s_px, r_px)
    rs_start(part, psib, s_ps, r_ps)
    rs_send(*attn_rs)

    def t1_copy(d):
        j = lax.rem(r + d, n_req)
        return req_copy(tail_ref.at[j], t1.at[r], s_t1.at[d], r_t1.at[d], j)

    loads[1].wait()
    resid = (hid_v[...].astype(F32) + rs_total(*attn_rs)).astype(BF16)

    s0 = slot_ref[0]
    s1 = slot_ref[1]
    lnf = lax.broadcasted_iota(jnp.int32, (rows, 128), 1).astype(F32)
    for k in range(nslp // 128):
        pick = (s0 == lnf + float(k * 128)) | (s1 == lnf + float(k * 128))
        dsend[k * 128 : (k + 1) * 128, :] = lax.dot_general(
            pick.astype(F32).astype(BF16), resid, (((0,), (0,)), ((), ())), preferred_element_type=F32
        ).astype(BF16)

    def block(j):
        return pl.ds(pl.multiple_of(j * capp, 16), capp)

    def d_copy(d):
        j = lax.rem(r + d, n_req)
        return req_copy(dsend.at[block(j)], drecv.at[block(r)], s_d.at[d], r_d.at[d], j)

    @pl.loop(1, n_req)
    def _(d):
        d_copy(d).start()

    drecv[block(r), :] = dsend[block(r), :]

    @pl.loop(1, n_req)
    def _(d):
        t1_copy(d).start()

    t1[r] = tail_ref[r]

    rf = resid.astype(F32)
    u = rf * gain_ref[:, lanes]
    lg = lax.dot_general(
        u.astype(BF16), router_ref[:, lanes], (((1,), (1,)), ((), ())), preferred_element_type=F32
    )
    e0 = col_form(ids_ref[0:1, :])
    e1 = col_form(ids_ref[1:2, :])
    n_e = lg.shape[1]
    ex = lnf[:, 0:n_e]
    diff = jnp.sum(
        jnp.where(ex == e0[:, 0:n_e], lg, 0.0) - jnp.where(ex == e1[:, 0:n_e], lg, 0.0), axis=1, keepdims=True
    )
    sq = jnp.sum(rf * rf, axis=1, keepdims=True)
    stat[...] = jnp.transpose(jnp.where(lnf == 0.0, sq, jnp.where(lnf == 1.0, diff, 0.0)))[0:8]

    def st_copy(d):
        return tp_copy(stat, statr.at[d], s_st.at[d], r_st.at[d], lax.rem(t + d, n_tp))

    for d in range(1, n_tp):
        st_copy(d).start()

    @pl.loop(1, n_req)
    def _(d):
        d_copy(d).wait_recv()

    def x_ag(h):
        return (xall.at[h], s_gx.at[h], r_gx.at[h], s_gs.at[h], r_gs.at[h])

    for h in range(NCH):
        xall[h, t] = jnp.concatenate(
            [drecv[j * capp : (j + 1) * capp, :].astype(F32)[0:cap] for j in range(h * per, (h + 1) * per)], axis=0
        ).astype(BF16)
        ag_start(*x_ag(h))

    @pl.loop(1, n_req)
    def _(d):
        t1_copy(d).wait_recv()

    @pl.loop(0, n_req)
    def _(j):
        t2[j] = t1[meta_s[1, j]]

    def t2_copy(d):
        j = lax.rem(r + d, n_req)
        return req_copy(t2.at[j], got.at[r], s_t2.at[d], r_t2.at[d], j)

    @pl.loop(1, n_req)
    def _(d):
        t2_copy(d).start()

    got[r] = t2[r]

    tot = stat[...]
    for d in range(1, n_tp):
        st_copy(d).wait_recv()
        tot = tot + statr[d]
    tot = jnp.transpose(jnp.concatenate([tot, jnp.zeros((120, rows), F32)], axis=0))
    gate = jax.nn.sigmoid(tot[:, 1:2] * lax.rsqrt(tot[:, 0:1] * (1.0 / width) + EPS))

    for cp in loads[2:]:
        cp.wait()

    def ffn(h):
        xm = jnp.concatenate([xall[h, tt] for tt in range(n_tp)], axis=1).astype(F32)
        ms = jnp.mean(xm * xm, axis=-1, keepdims=True)
        nm = (xm * lax.rsqrt(ms + EPS) * gain_ref[...]).astype(BF16)
        gh = lax.dot_general(nm, wg_v[...], (((1,), (1,)), ((), ())), preferred_element_type=F32)
        uh = lax.dot_general(nm, wu_v[...], (((1,), (1,)), ((), ())), preferred_element_type=F32)
        act = (jax.nn.gelu(gh, approximate=True) * uh).astype(BF16)
        y = jnp.dot(act, wd_v[...], preferred_element_type=F32).astype(BF16)
        for tt in range(n_tp):
            ypart[h, tt % 2, tt // 2] = y[:, tt * 128 : (tt + 1) * 128]

    def y_rs(h):
        return (
            ypart.at[h], ysib.at[h], ysend.at[h], yrecv.at[h], s_ys.at[h], r_ys.at[h], s_yx.at[h], r_yx.at[h]
        )

    ag_pass(*x_ag(0))
    for h in range(NCH):
        ag_wait(*x_ag(h))
        ffn(h)
        rs_start(ypart.at[h], ysib.at[h], s_ys.at[h], r_ys.at[h])
        if h + 1 < NCH:
            ag_pass(*x_ag(h + 1))
        rs_send(*y_rs(h))

    def r_copy(d):
        j = lax.rem(r + d, n_req)
        return req_copy(rsend.at[block(j)], rrecv.at[block(r)], s_r.at[d], r_r.at[d], j)

    pad = jnp.zeros((capp - cap, 128), F32)
    for h in range(NCH):
        tot = rs_total(*y_rs(h))
        for i in range(per):
            j = h * per + i
            rsend[j * capp : (j + 1) * capp, :] = jnp.concatenate(
                [tot[i * cap : (i + 1) * cap], pad], axis=0
            ).astype(BF16)

        @pl.loop(h * per, (h + 1) * per)
        def _(j):
            @pl.when(j != r)
            def _():
                r_copy(lax.rem(j + n_req - r, n_req)).start()

    rrecv[block(r), :] = rsend[block(r), :]

    @pl.loop(1, n_req)
    def _(d):
        r_copy(d).wait_recv()

    p0 = jnp.zeros((rows, 128), F32)
    p1 = jnp.zeros((rows, 128), F32)
    for k in range(nslp // 128):
        res = rrecv[k * 128 : (k + 1) * 128, :]
        p0 = p0 + jnp.dot((s0 == lnf + float(k * 128)).astype(F32).astype(BF16), res, preferred_element_type=F32)
        p1 = p1 + jnp.dot((s1 == lnf + float(k * 128)).astype(F32).astype(BF16), res, preferred_element_type=F32)
    mixed = (rf + gate * p0 + (1.0 - gate) * p1).astype(BF16)

    kk = lax.broadcasted_iota(jnp.int32, (16, rows), 0)
    rr = lax.broadcasted_iota(jnp.int32, (16, rows), 1)
    pick = jnp.zeros((16, rows), F32)
    for k in range(MIG):
        pick = jnp.where((kk == k) & (rr == meta_s[0, k]), 1.0, pick)
    mvs[...] = jnp.dot(pick.astype(BF16), mixed, preferred_element_type=F32).astype(BF16)

    def mv_copy(d):
        j = lax.rem(r + d, n_req)
        return req_copy(mvs, mvr.at[r], s_mv.at[d], r_mv.at[d], j)

    @pl.loop(1, n_req)
    def _(d):
        mv_copy(d).start()

    mvr[r] = mvs[...]
    mix[t] = mixed
    o_ag = (mix, s_ox, r_ox, s_os, r_os)
    ag_start(*o_ag)
    ag_pass(*o_ag)

    @pl.loop(1, n_req)
    def _(d):
        mv_copy(d).wait_recv()

    came[t] = mvr[meta_s[1, r]]

    def cm_copy(d):
        return tp_copy(came.at[t], came.at[t], s_cm.at[d], r_cm.at[d], lax.rem(t + d, n_tp))

    for d in range(1, n_tp):
        cm_copy(d).start()

    ag_wait(*o_ag)
    for d in range(1, n_tp):
        who = lax.rem(t + n_tp - d, n_tp)
        tp_copy(came.at[who], came.at[who], s_cm.at[d], r_cm.at[d], who).wait_recv()

    @pl.loop(1, n_req)
    def _(d):
        t2_copy(d).wait_recv()

    rs_finish(*attn_rs)
    for h in range(NCH):
        rs_finish(*y_rs(h))
        ag_finish(*x_ag(h))
    ag_finish(*o_ag)
    for d in range(1, n_tp):
        st_copy(d).wait_send()
        cm_copy(d).wait_send()

    @pl.loop(1, n_req)
    def _(d):
        t1_copy(d).wait_send()
        d_copy(d).wait_send()
        t2_copy(d).wait_send()
        r_copy(d).wait_send()
        mv_copy(d).wait_send()


def moe_call(n_req, n_tp, meta, head, gain, router_t, ids_t, slots, send_tail, hidden, w_out, wg_t, wu_t, wd):
    rows, width = hidden.shape
    cap = 5 * rows * TOP // (4 * n_req)
    nsl = n_req * cap
    crows = nsl // NCH
    nslp = n_req * slot_stride(cap)
    chunk = send_tail.shape[1]
    smem = pl.BlockSpec(memory_space=pltpu.SMEM)
    vmem = pl.BlockSpec(memory_space=pltpu.VMEM)
    anym = pl.BlockSpec(memory_space=pl.ANY)
    dma = pltpu.SemaphoreType.DMA
    n_x = n_tp // 2

    def bf(*shape):
        return pltpu.VMEM(shape, BF16)

    return pl.pallas_call(
        moe_kernel,
        out_shape=(
            jax.ShapeDtypeStruct((n_tp, rows, 128), BF16),
            jax.ShapeDtypeStruct((n_tp, 16, 128), BF16),
            jax.ShapeDtypeStruct((n_req, chunk, 128), BF16),
        ),
        in_specs=[smem] + [vmem] * 6 + [anym] * 5,
        out_specs=(vmem, vmem, vmem),
        scratch_shapes=[
            bf(rows, 128), bf(*w_out.shape), bf(*wg_t.shape), bf(*wu_t.shape), bf(*wd.shape),
            bf(n_req, chunk, 128), bf(n_req, chunk, 128),
            bf(2, n_x, rows, 128), bf(n_x, rows, 128), bf(n_x, rows, 128), bf(n_x, rows, 128),
            pltpu.VMEM((8, rows), F32), pltpu.VMEM((n_tp, 8, rows), F32),
            bf(nslp, 128), bf(nslp, 128), bf(NCH, n_tp, crows, 128),
            bf(NCH, 2, n_x, crows, 128), bf(NCH, n_x, crows, 128), bf(NCH, n_x, crows, 128), bf(NCH, n_x, crows, 128),
            bf(nslp, 128), bf(nslp, 128),
            bf(16, 128), bf(n_req, 16, 128),
        ]
        + [dma((5,))]
        + [dma((n_req,))] * 4
        + [dma((n_x,))] * 4
        + [dma((n_tp,))] * 2
        + [dma((n_req,))] * 2
        + [dma((NCH, n_x))] * 8
        + [dma((n_req,))] * 4
        + [dma((n_x,))] * 4
        + [dma((n_tp,))] * 2,
        compiler_params=pltpu.CompilerParams(collective_id=0, has_side_effects=True, vmem_limit_bytes=56 << 20),
        name="moe_exchange",
    )(meta, head, gain.reshape(1, -1), router_t, ids_t, slots, send_tail, hidden, w_out, wg_t, wu_t, wd)


def place_kernel(meta_s, mix_ref, came_ref, got_ref, tail_in, out_ref, tail_out, sems):
    rows = tail_out.shape[1]

    def put(k, kv):
        return pltpu.make_async_copy(got_ref.at[k, kv], tail_out.at[kv, meta_s[0, MIG + k]], sems.at[k, kv])

    for k in range(MIG):
        for kv in range(2):

            @pl.when(meta_s[0, MIG + k] < rows)
            def _():
                put(k, kv).start()

    for tt in range(mix_ref.shape[0]):
        out_ref[:, tt * 128 : (tt + 1) * 128] = mix_ref[tt]
    sub = lax.broadcasted_iota(jnp.int32, (16, 128), 0)
    for k in range(MIG):
        slot = meta_s[0, MIG + k]

        @pl.when(slot < rows)
        def _():
            base = pl.multiple_of((slot >> 4) << 4, 16)
            for tt in range(mix_ref.shape[0]):
                cols = slice(tt * 128, (tt + 1) * 128)
                row = came_ref[tt].astype(F32)[k : k + 1, :]
                w = out_ref[pl.ds(base, 16), cols].astype(F32)
                out_ref[pl.ds(base, 16), cols] = jnp.where(sub == slot - base, row, w).astype(BF16)

    for k in range(MIG):
        for kv in range(2):

            @pl.when(meta_s[0, MIG + k] < rows)
            def _():
                put(k, kv).wait()


def place_call(meta, mix, came, got, tail):
    n_tp, rows, wd = mix.shape
    vmem = pl.BlockSpec(memory_space=pltpu.VMEM)
    return pl.pallas_call(
        place_kernel,
        out_shape=(
            jax.ShapeDtypeStruct((rows, n_tp * wd), BF16),
            jax.ShapeDtypeStruct(tail.shape, tail.dtype),
        ),
        in_specs=[pl.BlockSpec(memory_space=pltpu.SMEM), vmem, vmem, vmem, pl.BlockSpec(memory_space=pl.ANY)],
        out_specs=(vmem, pl.BlockSpec(memory_space=pl.ANY)),
        scratch_shapes=[pltpu.SemaphoreType.DMA((MIG, 2))],
        input_output_aliases={4: 1},
        name="place_rows",
    )(meta, mix, came, got, tail)


def body(
    hidden_in, prompt_kv, tail_kv, group_of, prompt_len, tail_len, bucket_of, bias_table, attn_gain, w_query, w_key,
    w_value, w_out, ffn_gain, router_weight, expert_ids, w_gate, w_up, w_down, new_slot,
):
    n_req = lax.axis_size("req")
    n_tp = lax.axis_size("tp")
    ids_t = expert_ids.T
    tail_new, head, send_tail, slots, meta = attention_call(
        hidden_in, attn_gain, w_query, w_key, w_value, group_of, prompt_len, tail_len, bucket_of, bias_table.T,
        new_slot, ids_t, prompt_kv, tail_kv,
    )
    pieces = send_tail.reshape(n_req, -1, send_tail.shape[-1])
    mix, came, got = moe_call(
        n_req, n_tp, meta, head, ffn_gain, router_weight.T, ids_t, slots, pieces, hidden_in, w_out,
        w_gate[0].T, w_up[0].T, w_down[0],
    )
    return place_call(meta, mix, came, got.reshape(send_tail.shape), tail_new)


def solution(mesh):
    return jax.shard_map(
        body,
        mesh=mesh,
        in_specs=(
            P("req", None), P(None, "req", None, "tp"), P(None, "req", None, "tp"), P("req"), P("req"), P("req"), P(),
            P(None, "tp"), P(), P(None, "tp"), P(None, "tp"), P(None, "tp"), P("tp", None), P(), P(), P("req", None),
            P("req", None, "tp"), P("req", None, "tp"), P("req", "tp", None), P(),
        ),
        out_specs=(P("req", None), P(None, "req", None, "tp")),
        check_vma=False,
    )
```

```python
import functools

import jax
import jax.numpy as jnp
from jax import lax
from jax.experimental import pallas as pl
from jax.experimental.pallas import tpu as pltpu
from jax.sharding import PartitionSpec as P

F32 = jnp.float32
BF16 = jnp.bfloat16
EPS = 1e-06
NEG = -1e30
RB = 32
UB = 4
TB = 8
TOP = 2
MIG = 4


def slot_stride(cap):
    return -(-cap // 16) * 16


def col_form(row):
    n = row.shape[1]
    return jnp.transpose(jnp.broadcast_to(row.astype(F32), (128, n)))


def migration_tables(ns_ref, meta_ref, rows):
    me = lax.axis_index("req")
    per = rows // 128
    tiles = ns_ref[...].astype(F32)
    shape = tiles.shape
    lane = lax.broadcasted_iota(jnp.int32, shape, 1).astype(F32)
    sub = lax.broadcasted_iota(jnp.int32, shape, 0)
    moved = tiles != sub.astype(F32) * 128.0 + lane
    where_to = jnp.floor(tiles * (1.0 / rows))
    goes = jnp.max(jnp.where(moved, where_to, -1.0), axis=1, keepdims=True)
    src = jnp.max(jnp.where(goes == lane, (sub // per).astype(F32), -1.0), axis=0, keepdims=True)
    src = jnp.where(src < 0.0, lane[0:1], src)

    mine = ns_ref[pl.ds(me * per, per), :].astype(F32)
    row = jnp.concatenate([mine[i : i + 1] for i in range(per)], axis=1)
    col = col_form(row)
    base = (me * rows).astype(F32)
    rid = lax.broadcasted_iota(jnp.int32, (rows, 128), 0).astype(F32)
    rlane = lax.broadcasted_iota(jnp.int32, (rows, 128), 1).astype(F32)
    moved_col = col != rid + base
    order = jnp.zeros((rows, 128), F32)
    place = jnp.zeros((rows, 128), F32)
    for i in range(per):
        part = row[:, i * 128 : (i + 1) * 128]
        other = rlane + float(i * 128)
        moved_row = part != other[0:1] + base
        order = order + jnp.where(moved_row & (part < col), 1.0, 0.0)
        place = place + jnp.where(moved_row & (other < rid), 1.0, 0.0)
    order = jnp.sum(order, axis=1, keepdims=True)
    place = jnp.sum(place, axis=1, keepdims=True)
    out = float(rows)
    send = jnp.min(jnp.where(moved_col & (order == rlane), rid, out), axis=0, keepdims=True)
    send = jnp.minimum(send, out - 1.0)
    vac = jnp.min(jnp.where(moved_col & (place + float(MIG) == rlane), rid, out), axis=0, keepdims=True)
    idx = jnp.where(rlane[0:1] < float(MIG), send, vac)
    s8 = lax.broadcasted_iota(jnp.int32, (8, 128), 0)
    meta_ref[...] = jnp.where(s8 == 0, idx, jnp.where(s8 == 1, src, 0.0)).astype(jnp.int32)


def attn_kernel(
    tl_s, tab_s, plen_s, bkt_s,
    gain_ref, grp_ref, tlr_ref, ids_ref, ns_ref, hid_any, wq_any, wk_any, wv_any, pkv_any, tail_any,
    tail_out, head_ref, send_ref, slot_ref, meta_ref,
    hid_v, wcat, pkv_v, buf, q16, kvn, lhs, kcat, sco, prob, posb, plb, tlb, dtab, tbias, opart, mpart, lpart,
    first_s, meta_s, s_in, s_tin, s_tout, s_meta,
):
    rows = hid_v.shape[0]
    nb = rows // 8
    groups = pkv_v.shape[1]
    pre = pkv_v.shape[2]
    nbuck = tab_s.shape[1]
    mig = send_ref.shape[0]
    span = bkt_s.shape[0]
    nblk = rows // RB
    loads = [
        pltpu.make_async_copy(hid_any, hid_v, s_in.at[0]),
        pltpu.make_async_copy(wq_any, wcat.at[:, 0:128], s_in.at[1]),
        pltpu.make_async_copy(wk_any, wcat.at[:, 128:256], s_in.at[2]),
        pltpu.make_async_copy(wv_any, wcat.at[:, 256:384], s_in.at[3]),
        pltpu.make_async_copy(pkv_any.at[0], pkv_v.at[0], s_in.at[4]),
        pltpu.make_async_copy(pkv_any.at[1], pkv_v.at[1], s_in.at[5]),
    ]
    for cp in loads:
        cp.start()

    def t_in(s, kv):
        sl = pl.ds(s * RB, RB)
        return pltpu.make_async_copy(tail_any.at[kv, sl], buf.at[kv, sl], s_tin.at[s, kv])

    def t_out(s, kv):
        sl = pl.ds(s * RB, RB)
        return pltpu.make_async_copy(buf.at[kv, sl], tail_out.at[kv, sl], s_tout.at[s, kv])

    @pl.loop(0, nblk)
    def _(s):
        t_in(s, 0).start()
        t_in(s, 1).start()

    for k in range(nbuck):
        first_s[k] = span

    @pl.loop(0, span, unroll=8)
    def _(i):
        d = span - 1 - i
        first_s[bkt_s[d]] = d

    nd = dtab.shape[2] // 128
    dist = [lax.broadcasted_iota(jnp.int32, (8, 128), 1) + c * 128 for c in range(nd)]
    d0 = [jnp.full((8, 128), tab_s[0, 0], F32) for _ in range(nd)]
    d1 = [jnp.full((8, 128), tab_s[1, 0], F32) for _ in range(nd)]
    for k in range(1, nbuck):
        for c in range(nd):
            ge = dist[c] >= first_s[k]
            d0[c] = jnp.where(ge, tab_s[0, k], d0[c])
            d1[c] = jnp.where(ge, tab_s[1, k], d1[c])
    for c in range(nd):
        dtab[0, :, c * 128 : (c + 1) * 128] = d0[c]
        dtab[1, :, c * 128 : (c + 1) * 128] = d1[c]

    migration_tables(ns_ref, meta_ref, rows)
    meta_copy = pltpu.make_async_copy(meta_ref, meta_s, s_meta)
    meta_copy.start()

    g = col_form(grp_ref[...])
    tl = col_form(tlr_ref[...])
    pln = jnp.zeros_like(g)
    for i in range(groups):
        pln = jnp.where(g == float(i), plen_s[i].astype(F32), pln)
    posb[...] = (pln + tl).astype(jnp.int32)
    plb[...] = pln.astype(jnp.int32)
    tlb[...] = tl.astype(jnp.int32)
    g2 = jnp.broadcast_to(g.reshape(nb, 1, 8, 128), (nb, 2, 8, 128)).reshape(2 * rows, 128)

    e0 = col_form(ids_ref[0:1, :])
    e1 = col_form(ids_ref[1:2, :])
    ln = lax.broadcasted_iota(jnp.int32, (rows, 128), 1).astype(F32)
    hit0 = ln == e0
    hit1 = ln == e1
    ri = lax.broadcasted_iota(jnp.int32, (rows, rows), 0)
    ci = lax.broadcasted_iota(jnp.int32, (rows, rows), 1)
    lower = (ci < ri).astype(F32).astype(BF16)
    o0 = hit0.astype(F32)
    o1 = hit1.astype(F32)
    cum0 = jnp.dot(lower, o0.astype(BF16), preferred_element_type=F32)
    cum1 = jnp.dot(lower, o1.astype(BF16), preferred_element_type=F32)
    tot0 = jnp.sum(o0, axis=0, keepdims=True)
    p0 = jnp.sum(jnp.where(hit0, cum0, 0.0), axis=1, keepdims=True)
    p1 = jnp.sum(jnp.where(hit1, cum1 + tot0, 0.0), axis=1, keepdims=True)
    stride = float(slot_stride(5 * rows * TOP // (4 * 16)))
    slot_ref[0] = e0 * stride + p0
    slot_ref[1] = e1 * stride + p1

    for cp in loads[:4]:
        cp.wait()
    h = hid_v[...].astype(F32)
    ms = jnp.mean(h * h, axis=-1, keepdims=True)
    n1 = (h * lax.rsqrt(ms + EPS) * gain_ref[...]).astype(BF16)
    qkv = jnp.dot(n1, wcat[...], preferred_element_type=F32).astype(BF16).astype(F32)
    q = qkv[:, 0:128]
    kvn[0] = qkv[:, 128:256]
    kvn[1] = qkv[:, 256:384]
    sub16 = lax.broadcasted_iota(jnp.int32, (16, 128), 0)

    @pl.loop(0, nblk)
    def _(s):
        t_in(s, 0).wait()
        t_in(s, 1).wait()
        for i in range(RB):
            r = s * RB + i
            length = tl_s[r]
            base = pl.multiple_of((length >> 4) << 4, 16)
            for kv in range(2):
                w = buf[kv, r, pl.ds(base, 16), :].astype(F32)
                row = kvn[kv, pl.ds(r, 1), :]
                buf[kv, r, pl.ds(base, 16), :] = jnp.where(sub16 == length - base, row, w).astype(BF16)
        t_out(s, 0).start()
        t_out(s, 1).start()

    lane = lax.broadcasted_iota(jnp.int32, (nb, 2, 8, 128), 3)
    head = lax.broadcasted_iota(jnp.int32, (nb, 2, 8, 128), 1)
    qh = jnp.broadcast_to((q * 0.125).reshape(nb, 1, 8, 128), (nb, 2, 8, 128))
    qh = jnp.where((lane // 64) == head, qh, 0.0).reshape(2 * rows, 128)
    q16[...] = qh.astype(BF16)
    loads[4].wait()
    for i in range(groups):
        lhs[:, i * 128 : (i + 1) * 128] = jnp.where(g2 == float(i), qh, 0.0).astype(BF16)
        kcat[:, i * 128 : (i + 1) * 128] = pkv_v[0, i]
    sco[...] = lax.dot_general(lhs[...], kcat[...], (((1,), (1,)), ((), ())), preferred_element_type=F32)

    def take(tab, i):
        return jnp.take_along_axis(tab, i, axis=1, mode="promise_in_bounds")

    nch = pre // 128

    ln = lax.broadcasted_iota(jnp.int32, (8, 128), 1)
    sub = lax.broadcasted_iota(jnp.int32, (8, 128), 0)
    mine = (ln >> 6) == (sub & 1)

    @pl.loop(0, nb // UB)
    def _(i):
        at = [i * UB + n for n in range(UB)]
        pos = [posb[pl.ds(b * 8, 8), :] for b in at]
        pb = [plb[pl.ds(b * 8, 8), :] for b in at]
        tb = [tlb[pl.ds(b * 8, 8), :] for b in at]
        raw = [
            [[sco[pl.ds(b * 16 + hh * 8, 8), c * 128 : (c + 1) * 128] for c in range(nch)] for hh in range(2)]
            for b in at
        ]
        tabs = [[dtab[hh, :, k * 128 : (k + 1) * 128] for k in range(nd)] for hh in range(2)]
        out = []
        for n in range(UB):
            low = pos[n] & 127
            gi = (low - ln) & 127
            blk = (pos[n] >> 7) - (ln > low).astype(jnp.int32)
            is_blk = [blk == k for k in range(nd)]
            td = tb[n] - (ln & 63)
            valid = (td >= 0) & mine
            td = jnp.maximum(td, 0)
            for hh in range(2):
                tail = jnp.where(valid, take(tabs[hh][0], td), NEG)
                gs = [take(tabs[hh][k], gi) for k in range(nd)]
                s = []
                for c in range(nch):
                    bias = gs[0]
                    for k in range(1, nd - c):
                        bias = jnp.where(is_blk[k + c], gs[k], bias)
                    s.append(jnp.where(ln + c * 128 < pb[n], raw[n][hh][c] + bias, NEG))
                mx = jnp.max(functools.reduce(jnp.maximum, s), axis=1, keepdims=True)
                e = [jnp.exp(v - mx) for v in s]
                tot = jnp.sum(functools.reduce(jnp.add, e), axis=1, keepdims=True)
                out.append((tail, mx, e, tot))
        for n in range(UB):
            for hh in range(2):
                tail, mx, e, tot = out[n * 2 + hh]
                rs = pl.ds(at[n] * 16 + hh * 8, 8)
                tbias[rs, :] = tail
                mpart[rs, :] = jnp.broadcast_to(mx, (8, 128))
                lpart[rs, :] = jnp.broadcast_to(tot, (8, 128))
            for c in range(nch):
                prob[pl.ds(at[n] * 16, 16), c * 128 : (c + 1) * 128] = jnp.concatenate(
                    [out[n * 2][2][c], out[n * 2 + 1][2][c]], axis=0
                ).astype(BF16)

    loads[5].wait()
    acc = jnp.zeros((2 * rows, 128), F32)
    for i in range(0, groups, 2):
        rhs = jnp.concatenate([pkv_v[1, i], pkv_v[1, i + 1]], axis=1)
        o = jnp.dot(prob[...], rhs, preferred_element_type=F32)
        acc = jnp.where(g2 == float(i), o[:, 0:128], acc)
        acc = jnp.where(g2 == float(i + 1), o[:, 128:256], acc)
    opart[...] = acc

    pair = lax.rem(sub16, 8) // 2
    lane4 = lax.broadcasted_iota(jnp.int32, (TB, 8, 128), 2)

    @pl.loop(0, nb // TB)
    def _(i):
        rs = pl.ds(pl.multiple_of(i * TB * 16, TB * 16), TB * 16)
        scs = []
        for n in range(TB):
            b = i * TB + n
            kb = buf[0, pl.ds(b * 8, 8)].reshape(512, 128)
            qb = q16[pl.ds(pl.multiple_of(b * 16, 16), 16), :]
            s4 = lax.dot_general(qb, kb, (((1,), (1,)), ((), ())), preferred_element_type=F32)
            sc = s4[:, 0:128]
            for c in range(1, 4):
                sc = jnp.where(pair == c, s4[:, c * 128 : (c + 1) * 128], sc)
            scs.append(sc)
        sc = jnp.concatenate(scs, axis=0) + tbias[rs, :]
        mp = mpart[rs, :]
        mx = jnp.maximum(jnp.max(sc, axis=1, keepdims=True), mp)
        e = jnp.exp(sc - mx)
        ap = jnp.exp(mp - mx)
        tot = jnp.sum(e, axis=1, keepdims=True) + lpart[rs, :] * ap
        os = []
        for n in range(TB):
            b = i * TB + n
            vb = buf[1, pl.ds(b * 8, 8)].reshape(512, 128)
            en = e[n * 16 : (n + 1) * 16]
            p4 = jnp.concatenate([jnp.where(pair == c, en, 0.0) for c in range(4)], axis=1).astype(BF16)
            os.append(jnp.dot(p4, vb, preferred_element_type=F32))
        o = (jnp.concatenate(os, axis=0) + opart[rs, :] * ap) / tot
        o = o.reshape(TB, 2, 8, 128)
        o = jnp.where(lane4 < 64, o[:, 0], o[:, 1]).reshape(TB * 8, 128)
        head_ref[pl.ds(pl.multiple_of(i * TB * 8, TB * 8), TB * 8), :] = o

    meta_copy.wait()
    for m in range(mig):
        for kv in range(2):
            send_ref[m, kv] = buf[kv, meta_s[0, m]]

    @pl.loop(0, nblk)
    def _(s):
        t_out(s, 0).wait()
        t_out(s, 1).wait()


def attention_call(
    hidden_in, gain, wq, wk, wv, group_of, prompt_len, tail_len, bucket_of, table_t, new_slot, ids_t, prompt_kv, tail_kv
):
    rows, width = hidden_in.shape
    smem = pl.BlockSpec(memory_space=pltpu.SMEM)
    vmem = pl.BlockSpec(memory_space=pltpu.VMEM)
    anym = pl.BlockSpec(memory_space=pl.ANY)
    _, groups, pre, wd = prompt_kv.shape
    tail_rows = tail_kv.shape[2]
    nd = -(-bucket_of.shape[0] // 128)
    nblk = rows // RB
    dma = pltpu.SemaphoreType.DMA
    return pl.pallas_call(
        attn_kernel,
        out_shape=(
            jax.ShapeDtypeStruct(tail_kv.shape, BF16),
            jax.ShapeDtypeStruct((rows, wd), F32),
            jax.ShapeDtypeStruct((MIG, 2, tail_rows, wd), BF16),
            jax.ShapeDtypeStruct((2, rows, 128), F32),
            jax.ShapeDtypeStruct((8, 128), jnp.int32),
        ),
        in_specs=[smem] * 4 + [vmem] * 5 + [anym] * 6,
        out_specs=(anym, vmem, vmem, vmem, vmem),
        scratch_shapes=[
            pltpu.VMEM((rows, width), BF16),
            pltpu.VMEM((width, 3 * wd), BF16),
            pltpu.VMEM(prompt_kv.shape, BF16),
            pltpu.VMEM(tail_kv.shape, BF16),
            pltpu.VMEM((2 * rows, wd), BF16),
            pltpu.VMEM((2, rows, wd), F32),
            pltpu.VMEM((2 * rows, groups * wd), BF16),
            pltpu.VMEM((pre, groups * wd), BF16),
            pltpu.VMEM((2 * rows, pre), F32),
            pltpu.VMEM((2 * rows, pre), BF16),
            pltpu.VMEM((rows, 128), jnp.int32),
            pltpu.VMEM((rows, 128), jnp.int32),
            pltpu.VMEM((rows, 128), jnp.int32),
            pltpu.VMEM((2, 8, nd * 128), F32),
            pltpu.VMEM((2 * rows, 128), F32),
            pltpu.VMEM((2 * rows, 128), F32),
            pltpu.VMEM((2 * rows, 128), F32),
            pltpu.VMEM((2 * rows, 128), F32),
            pltpu.SMEM((table_t.shape[1],), jnp.int32),
            pltpu.SMEM((8, 128), jnp.int32),
            dma((6,)),
            dma((nblk, 2)),
            dma((nblk, 2)),
            dma,
        ],
        compiler_params=pltpu.CompilerParams(vmem_limit_bytes=60 << 20),
        name="attention_tails",
    )(
        tail_len, table_t, prompt_len, bucket_of,
        gain.reshape(1, -1), group_of.reshape(1, -1), tail_len.reshape(1, -1), ids_t, new_slot.reshape(-1, 128),
        hidden_in, wq, wk, wv, prompt_kv, tail_kv,
    )


MESH = pl.DeviceIdType.MESH
NCH = 2


def moe_kernel(
    meta_s,
    head_ref, gain_ref, router_ref, ids_ref, slot_ref, tail_ref, hid_any, wout_any, wg_any, wu_any, wd_any,
    mix, came, got,
    hid_v, wout_v, wg_v, wu_v, wd_v,
    t1, t2, part, psib, psend, precv, stat, statr, dsend, drecv, xall, ypart, ysib, ysend, yrecv, rsend, rrecv, mvs, mvr,
    s_in, s_t1, r_t1, s_t2, r_t2, s_ps, r_ps, s_px, r_px, s_st, r_st, s_d, r_d, s_gx, r_gx, s_gs, r_gs,
    s_ys, r_ys, s_yx, r_yx, s_r, r_r, s_mv, r_mv, s_ox, r_ox, s_os, r_os, s_cm, r_cm,
):
    r = lax.axis_index("req")
    t = lax.axis_index("tp")
    n_req = t1.shape[0]
    n_tp = mix.shape[0]
    n_x = n_tp // 2
    rows = hid_v.shape[0]
    width = wout_v.shape[1]
    crows = xall.shape[2]
    per = n_req // NCH
    cap = crows // per
    nslp = dsend.shape[0]
    capp = nslp // n_req
    c = lax.rem(t, 2)
    x = t // 2
    sib = x * 2 + 1 - c
    lanes = pl.ds(pl.multiple_of(t * 128, 128), 128)

    loads = [
        pltpu.make_async_copy(wout_any, wout_v, s_in.at[0]),
        pltpu.make_async_copy(hid_any.at[:, lanes], hid_v, s_in.at[1]),
        pltpu.make_async_copy(wg_any, wg_v, s_in.at[2]),
        pltpu.make_async_copy(wu_any, wu_v, s_in.at[3]),
        pltpu.make_async_copy(wd_any, wd_v, s_in.at[4]),
    ]
    for cp in loads:
        cp.start()

    def tp_copy(src, dst, ss, rs, peer):
        return pltpu.make_async_remote_copy(
            src_ref=src, dst_ref=dst, send_sem=ss, recv_sem=rs, device_id=(r, peer), device_id_type=MESH
        )

    def req_copy(src, dst, ss, rs, peer):
        return pltpu.make_async_remote_copy(
            src_ref=src, dst_ref=dst, send_sem=ss, recv_sem=rs, device_id=(peer, t), device_id_type=MESH
        )

    def xpeer(d):
        return lax.rem(x + d, n_x) * 2 + c

    def xfrom(d):
        return lax.rem(x + n_x - d, n_x) * 2 + c

    barrier = pltpu.get_barrier_semaphore()

    @pl.loop(1, n_tp)
    def _(d):
        pl.semaphore_signal(barrier, inc=1, device_id=(r, lax.rem(t + d, n_tp)), device_id_type=MESH)

    @pl.loop(1, n_req)
    def _(d):
        pl.semaphore_signal(barrier, inc=1, device_id=(lax.rem(r + d, n_req), t), device_id_type=MESH)

    head = head_ref[...].astype(BF16)
    loads[0].wait()
    for tt in range(n_tp):
        part[tt % 2, tt // 2] = jnp.dot(
            head, wout_v[:, tt * 128 : (tt + 1) * 128], preferred_element_type=F32
        ).astype(BF16)

    pl.semaphore_wait(barrier, n_tp - 1 + n_req - 1)

    def rs_sib(d, buf, dst, ss, rs):
        xx = lax.rem(x + d, n_x)
        return tp_copy(buf.at[1 - c, xx], dst.at[xx], ss.at[d], rs.at[d], sib)

    def rs_x(d, buf, dst, ss, rs):
        return tp_copy(buf.at[d], dst.at[d], ss.at[d], rs.at[d], xpeer(d))

    def rs_start(buf, bsib, ss1, rs1):
        for d in (2, 1, 3, 0):
            rs_sib(d, buf, bsib, ss1, rs1).start()

    def rs_send(buf, bsib, bsend, brecv, ss1, rs1, ss2, rs2):
        for d in (2, 1, 3):
            xx = lax.rem(x + d, n_x)
            rs_sib(d, buf, bsib, ss1, rs1).wait_recv()
            bsend[d] = (buf[c, xx].astype(F32) + bsib[xx].astype(F32)).astype(BF16)
            rs_x(d, bsend, brecv, ss2, rs2).start()

    def rs_total(buf, bsib, bsend, brecv, ss1, rs1, ss2, rs2):
        rs_sib(0, buf, bsib, ss1, rs1).wait_recv()
        tot = buf[c, x].astype(F32) + bsib[x].astype(F32)
        for d in (1, 3, 2):
            rs_x(d, bsend, brecv, ss2, rs2).wait_recv()
            tot = tot + brecv[d].astype(F32)
        return tot

    def rs_finish(buf, bsib, bsend, brecv, ss1, rs1, ss2, rs2):
        for d in (0, 1, 2, 3):
            rs_sib(d, buf, bsib, ss1, rs1).wait_send()
        for d in (1, 2, 3):
            rs_x(d, bsend, brecv, ss2, rs2).wait_send()

    def ag_x(d, buf, ss, rs):
        return tp_copy(buf.at[t], buf.at[t], ss.at[d], rs.at[d], xpeer(d))

    def ag_s(d, buf, ss, rs):
        who = xfrom(d)
        return tp_copy(buf.at[who], buf.at[who], ss.at[d], rs.at[d], sib)

    def ag_start(buf, ss1, rs1, ss2, rs2):
        for d in (2, 1, 3):
            ag_x(d, buf, ss1, rs1).start()
        ag_s(0, buf, ss2, rs2).start()

    def ag_pass(buf, ss1, rs1, ss2, rs2):
        for d in (1, 3, 2):
            who = xfrom(d)
            tp_copy(buf.at[who], buf.at[who], ss1.at[d], rs1.at[d], xpeer(d)).wait_recv()
            ag_s(d, buf, ss2, rs2).start()

    def ag_wait(buf, ss1, rs1, ss2, rs2):
        for d in (0, 1, 3, 2):
            mine = xfrom(d)
            other = lax.rem(x + n_x - d, n_x) * 2 + 1 - c
            tp_copy(buf.at[mine], buf.at[other], ss2.at[d], rs2.at[d], sib).wait_recv()

    def ag_finish(buf, ss1, rs1, ss2, rs2):
        for d in (1, 2, 3):
            ag_x(d, buf, ss1, rs1).wait_send()
        for d in (0, 1, 2, 3):
            ag_s(d, buf, ss2, rs2).wait_send()

    attn_rs = (part, psib, psend, precv, s_ps, r_ps, s_px, r_px)
    rs_start(part, psib, s_ps, r_ps)
    rs_send(*attn_rs)

    def t1_copy(d):
        j = lax.rem(r + d, n_req)
        return req_copy(tail_ref.at[j], t1.at[r], s_t1.at[d], r_t1.at[d], j)

    loads[1].wait()
    resid = (hid_v[...].astype(F32) + rs_total(*attn_rs)).astype(BF16)

    s0 = slot_ref[0]
    s1 = slot_ref[1]
    lnf = lax.broadcasted_iota(jnp.int32, (rows, 128), 1).astype(F32)
    for k in range(nslp // 128):
        pick = (s0 == lnf + float(k * 128)) | (s1 == lnf + float(k * 128))
        dsend[k * 128 : (k + 1) * 128, :] = lax.dot_general(
            pick.astype(F32).astype(BF16), resid, (((0,), (0,)), ((), ())), preferred_element_type=F32
        ).astype(BF16)

    def block(j):
        return pl.ds(pl.multiple_of(j * capp, 16), capp)

    def d_copy(d):
        j = lax.rem(r + d, n_req)
        return req_copy(dsend.at[block(j)], drecv.at[block(r)], s_d.at[d], r_d.at[d], j)

    @pl.loop(1, n_req)
    def _(d):
        d_copy(d).start()

    drecv[block(r), :] = dsend[block(r), :]

    @pl.loop(1, n_req)
    def _(d):
        t1_copy(d).start()

    t1[r] = tail_ref[r]

    rf = resid.astype(F32)
    u = rf * gain_ref[:, lanes]
    lg = lax.dot_general(
        u.astype(BF16), router_ref[:, lanes], (((1,), (1,)), ((), ())), preferred_element_type=F32
    )
    e0 = col_form(ids_ref[0:1, :])
    e1 = col_form(ids_ref[1:2, :])
    n_e = lg.shape[1]
    ex = lnf[:, 0:n_e]
    diff = jnp.sum(
        jnp.where(ex == e0[:, 0:n_e], lg, 0.0) - jnp.where(ex == e1[:, 0:n_e], lg, 0.0), axis=1, keepdims=True
    )
    sq = jnp.sum(rf * rf, axis=1, keepdims=True)
    stat[...] = jnp.transpose(jnp.where(lnf == 0.0, sq, jnp.where(lnf == 1.0, diff, 0.0)))[0:8]

    def st_copy(d):
        return tp_copy(stat, statr.at[d], s_st.at[d], r_st.at[d], lax.rem(t + d, n_tp))

    for d in range(1, n_tp):
        st_copy(d).start()

    @pl.loop(1, n_req)
    def _(d):
        d_copy(d).wait_recv()

    def x_ag(h):
        return (xall.at[h], s_gx.at[h], r_gx.at[h], s_gs.at[h], r_gs.at[h])

    for h in range(NCH):
        xall[h, t] = jnp.concatenate(
            [drecv[j * capp : (j + 1) * capp, :].astype(F32)[0:cap] for j in range(h * per, (h + 1) * per)], axis=0
        ).astype(BF16)
        ag_start(*x_ag(h))

    @pl.loop(1, n_req)
    def _(d):
        t1_copy(d).wait_recv()

    @pl.loop(0, n_req)
    def _(j):
        t2[j] = t1[meta_s[1, j]]

    def t2_copy(d):
        j = lax.rem(r + d, n_req)
        return req_copy(t2.at[j], got.at[r], s_t2.at[d], r_t2.at[d], j)

    @pl.loop(1, n_req)
    def _(d):
        t2_copy(d).start()

    got[r] = t2[r]

    tot = stat[...]
    for d in range(1, n_tp):
        st_copy(d).wait_recv()
        tot = tot + statr[d]
    tot = jnp.transpose(jnp.concatenate([tot, jnp.zeros((120, rows), F32)], axis=0))
    gate = jax.nn.sigmoid(tot[:, 1:2] * lax.rsqrt(tot[:, 0:1] * (1.0 / width) + EPS))

    for cp in loads[2:]:
        cp.wait()

    def ffn(h):
        xm = jnp.concatenate([xall[h, tt] for tt in range(n_tp)], axis=1).astype(F32)
        ms = jnp.mean(xm * xm, axis=-1, keepdims=True)
        nm = (xm * lax.rsqrt(ms + EPS) * gain_ref[...]).astype(BF16)
        gh = lax.dot_general(nm, wg_v[...], (((1,), (1,)), ((), ())), preferred_element_type=F32)
        uh = lax.dot_general(nm, wu_v[...], (((1,), (1,)), ((), ())), preferred_element_type=F32)
        act = (jax.nn.gelu(gh, approximate=True) * uh).astype(BF16)
        y = jnp.dot(act, wd_v[...], preferred_element_type=F32).astype(BF16)
        for tt in range(n_tp):
            ypart[h, tt % 2, tt // 2] = y[:, tt * 128 : (tt + 1) * 128]

    def y_rs(h):
        return (
            ypart.at[h], ysib.at[h], ysend.at[h], yrecv.at[h], s_ys.at[h], r_ys.at[h], s_yx.at[h], r_yx.at[h]
        )

    ag_pass(*x_ag(0))
    for h in range(NCH):
        ag_wait(*x_ag(h))
        ffn(h)
        rs_start(ypart.at[h], ysib.at[h], s_ys.at[h], r_ys.at[h])
        if h + 1 < NCH:
            ag_pass(*x_ag(h + 1))
        rs_send(*y_rs(h))

    def r_copy(d):
        j = lax.rem(r + d, n_req)
        return req_copy(rsend.at[block(j)], rrecv.at[block(r)], s_r.at[d], r_r.at[d], j)

    pad = jnp.zeros((capp - cap, 128), F32)
    for h in range(NCH):
        tot = rs_total(*y_rs(h))
        for i in range(per):
            j = h * per + i
            rsend[j * capp : (j + 1) * capp, :] = jnp.concatenate(
                [tot[i * cap : (i + 1) * cap], pad], axis=0
            ).astype(BF16)

        @pl.loop(h * per, (h + 1) * per)
        def _(j):
            @pl.when(j != r)
            def _():
                r_copy(lax.rem(j + n_req - r, n_req)).start()

    rrecv[block(r), :] = rsend[block(r), :]

    @pl.loop(1, n_req)
    def _(d):
        r_copy(d).wait_recv()

    p0 = jnp.zeros((rows, 128), F32)
    p1 = jnp.zeros((rows, 128), F32)
    for k in range(nslp // 128):
        res = rrecv[k * 128 : (k + 1) * 128, :]
        p0 = p0 + jnp.dot((s0 == lnf + float(k * 128)).astype(F32).astype(BF16), res, preferred_element_type=F32)
        p1 = p1 + jnp.dot((s1 == lnf + float(k * 128)).astype(F32).astype(BF16), res, preferred_element_type=F32)
    mixed = (rf + gate * p0 + (1.0 - gate) * p1).astype(BF16)

    kk = lax.broadcasted_iota(jnp.int32, (16, rows), 0)
    rr = lax.broadcasted_iota(jnp.int32, (16, rows), 1)
    pick = jnp.zeros((16, rows), F32)
    for k in range(MIG):
        pick = jnp.where((kk == k) & (rr == meta_s[0, k]), 1.0, pick)
    mvs[...] = jnp.dot(pick.astype(BF16), mixed, preferred_element_type=F32).astype(BF16)

    def mv_copy(d):
        j = lax.rem(r + d, n_req)
        return req_copy(mvs, mvr.at[r], s_mv.at[d], r_mv.at[d], j)

    mix[t] = mixed
    o_ag = (mix, s_ox, r_ox, s_os, r_os)
    ag_start(*o_ag)

    @pl.loop(1, n_req)
    def _(d):
        mv_copy(d).start()

    mvr[r] = mvs[...]

    def cm_copy(d):
        return tp_copy(came.at[t], came.at[t], s_cm.at[d], r_cm.at[d], lax.rem(t + d, n_tp))

    @pl.loop(1, n_req)
    def _(d):
        mv_copy(d).wait_recv()

    came[t] = mvr[meta_s[1, r]]
    for d in range(1, n_tp):
        cm_copy(d).start()

    ag_pass(*o_ag)
    ag_wait(*o_ag)
    for d in range(1, n_tp):
        who = lax.rem(t + n_tp - d, n_tp)
        tp_copy(came.at[who], came.at[who], s_cm.at[d], r_cm.at[d], who).wait_recv()

    @pl.loop(1, n_req)
    def _(d):
        t2_copy(d).wait_recv()

    rs_finish(*attn_rs)
    for h in range(NCH):
        rs_finish(*y_rs(h))
        ag_finish(*x_ag(h))
    ag_finish(*o_ag)
    for d in range(1, n_tp):
        st_copy(d).wait_send()
        cm_copy(d).wait_send()

    @pl.loop(1, n_req)
    def _(d):
        t1_copy(d).wait_send()
        d_copy(d).wait_send()
        t2_copy(d).wait_send()
        r_copy(d).wait_send()
        mv_copy(d).wait_send()


def moe_call(n_req, n_tp, meta, head, gain, router_t, ids_t, slots, send_tail, hidden, w_out, wg_t, wu_t, wd):
    rows, width = hidden.shape
    cap = 5 * rows * TOP // (4 * n_req)
    nsl = n_req * cap
    crows = nsl // NCH
    nslp = n_req * slot_stride(cap)
    chunk = send_tail.shape[1]
    smem = pl.BlockSpec(memory_space=pltpu.SMEM)
    vmem = pl.BlockSpec(memory_space=pltpu.VMEM)
    anym = pl.BlockSpec(memory_space=pl.ANY)
    dma = pltpu.SemaphoreType.DMA
    n_x = n_tp // 2

    def bf(*shape):
        return pltpu.VMEM(shape, BF16)

    return pl.pallas_call(
        moe_kernel,
        out_shape=(
            jax.ShapeDtypeStruct((n_tp, rows, 128), BF16),
            jax.ShapeDtypeStruct((n_tp, 16, 128), BF16),
            jax.ShapeDtypeStruct((n_req, chunk, 128), BF16),
        ),
        in_specs=[smem] + [vmem] * 6 + [anym] * 5,
        out_specs=(vmem, vmem, vmem),
        scratch_shapes=[
            bf(rows, 128), bf(*w_out.shape), bf(*wg_t.shape), bf(*wu_t.shape), bf(*wd.shape),
            bf(n_req, chunk, 128), bf(n_req, chunk, 128),
            bf(2, n_x, rows, 128), bf(n_x, rows, 128), bf(n_x, rows, 128), bf(n_x, rows, 128),
            pltpu.VMEM((8, rows), F32), pltpu.VMEM((n_tp, 8, rows), F32),
            bf(nslp, 128), bf(nslp, 128), bf(NCH, n_tp, crows, 128),
            bf(NCH, 2, n_x, crows, 128), bf(NCH, n_x, crows, 128), bf(NCH, n_x, crows, 128), bf(NCH, n_x, crows, 128),
            bf(nslp, 128), bf(nslp, 128),
            bf(16, 128), bf(n_req, 16, 128),
        ]
        + [dma((5,))]
        + [dma((n_req,))] * 4
        + [dma((n_x,))] * 4
        + [dma((n_tp,))] * 2
        + [dma((n_req,))] * 2
        + [dma((NCH, n_x))] * 8
        + [dma((n_req,))] * 4
        + [dma((n_x,))] * 4
        + [dma((n_tp,))] * 2,
        compiler_params=pltpu.CompilerParams(collective_id=0, has_side_effects=True, vmem_limit_bytes=56 << 20),
        name="moe_exchange",
    )(meta, head, gain.reshape(1, -1), router_t, ids_t, slots, send_tail, hidden, w_out, wg_t, wu_t, wd)


def place_kernel(meta_s, mix_ref, came_ref, got_ref, tail_in, out_ref, tail_out, sems):
    rows = tail_out.shape[1]

    def put(k, kv):
        return pltpu.make_async_copy(got_ref.at[k, kv], tail_out.at[kv, meta_s[0, MIG + k]], sems.at[k, kv])

    for k in range(MIG):
        for kv in range(2):

            @pl.when(meta_s[0, MIG + k] < rows)
            def _():
                put(k, kv).start()

    for tt in range(mix_ref.shape[0]):
        out_ref[:, tt * 128 : (tt + 1) * 128] = mix_ref[tt]
    sub = lax.broadcasted_iota(jnp.int32, (16, 128), 0)
    for k in range(MIG):
        slot = meta_s[0, MIG + k]

        @pl.when(slot < rows)
        def _():
            base = pl.multiple_of((slot >> 4) << 4, 16)
            for tt in range(mix_ref.shape[0]):
                cols = slice(tt * 128, (tt + 1) * 128)
                row = came_ref[tt].astype(F32)[k : k + 1, :]
                w = out_ref[pl.ds(base, 16), cols].astype(F32)
                out_ref[pl.ds(base, 16), cols] = jnp.where(sub == slot - base, row, w).astype(BF16)

    for k in range(MIG):
        for kv in range(2):

            @pl.when(meta_s[0, MIG + k] < rows)
            def _():
                put(k, kv).wait()


def place_call(meta, mix, came, got, tail):
    n_tp, rows, wd = mix.shape
    vmem = pl.BlockSpec(memory_space=pltpu.VMEM)
    return pl.pallas_call(
        place_kernel,
        out_shape=(
            jax.ShapeDtypeStruct((rows, n_tp * wd), BF16),
            jax.ShapeDtypeStruct(tail.shape, tail.dtype),
        ),
        in_specs=[pl.BlockSpec(memory_space=pltpu.SMEM), vmem, vmem, vmem, pl.BlockSpec(memory_space=pl.ANY)],
        out_specs=(vmem, pl.BlockSpec(memory_space=pl.ANY)),
        scratch_shapes=[pltpu.SemaphoreType.DMA((MIG, 2))],
        input_output_aliases={4: 1},
        name="place_rows",
    )(meta, mix, came, got, tail)


def body(
    hidden_in, prompt_kv, tail_kv, group_of, prompt_len, tail_len, bucket_of, bias_table, attn_gain, w_query, w_key,
    w_value, w_out, ffn_gain, router_weight, expert_ids, w_gate, w_up, w_down, new_slot,
):
    n_req = lax.axis_size("req")
    n_tp = lax.axis_size("tp")
    ids_t = expert_ids.T
    tail_new, head, send_tail, slots, meta = attention_call(
        hidden_in, attn_gain, w_query, w_key, w_value, group_of, prompt_len, tail_len, bucket_of, bias_table.T,
        new_slot, ids_t, prompt_kv, tail_kv,
    )
    pieces = send_tail.reshape(n_req, -1, send_tail.shape[-1])
    mix, came, got = moe_call(
        n_req, n_tp, meta, head, ffn_gain, router_weight.T, ids_t, slots, pieces, hidden_in, w_out,
        w_gate[0].T, w_up[0].T, w_down[0],
    )
    return place_call(meta, mix, came, got.reshape(send_tail.shape), tail_new)


def solution(mesh):
    return jax.shard_map(
        body,
        mesh=mesh,
        in_specs=(
            P("req", None), P(None, "req", None, "tp"), P(None, "req", None, "tp"), P("req"), P("req"), P("req"), P(),
            P(None, "tp"), P(), P(None, "tp"), P(None, "tp"), P(None, "tp"), P("tp", None), P(), P(), P("req", None),
            P("req", None, "tp"), P("req", None, "tp"), P("req", "tp", None), P(),
        ),
        out_specs=(P("req", None), P(None, "req", None, "tp")),
        check_vma=False,
    )
```

```python
import functools

import jax
import jax.numpy as jnp
from jax import lax
from jax.experimental import pallas as pl
from jax.experimental.pallas import tpu as pltpu
from jax.sharding import PartitionSpec as P

F32 = jnp.float32
BF16 = jnp.bfloat16
EPS = 1e-06
NEG = -1e30
RB = 32
UB = 4
TB = 8
TOP = 2
MIG = 4


def slot_stride(cap):
    return -(-cap // 16) * 16


def col_form(row):
    n = row.shape[1]
    return jnp.transpose(jnp.broadcast_to(row.astype(F32), (128, n)))


def migration_tables(ns_ref, meta_ref, rows):
    me = lax.axis_index("req")
    per = rows // 128
    tiles = ns_ref[...].astype(F32)
    shape = tiles.shape
    lane = lax.broadcasted_iota(jnp.int32, shape, 1).astype(F32)
    sub = lax.broadcasted_iota(jnp.int32, shape, 0)
    moved = tiles != sub.astype(F32) * 128.0 + lane
    where_to = jnp.floor(tiles * (1.0 / rows))
    goes = jnp.max(jnp.where(moved, where_to, -1.0), axis=1, keepdims=True)
    src = jnp.max(jnp.where(goes == lane, (sub // per).astype(F32), -1.0), axis=0, keepdims=True)
    src = jnp.where(src < 0.0, lane[0:1], src)

    mine = ns_ref[pl.ds(me * per, per), :].astype(F32)
    row = jnp.concatenate([mine[i : i + 1] for i in range(per)], axis=1)
    col = col_form(row)
    base = (me * rows).astype(F32)
    rid = lax.broadcasted_iota(jnp.int32, (rows, 128), 0).astype(F32)
    rlane = lax.broadcasted_iota(jnp.int32, (rows, 128), 1).astype(F32)
    moved_col = col != rid + base
    order = jnp.zeros((rows, 128), F32)
    place = jnp.zeros((rows, 128), F32)
    for i in range(per):
        part = row[:, i * 128 : (i + 1) * 128]
        other = rlane + float(i * 128)
        moved_row = part != other[0:1] + base
        order = order + jnp.where(moved_row & (part < col), 1.0, 0.0)
        place = place + jnp.where(moved_row & (other < rid), 1.0, 0.0)
    order = jnp.sum(order, axis=1, keepdims=True)
    place = jnp.sum(place, axis=1, keepdims=True)
    out = float(rows)
    send = jnp.min(jnp.where(moved_col & (order == rlane), rid, out), axis=0, keepdims=True)
    send = jnp.minimum(send, out - 1.0)
    vac = jnp.min(jnp.where(moved_col & (place + float(MIG) == rlane), rid, out), axis=0, keepdims=True)
    idx = jnp.where(rlane[0:1] < float(MIG), send, vac)
    s8 = lax.broadcasted_iota(jnp.int32, (8, 128), 0)
    meta_ref[...] = jnp.where(s8 == 0, idx, jnp.where(s8 == 1, src, 0.0)).astype(jnp.int32)


def attn_kernel(
    tl_s, tab_s, plen_s, bkt_s,
    gain_ref, grp_ref, tlr_ref, ids_ref, ns_ref, hid_any, wq_any, wk_any, wv_any, pkv_any, tail_any,
    tail_out, send_ref, slot_ref, meta_ref, q16, tbias, mpart, lpart, opart,
    hid_v, wcat, pkv_v, buf, kvn, lhs, kcat, sco, prob, posb, plb, tlb, dtab,
    first_s, meta_s, s_in, s_tin, s_tout, s_meta,
):
    rows = hid_v.shape[0]
    nb = rows // 8
    groups = pkv_v.shape[1]
    pre = pkv_v.shape[2]
    nbuck = tab_s.shape[1]
    mig = send_ref.shape[0]
    span = bkt_s.shape[0]
    nblk = rows // RB
    loads = [
        pltpu.make_async_copy(hid_any, hid_v, s_in.at[0]),
        pltpu.make_async_copy(wq_any, wcat.at[:, 0:128], s_in.at[1]),
        pltpu.make_async_copy(wk_any, wcat.at[:, 128:256], s_in.at[2]),
        pltpu.make_async_copy(wv_any, wcat.at[:, 256:384], s_in.at[3]),
        pltpu.make_async_copy(pkv_any.at[0], pkv_v.at[0], s_in.at[4]),
        pltpu.make_async_copy(pkv_any.at[1], pkv_v.at[1], s_in.at[5]),
    ]
    for cp in loads:
        cp.start()

    def t_in(s, kv):
        sl = pl.ds(s * RB, RB)
        return pltpu.make_async_copy(tail_any.at[kv, sl], buf.at[kv, sl], s_tin.at[s, kv])

    def t_out(s, kv):
        sl = pl.ds(s * RB, RB)
        return pltpu.make_async_copy(buf.at[kv, sl], tail_out.at[kv, sl], s_tout.at[s, kv])

    @pl.loop(0, nblk)
    def _(s):
        t_in(s, 0).start()
        t_in(s, 1).start()

    for k in range(nbuck):
        first_s[k] = span

    @pl.loop(0, span, unroll=8)
    def _(i):
        d = span - 1 - i
        first_s[bkt_s[d]] = d

    nd = dtab.shape[2] // 128
    dist = [lax.broadcasted_iota(jnp.int32, (8, 128), 1) + c * 128 for c in range(nd)]
    d0 = [jnp.full((8, 128), tab_s[0, 0], F32) for _ in range(nd)]
    d1 = [jnp.full((8, 128), tab_s[1, 0], F32) for _ in range(nd)]
    for k in range(1, nbuck):
        for c in range(nd):
            ge = dist[c] >= first_s[k]
            d0[c] = jnp.where(ge, tab_s[0, k], d0[c])
            d1[c] = jnp.where(ge, tab_s[1, k], d1[c])
    for c in range(nd):
        dtab[0, :, c * 128 : (c + 1) * 128] = d0[c]
        dtab[1, :, c * 128 : (c + 1) * 128] = d1[c]

    migration_tables(ns_ref, meta_ref, rows)
    meta_copy = pltpu.make_async_copy(meta_ref, meta_s, s_meta)
    meta_copy.start()

    g = col_form(grp_ref[...])
    tl = col_form(tlr_ref[...])
    pln = jnp.zeros_like(g)
    for i in range(groups):
        pln = jnp.where(g == float(i), plen_s[i].astype(F32), pln)
    posb[...] = (pln + tl).astype(jnp.int32)
    plb[...] = pln.astype(jnp.int32)
    tlb[...] = tl.astype(jnp.int32)
    g2 = jnp.broadcast_to(g.reshape(nb, 1, 8, 128), (nb, 2, 8, 128)).reshape(2 * rows, 128)

    e0 = col_form(ids_ref[0:1, :])
    e1 = col_form(ids_ref[1:2, :])
    ln = lax.broadcasted_iota(jnp.int32, (rows, 128), 1).astype(F32)
    hit0 = ln == e0
    hit1 = ln == e1
    ri = lax.broadcasted_iota(jnp.int32, (rows, rows), 0)
    ci = lax.broadcasted_iota(jnp.int32, (rows, rows), 1)
    lower = (ci < ri).astype(F32).astype(BF16)
    o0 = hit0.astype(F32)
    o1 = hit1.astype(F32)
    cum0 = jnp.dot(lower, o0.astype(BF16), preferred_element_type=F32)
    cum1 = jnp.dot(lower, o1.astype(BF16), preferred_element_type=F32)
    tot0 = jnp.sum(o0, axis=0, keepdims=True)
    p0 = jnp.sum(jnp.where(hit0, cum0, 0.0), axis=1, keepdims=True)
    p1 = jnp.sum(jnp.where(hit1, cum1 + tot0, 0.0), axis=1, keepdims=True)
    stride = float(slot_stride(5 * rows * TOP // (4 * 16)))
    slot_ref[0] = e0 * stride + p0
    slot_ref[1] = e1 * stride + p1

    for cp in loads[:4]:
        cp.wait()
    h = hid_v[...].astype(F32)
    ms = jnp.mean(h * h, axis=-1, keepdims=True)
    n1 = (h * lax.rsqrt(ms + EPS) * gain_ref[...]).astype(BF16)
    qkv = jnp.dot(n1, wcat[...], preferred_element_type=F32).astype(BF16).astype(F32)
    q = qkv[:, 0:128]
    kvn[0] = qkv[:, 128:256]
    kvn[1] = qkv[:, 256:384]
    sub16 = lax.broadcasted_iota(jnp.int32, (16, 128), 0)

    @pl.loop(0, nblk)
    def _(s):
        t_in(s, 0).wait()
        t_in(s, 1).wait()
        for i in range(RB):
            r = s * RB + i
            length = tl_s[r]
            base = pl.multiple_of((length >> 4) << 4, 16)
            for kv in range(2):
                w = buf[kv, r, pl.ds(base, 16), :].astype(F32)
                row = kvn[kv, pl.ds(r, 1), :]
                buf[kv, r, pl.ds(base, 16), :] = jnp.where(sub16 == length - base, row, w).astype(BF16)
        t_out(s, 0).start()
        t_out(s, 1).start()

    lane = lax.broadcasted_iota(jnp.int32, (nb, 2, 8, 128), 3)
    head = lax.broadcasted_iota(jnp.int32, (nb, 2, 8, 128), 1)
    qh = jnp.broadcast_to((q * 0.125).reshape(nb, 1, 8, 128), (nb, 2, 8, 128))
    qh = jnp.where((lane // 64) == head, qh, 0.0).reshape(2 * rows, 128)
    q16[...] = qh.astype(BF16)
    loads[4].wait()
    for i in range(groups):
        lhs[:, i * 128 : (i + 1) * 128] = jnp.where(g2 == float(i), qh, 0.0).astype(BF16)
        kcat[:, i * 128 : (i + 1) * 128] = pkv_v[0, i]
    sco[...] = lax.dot_general(lhs[...], kcat[...], (((1,), (1,)), ((), ())), preferred_element_type=F32)

    def take(tab, i):
        return jnp.take_along_axis(tab, i, axis=1, mode="promise_in_bounds")

    nch = pre // 128

    ln = lax.broadcasted_iota(jnp.int32, (8, 128), 1)
    sub = lax.broadcasted_iota(jnp.int32, (8, 128), 0)
    mine = (ln >> 6) == (sub & 1)

    @pl.loop(0, nb // UB)
    def _(i):
        at = [i * UB + n for n in range(UB)]
        pos = [posb[pl.ds(b * 8, 8), :] for b in at]
        pb = [plb[pl.ds(b * 8, 8), :] for b in at]
        tb = [tlb[pl.ds(b * 8, 8), :] for b in at]
        raw = [
            [[sco[pl.ds(b * 16 + hh * 8, 8), c * 128 : (c + 1) * 128] for c in range(nch)] for hh in range(2)]
            for b in at
        ]
        tabs = [[dtab[hh, :, k * 128 : (k + 1) * 128] for k in range(nd)] for hh in range(2)]
        out = []
        for n in range(UB):
            low = pos[n] & 127
            gi = (low - ln) & 127
            blk = (pos[n] >> 7) - (ln > low).astype(jnp.int32)
            is_blk = [blk == k for k in range(nd)]
            td = tb[n] - (ln & 63)
            valid = (td >= 0) & mine
            td = jnp.maximum(td, 0)
            for hh in range(2):
                tail = jnp.where(valid, take(tabs[hh][0], td), NEG)
                gs = [take(tabs[hh][k], gi) for k in range(nd)]
                s = []
                for c in range(nch):
                    bias = gs[0]
                    for k in range(1, nd - c):
                        bias = jnp.where(is_blk[k + c], gs[k], bias)
                    s.append(jnp.where(ln + c * 128 < pb[n], raw[n][hh][c] + bias, NEG))
                mx = jnp.max(functools.reduce(jnp.maximum, s), axis=1, keepdims=True)
                e = [jnp.exp(v - mx) for v in s]
                tot = jnp.sum(functools.reduce(jnp.add, e), axis=1, keepdims=True)
                out.append((tail, mx, e, tot))
        for n in range(UB):
            for hh in range(2):
                tail, mx, e, tot = out[n * 2 + hh]
                rs = pl.ds(at[n] * 16 + hh * 8, 8)
                tbias[rs, :] = tail
                mpart[rs, :] = jnp.broadcast_to(mx, (8, 128))
                lpart[rs, :] = jnp.broadcast_to(tot, (8, 128))
            for c in range(nch):
                prob[pl.ds(at[n] * 16, 16), c * 128 : (c + 1) * 128] = jnp.concatenate(
                    [out[n * 2][2][c], out[n * 2 + 1][2][c]], axis=0
                ).astype(BF16)

    loads[5].wait()
    acc = jnp.zeros((2 * rows, 128), F32)
    for i in range(0, groups, 2):
        rhs = jnp.concatenate([pkv_v[1, i], pkv_v[1, i + 1]], axis=1)
        o = jnp.dot(prob[...], rhs, preferred_element_type=F32)
        acc = jnp.where(g2 == float(i), o[:, 0:128], acc)
        acc = jnp.where(g2 == float(i + 1), o[:, 128:256], acc)
    opart[...] = acc

    meta_copy.wait()
    for m in range(mig):
        for kv in range(2):
            send_ref[m, kv] = buf[kv, meta_s[0, m]]

    @pl.loop(0, nblk)
    def _(s):
        t_out(s, 0).wait()
        t_out(s, 1).wait()


def attention_call(
    hidden_in, gain, wq, wk, wv, group_of, prompt_len, tail_len, bucket_of, table_t, new_slot, ids_t, prompt_kv, tail_kv
):
    rows, width = hidden_in.shape
    smem = pl.BlockSpec(memory_space=pltpu.SMEM)
    vmem = pl.BlockSpec(memory_space=pltpu.VMEM)
    anym = pl.BlockSpec(memory_space=pl.ANY)
    _, groups, pre, wd = prompt_kv.shape
    tail_rows = tail_kv.shape[2]
    nd = -(-bucket_of.shape[0] // 128)
    nblk = rows // RB
    dma = pltpu.SemaphoreType.DMA
    return pl.pallas_call(
        attn_kernel,
        out_shape=(
            jax.ShapeDtypeStruct(tail_kv.shape, BF16),
            jax.ShapeDtypeStruct((MIG, 2, tail_rows, wd), BF16),
            jax.ShapeDtypeStruct((2, rows, 128), F32),
            jax.ShapeDtypeStruct((8, 128), jnp.int32),
            jax.ShapeDtypeStruct((2 * rows, wd), BF16),
        )
        + (jax.ShapeDtypeStruct((2 * rows, 128), F32),) * 4,
        in_specs=[smem] * 4 + [vmem] * 5 + [anym] * 6,
        out_specs=(anym,) + (vmem,) * 8,
        scratch_shapes=[
            pltpu.VMEM((rows, width), BF16),
            pltpu.VMEM((width, 3 * wd), BF16),
            pltpu.VMEM(prompt_kv.shape, BF16),
            pltpu.VMEM(tail_kv.shape, BF16),
            pltpu.VMEM((2, rows, wd), F32),
            pltpu.VMEM((2 * rows, groups * wd), BF16),
            pltpu.VMEM((pre, groups * wd), BF16),
            pltpu.VMEM((2 * rows, pre), F32),
            pltpu.VMEM((2 * rows, pre), BF16),
            pltpu.VMEM((rows, 128), jnp.int32),
            pltpu.VMEM((rows, 128), jnp.int32),
            pltpu.VMEM((rows, 128), jnp.int32),
            pltpu.VMEM((2, 8, nd * 128), F32),
            pltpu.SMEM((table_t.shape[1],), jnp.int32),
            pltpu.SMEM((8, 128), jnp.int32),
            dma((6,)),
            dma((nblk, 2)),
            dma((nblk, 2)),
            dma,
        ],
        compiler_params=pltpu.CompilerParams(vmem_limit_bytes=60 << 20),
        name="attention_tails",
    )(
        tail_len, table_t, prompt_len, bucket_of,
        gain.reshape(1, -1), group_of.reshape(1, -1), tail_len.reshape(1, -1), ids_t, new_slot.reshape(-1, 128),
        hidden_in, wq, wk, wv, prompt_kv, tail_kv,
    )


MESH = pl.DeviceIdType.MESH
NCH = 2


def moe_kernel(
    meta_s,
    q16, tbias, mpart, lpart, opart, gain_ref, router_ref, ids_ref, slot_ref, tail_ref, kv_any, hid_any, wout_any, wg_any, wu_any, wd_any,
    mix, came, got,
    buf, head_v, hid_v, wout_v, wg_v, wu_v, wd_v,
    t1, t2, part, psib, psend, precv, stat, statr, dsend, drecv, xall, ypart, ysib, ysend, yrecv, rsend, rrecv, mvs, mvr,
    s_in, s_kv, s_t1, r_t1, s_t2, r_t2, s_ps, r_ps, s_px, r_px, s_st, r_st, s_d, r_d, s_gx, r_gx, s_gs, r_gs,
    s_ys, r_ys, s_yx, r_yx, s_r, r_r, s_mv, r_mv, s_ox, r_ox, s_os, r_os, s_cm, r_cm,
):
    r = lax.axis_index("req")
    t = lax.axis_index("tp")
    n_req = t1.shape[0]
    n_tp = mix.shape[0]
    n_x = n_tp // 2
    rows = hid_v.shape[0]
    width = wout_v.shape[1]
    crows = xall.shape[2]
    per = n_req // NCH
    cap = crows // per
    nslp = dsend.shape[0]
    capp = nslp // n_req
    c = lax.rem(t, 2)
    x = t // 2
    sib = x * 2 + 1 - c
    lanes = pl.ds(pl.multiple_of(t * 128, 128), 128)

    loads = [
        pltpu.make_async_copy(wout_any, wout_v, s_in.at[0]),
        pltpu.make_async_copy(hid_any.at[:, lanes], hid_v, s_in.at[1]),
        pltpu.make_async_copy(wg_any, wg_v, s_in.at[2]),
        pltpu.make_async_copy(wu_any, wu_v, s_in.at[3]),
        pltpu.make_async_copy(wd_any, wd_v, s_in.at[4]),
    ]
    nkv = rows // (TB * 8)

    def kv_load(i):
        sl = pl.ds(i * TB * 8, TB * 8)
        return pltpu.make_async_copy(kv_any.at[:, sl], buf.at[:, sl], s_kv.at[i])

    @pl.loop(0, nkv)
    def _(i):
        kv_load(i).start()

    for cp in loads:
        cp.start()

    def tp_copy(src, dst, ss, rs, peer):
        return pltpu.make_async_remote_copy(
            src_ref=src, dst_ref=dst, send_sem=ss, recv_sem=rs, device_id=(r, peer), device_id_type=MESH
        )

    def req_copy(src, dst, ss, rs, peer):
        return pltpu.make_async_remote_copy(
            src_ref=src, dst_ref=dst, send_sem=ss, recv_sem=rs, device_id=(peer, t), device_id_type=MESH
        )

    def xpeer(d):
        return lax.rem(x + d, n_x) * 2 + c

    def xfrom(d):
        return lax.rem(x + n_x - d, n_x) * 2 + c

    barrier = pltpu.get_barrier_semaphore()

    @pl.loop(1, n_tp)
    def _(d):
        pl.semaphore_signal(barrier, inc=1, device_id=(r, lax.rem(t + d, n_tp)), device_id_type=MESH)

    @pl.loop(1, n_req)
    def _(d):
        pl.semaphore_signal(barrier, inc=1, device_id=(lax.rem(r + d, n_req), t), device_id_type=MESH)

    sub16 = lax.broadcasted_iota(jnp.int32, (16, 128), 0)
    pair = lax.rem(sub16, 8) // 2
    lane4 = lax.broadcasted_iota(jnp.int32, (TB, 8, 128), 2)

    @pl.loop(0, nkv)
    def _(i):
        kv_load(i).wait()
        rs = pl.ds(pl.multiple_of(i * TB * 16, TB * 16), TB * 16)
        scs = []
        for n in range(TB):
            b = i * TB + n
            kb = buf[0, pl.ds(b * 8, 8)].reshape(512, 128)
            qb = q16[pl.ds(pl.multiple_of(b * 16, 16), 16), :]
            s4 = lax.dot_general(qb, kb, (((1,), (1,)), ((), ())), preferred_element_type=F32)
            sc = s4[:, 0:128]
            for j in range(1, 4):
                sc = jnp.where(pair == j, s4[:, j * 128 : (j + 1) * 128], sc)
            scs.append(sc)
        sc = jnp.concatenate(scs, axis=0) + tbias[rs, :]
        mp = mpart[rs, :]
        mx = jnp.maximum(jnp.max(sc, axis=1, keepdims=True), mp)
        e = jnp.exp(sc - mx)
        ap = jnp.exp(mp - mx)
        tot = jnp.sum(e, axis=1, keepdims=True) + lpart[rs, :] * ap
        os = []
        for n in range(TB):
            b = i * TB + n
            vb = buf[1, pl.ds(b * 8, 8)].reshape(512, 128)
            en = e[n * 16 : (n + 1) * 16]
            p4 = jnp.concatenate([jnp.where(pair == j, en, 0.0) for j in range(4)], axis=1).astype(BF16)
            os.append(jnp.dot(p4, vb, preferred_element_type=F32))
        o = (jnp.concatenate(os, axis=0) + opart[rs, :] * ap) / tot
        o = o.reshape(TB, 2, 8, 128)
        o = jnp.where(lane4 < 64, o[:, 0], o[:, 1]).reshape(TB * 8, 128)
        head_v[pl.ds(pl.multiple_of(i * TB * 8, TB * 8), TB * 8), :] = o.astype(BF16)

    head = head_v[...]
    loads[0].wait()
    for tt in range(n_tp):
        part[tt % 2, tt // 2] = jnp.dot(
            head, wout_v[:, tt * 128 : (tt + 1) * 128], preferred_element_type=F32
        ).astype(BF16)

    pl.semaphore_wait(barrier, n_tp - 1 + n_req - 1)

    def rs_sib(d, buf, dst, ss, rs):
        xx = lax.rem(x + d, n_x)
        return tp_copy(buf.at[1 - c, xx], dst.at[xx], ss.at[d], rs.at[d], sib)

    def rs_x(d, buf, dst, ss, rs):
        return tp_copy(buf.at[d], dst.at[d], ss.at[d], rs.at[d], xpeer(d))

    def rs_start(buf, bsib, ss1, rs1):
        for d in (2, 1, 3, 0):
            rs_sib(d, buf, bsib, ss1, rs1).start()

    def rs_send(buf, bsib, bsend, brecv, ss1, rs1, ss2, rs2):
        for d in (2, 1, 3):
            xx = lax.rem(x + d, n_x)
            rs_sib(d, buf, bsib, ss1, rs1).wait_recv()
            bsend[d] = (buf[c, xx].astype(F32) + bsib[xx].astype(F32)).astype(BF16)
            rs_x(d, bsend, brecv, ss2, rs2).start()

    def rs_total(buf, bsib, bsend, brecv, ss1, rs1, ss2, rs2):
        rs_sib(0, buf, bsib, ss1, rs1).wait_recv()
        tot = buf[c, x].astype(F32) + bsib[x].astype(F32)
        for d in (1, 3, 2):
            rs_x(d, bsend, brecv, ss2, rs2).wait_recv()
            tot = tot + brecv[d].astype(F32)
        return tot

    def rs_finish(buf, bsib, bsend, brecv, ss1, rs1, ss2, rs2):
        for d in (0, 1, 2, 3):
            rs_sib(d, buf, bsib, ss1, rs1).wait_send()
        for d in (1, 2, 3):
            rs_x(d, bsend, brecv, ss2, rs2).wait_send()

    def ag_x(d, buf, ss, rs):
        return tp_copy(buf.at[t], buf.at[t], ss.at[d], rs.at[d], xpeer(d))

    def ag_s(d, buf, ss, rs):
        who = xfrom(d)
        return tp_copy(buf.at[who], buf.at[who], ss.at[d], rs.at[d], sib)

    def ag_start(buf, ss1, rs1, ss2, rs2):
        for d in (2, 1, 3):
            ag_x(d, buf, ss1, rs1).start()
        ag_s(0, buf, ss2, rs2).start()

    def ag_pass(buf, ss1, rs1, ss2, rs2):
        for d in (1, 3, 2):
            who = xfrom(d)
            tp_copy(buf.at[who], buf.at[who], ss1.at[d], rs1.at[d], xpeer(d)).wait_recv()
            ag_s(d, buf, ss2, rs2).start()

    def ag_wait(buf, ss1, rs1, ss2, rs2):
        for d in (0, 1, 3, 2):
            mine = xfrom(d)
            other = lax.rem(x + n_x - d, n_x) * 2 + 1 - c
            tp_copy(buf.at[mine], buf.at[other], ss2.at[d], rs2.at[d], sib).wait_recv()

    def ag_finish(buf, ss1, rs1, ss2, rs2):
        for d in (1, 2, 3):
            ag_x(d, buf, ss1, rs1).wait_send()
        for d in (0, 1, 2, 3):
            ag_s(d, buf, ss2, rs2).wait_send()

    attn_rs = (part, psib, psend, precv, s_ps, r_ps, s_px, r_px)
    rs_start(part, psib, s_ps, r_ps)
    rs_send(*attn_rs)

    def t1_copy(d):
        j = lax.rem(r + d, n_req)
        return req_copy(tail_ref.at[j], t1.at[r], s_t1.at[d], r_t1.at[d], j)

    loads[1].wait()
    resid = (hid_v[...].astype(F32) + rs_total(*attn_rs)).astype(BF16)

    s0 = slot_ref[0]
    s1 = slot_ref[1]
    lnf = lax.broadcasted_iota(jnp.int32, (rows, 128), 1).astype(F32)
    for k in range(nslp // 128):
        pick = (s0 == lnf + float(k * 128)) | (s1 == lnf + float(k * 128))
        dsend[k * 128 : (k + 1) * 128, :] = lax.dot_general(
            pick.astype(F32).astype(BF16), resid, (((0,), (0,)), ((), ())), preferred_element_type=F32
        ).astype(BF16)

    def block(j):
        return pl.ds(pl.multiple_of(j * capp, 16), capp)

    def d_copy(d):
        j = lax.rem(r + d, n_req)
        return req_copy(dsend.at[block(j)], drecv.at[block(r)], s_d.at[d], r_d.at[d], j)

    @pl.loop(1, n_req)
    def _(d):
        d_copy(d).start()

    drecv[block(r), :] = dsend[block(r), :]

    @pl.loop(1, n_req)
    def _(d):
        t1_copy(d).start()

    t1[r] = tail_ref[r]

    rf = resid.astype(F32)
    u = rf * gain_ref[:, lanes]
    lg = lax.dot_general(
        u.astype(BF16), router_ref[:, lanes], (((1,), (1,)), ((), ())), preferred_element_type=F32
    )
    e0 = col_form(ids_ref[0:1, :])
    e1 = col_form(ids_ref[1:2, :])
    n_e = lg.shape[1]
    ex = lnf[:, 0:n_e]
    diff = jnp.sum(
        jnp.where(ex == e0[:, 0:n_e], lg, 0.0) - jnp.where(ex == e1[:, 0:n_e], lg, 0.0), axis=1, keepdims=True
    )
    sq = jnp.sum(rf * rf, axis=1, keepdims=True)
    stat[...] = jnp.transpose(jnp.where(lnf == 0.0, sq, jnp.where(lnf == 1.0, diff, 0.0)))[0:8]

    def st_copy(d):
        return tp_copy(stat, statr.at[d], s_st.at[d], r_st.at[d], lax.rem(t + d, n_tp))

    for d in range(1, n_tp):
        st_copy(d).start()

    @pl.loop(1, n_req)
    def _(d):
        d_copy(d).wait_recv()

    def x_ag(h):
        return (xall.at[h], s_gx.at[h], r_gx.at[h], s_gs.at[h], r_gs.at[h])

    for h in range(NCH):
        xall[h, t] = jnp.concatenate(
            [drecv[j * capp : (j + 1) * capp, :].astype(F32)[0:cap] for j in range(h * per, (h + 1) * per)], axis=0
        ).astype(BF16)
        ag_start(*x_ag(h))

    @pl.loop(1, n_req)
    def _(d):
        t1_copy(d).wait_recv()

    @pl.loop(0, n_req)
    def _(j):
        t2[j] = t1[meta_s[1, j]]

    def t2_copy(d):
        j = lax.rem(r + d, n_req)
        return req_copy(t2.at[j], got.at[r], s_t2.at[d], r_t2.at[d], j)

    @pl.loop(1, n_req)
    def _(d):
        t2_copy(d).start()

    got[r] = t2[r]

    tot = stat[...]
    for d in range(1, n_tp):
        st_copy(d).wait_recv()
        tot = tot + statr[d]
    tot = jnp.transpose(jnp.concatenate([tot, jnp.zeros((120, rows), F32)], axis=0))
    gate = jax.nn.sigmoid(tot[:, 1:2] * lax.rsqrt(tot[:, 0:1] * (1.0 / width) + EPS))

    for cp in loads[2:]:
        cp.wait()

    def ffn(h):
        xm = jnp.concatenate([xall[h, tt] for tt in range(n_tp)], axis=1).astype(F32)
        ms = jnp.mean(xm * xm, axis=-1, keepdims=True)
        nm = (xm * lax.rsqrt(ms + EPS) * gain_ref[...]).astype(BF16)
        gh = lax.dot_general(nm, wg_v[...], (((1,), (1,)), ((), ())), preferred_element_type=F32)
        uh = lax.dot_general(nm, wu_v[...], (((1,), (1,)), ((), ())), preferred_element_type=F32)
        act = (jax.nn.gelu(gh, approximate=True) * uh).astype(BF16)
        y = jnp.dot(act, wd_v[...], preferred_element_type=F32).astype(BF16)
        for tt in range(n_tp):
            ypart[h, tt % 2, tt // 2] = y[:, tt * 128 : (tt + 1) * 128]

    def y_rs(h):
        return (
            ypart.at[h], ysib.at[h], ysend.at[h], yrecv.at[h], s_ys.at[h], r_ys.at[h], s_yx.at[h], r_yx.at[h]
        )

    ag_pass(*x_ag(0))
    for h in range(NCH):
        ag_wait(*x_ag(h))
        ffn(h)
        rs_start(ypart.at[h], ysib.at[h], s_ys.at[h], r_ys.at[h])
        if h + 1 < NCH:
            ag_pass(*x_ag(h + 1))
        rs_send(*y_rs(h))

    def r_copy(d):
        j = lax.rem(r + d, n_req)
        return req_copy(rsend.at[block(j)], rrecv.at[block(r)], s_r.at[d], r_r.at[d], j)

    pad = jnp.zeros((capp - cap, 128), F32)
    for h in range(NCH):
        tot = rs_total(*y_rs(h))
        for i in range(per):
            j = h * per + i
            rsend[j * capp : (j + 1) * capp, :] = jnp.concatenate(
                [tot[i * cap : (i + 1) * cap], pad], axis=0
            ).astype(BF16)

        @pl.loop(h * per, (h + 1) * per)
        def _(j):
            @pl.when(j != r)
            def _():
                r_copy(lax.rem(j + n_req - r, n_req)).start()

    rrecv[block(r), :] = rsend[block(r), :]

    @pl.loop(1, n_req)
    def _(d):
        r_copy(d).wait_recv()

    p0 = jnp.zeros((rows, 128), F32)
    p1 = jnp.zeros((rows, 128), F32)
    for k in range(nslp // 128):
        res = rrecv[k * 128 : (k + 1) * 128, :]
        p0 = p0 + jnp.dot((s0 == lnf + float(k * 128)).astype(F32).astype(BF16), res, preferred_element_type=F32)
        p1 = p1 + jnp.dot((s1 == lnf + float(k * 128)).astype(F32).astype(BF16), res, preferred_element_type=F32)
    mixed = (rf + gate * p0 + (1.0 - gate) * p1).astype(BF16)

    kk = lax.broadcasted_iota(jnp.int32, (16, rows), 0)
    rr = lax.broadcasted_iota(jnp.int32, (16, rows), 1)
    pick = jnp.zeros((16, rows), F32)
    for k in range(MIG):
        pick = jnp.where((kk == k) & (rr == meta_s[0, k]), 1.0, pick)
    mvs[...] = jnp.dot(pick.astype(BF16), mixed, preferred_element_type=F32).astype(BF16)

    def mv_copy(d):
        j = lax.rem(r + d, n_req)
        return req_copy(mvs, mvr.at[r], s_mv.at[d], r_mv.at[d], j)

    mix[t] = mixed
    o_ag = (mix, s_ox, r_ox, s_os, r_os)
    ag_start(*o_ag)

    @pl.loop(1, n_req)
    def _(d):
        mv_copy(d).start()

    mvr[r] = mvs[...]

    def cm_copy(d):
        return tp_copy(came.at[t], came.at[t], s_cm.at[d], r_cm.at[d], lax.rem(t + d, n_tp))

    @pl.loop(1, n_req)
    def _(d):
        mv_copy(d).wait_recv()

    came[t] = mvr[meta_s[1, r]]
    for d in range(1, n_tp):
        cm_copy(d).start()

    ag_pass(*o_ag)
    ag_wait(*o_ag)
    for d in range(1, n_tp):
        who = lax.rem(t + n_tp - d, n_tp)
        tp_copy(came.at[who], came.at[who], s_cm.at[d], r_cm.at[d], who).wait_recv()

    @pl.loop(1, n_req)
    def _(d):
        t2_copy(d).wait_recv()

    rs_finish(*attn_rs)
    for h in range(NCH):
        rs_finish(*y_rs(h))
        ag_finish(*x_ag(h))
    ag_finish(*o_ag)
    for d in range(1, n_tp):
        st_copy(d).wait_send()
        cm_copy(d).wait_send()

    @pl.loop(1, n_req)
    def _(d):
        t1_copy(d).wait_send()
        d_copy(d).wait_send()
        t2_copy(d).wait_send()
        r_copy(d).wait_send()
        mv_copy(d).wait_send()


def moe_call(n_req, n_tp, meta, parts, gain, router_t, ids_t, slots, send_tail, tail, hidden, w_out, wg_t, wu_t, wd):
    rows, width = hidden.shape
    cap = 5 * rows * TOP // (4 * n_req)
    nsl = n_req * cap
    crows = nsl // NCH
    nslp = n_req * slot_stride(cap)
    chunk = send_tail.shape[1]
    smem = pl.BlockSpec(memory_space=pltpu.SMEM)
    vmem = pl.BlockSpec(memory_space=pltpu.VMEM)
    anym = pl.BlockSpec(memory_space=pl.ANY)
    dma = pltpu.SemaphoreType.DMA
    n_x = n_tp // 2

    def bf(*shape):
        return pltpu.VMEM(shape, BF16)

    return pl.pallas_call(
        moe_kernel,
        out_shape=(
            jax.ShapeDtypeStruct((n_tp, rows, 128), BF16),
            jax.ShapeDtypeStruct((n_tp, 16, 128), BF16),
            jax.ShapeDtypeStruct((n_req, chunk, 128), BF16),
        ),
        in_specs=[smem] + [vmem] * 10 + [anym] * 6,
        out_specs=(vmem, vmem, vmem),
        scratch_shapes=[
            bf(*tail.shape), bf(rows, 128), bf(rows, 128), bf(*w_out.shape), bf(*wg_t.shape), bf(*wu_t.shape), bf(*wd.shape),
            bf(n_req, chunk, 128), bf(n_req, chunk, 128),
            bf(2, n_x, rows, 128), bf(n_x, rows, 128), bf(n_x, rows, 128), bf(n_x, rows, 128),
            pltpu.VMEM((8, rows), F32), pltpu.VMEM((n_tp, 8, rows), F32),
            bf(nslp, 128), bf(nslp, 128), bf(NCH, n_tp, crows, 128),
            bf(NCH, 2, n_x, crows, 128), bf(NCH, n_x, crows, 128), bf(NCH, n_x, crows, 128), bf(NCH, n_x, crows, 128),
            bf(nslp, 128), bf(nslp, 128),
            bf(16, 128), bf(n_req, 16, 128),
        ]
        + [dma((5,))]
        + [dma((rows // (TB * 8),))]
        + [dma((n_req,))] * 4
        + [dma((n_x,))] * 4
        + [dma((n_tp,))] * 2
        + [dma((n_req,))] * 2
        + [dma((NCH, n_x))] * 8
        + [dma((n_req,))] * 4
        + [dma((n_x,))] * 4
        + [dma((n_tp,))] * 2,
        compiler_params=pltpu.CompilerParams(collective_id=0, has_side_effects=True, vmem_limit_bytes=56 << 20),
        name="moe_exchange",
    )(meta, *parts, gain.reshape(1, -1), router_t, ids_t, slots, send_tail, tail, hidden, w_out, wg_t, wu_t, wd)


def place_kernel(meta_s, mix_ref, came_ref, got_ref, tail_in, out_ref, tail_out, sems):
    rows = tail_out.shape[1]

    def put(k, kv):
        return pltpu.make_async_copy(got_ref.at[k, kv], tail_out.at[kv, meta_s[0, MIG + k]], sems.at[k, kv])

    for k in range(MIG):
        for kv in range(2):

            @pl.when(meta_s[0, MIG + k] < rows)
            def _():
                put(k, kv).start()

    for tt in range(mix_ref.shape[0]):
        out_ref[:, tt * 128 : (tt + 1) * 128] = mix_ref[tt]
    sub = lax.broadcasted_iota(jnp.int32, (16, 128), 0)
    for k in range(MIG):
        slot = meta_s[0, MIG + k]

        @pl.when(slot < rows)
        def _():
            base = pl.multiple_of((slot >> 4) << 4, 16)
            for tt in range(mix_ref.shape[0]):
                cols = slice(tt * 128, (tt + 1) * 128)
                row = came_ref[tt].astype(F32)[k : k + 1, :]
                w = out_ref[pl.ds(base, 16), cols].astype(F32)
                out_ref[pl.ds(base, 16), cols] = jnp.where(sub == slot - base, row, w).astype(BF16)

    for k in range(MIG):
        for kv in range(2):

            @pl.when(meta_s[0, MIG + k] < rows)
            def _():
                put(k, kv).wait()


def place_call(meta, mix, came, got, tail):
    n_tp, rows, wd = mix.shape
    vmem = pl.BlockSpec(memory_space=pltpu.VMEM)
    return pl.pallas_call(
        place_kernel,
        out_shape=(
            jax.ShapeDtypeStruct((rows, n_tp * wd), BF16),
            jax.ShapeDtypeStruct(tail.shape, tail.dtype),
        ),
        in_specs=[pl.BlockSpec(memory_space=pltpu.SMEM), vmem, vmem, vmem, pl.BlockSpec(memory_space=pl.ANY)],
        out_specs=(vmem, pl.BlockSpec(memory_space=pl.ANY)),
        scratch_shapes=[pltpu.SemaphoreType.DMA((MIG, 2))],
        input_output_aliases={4: 1},
        name="place_rows",
    )(meta, mix, came, got, tail)


def body(
    hidden_in, prompt_kv, tail_kv, group_of, prompt_len, tail_len, bucket_of, bias_table, attn_gain, w_query, w_key,
    w_value, w_out, ffn_gain, router_weight, expert_ids, w_gate, w_up, w_down, new_slot,
):
    n_req = lax.axis_size("req")
    n_tp = lax.axis_size("tp")
    ids_t = expert_ids.T
    tail_new, send_tail, slots, meta, *parts = attention_call(
        hidden_in, attn_gain, w_query, w_key, w_value, group_of, prompt_len, tail_len, bucket_of, bias_table.T,
        new_slot, ids_t, prompt_kv, tail_kv,
    )
    pieces = send_tail.reshape(n_req, -1, send_tail.shape[-1])
    mix, came, got = moe_call(
        n_req, n_tp, meta, parts, ffn_gain, router_weight.T, ids_t, slots, pieces, tail_new, hidden_in, w_out,
        w_gate[0].T, w_up[0].T, w_down[0],
    )
    return place_call(meta, mix, came, got.reshape(send_tail.shape), tail_new)


def solution(mesh):
    return jax.shard_map(
        body,
        mesh=mesh,
        in_specs=(
            P("req", None), P(None, "req", None, "tp"), P(None, "req", None, "tp"), P("req"), P("req"), P("req"), P(),
            P(None, "tp"), P(), P(None, "tp"), P(None, "tp"), P(None, "tp"), P("tp", None), P(), P(), P("req", None),
            P("req", None, "tp"), P("req", None, "tp"), P("req", "tp", None), P(),
        ),
        out_specs=(P("req", None), P(None, "req", None, "tp")),
        check_vma=False,
    )
```

```python
import functools

import jax
import jax.numpy as jnp
from jax import lax
from jax.experimental import pallas as pl
from jax.experimental.pallas import tpu as pltpu
from jax.sharding import PartitionSpec as P

F32 = jnp.float32
BF16 = jnp.bfloat16
EPS = 1e-06
NEG = -1e30
RB = 32
UB = 4
TB = 8
TOP = 2
MIG = 4


def slot_stride(cap):
    return -(-cap // 16) * 16


def col_form(row):
    n = row.shape[1]
    return jnp.transpose(jnp.broadcast_to(row.astype(F32), (128, n)))


def migration_tables(ns_ref, meta_ref, rows):
    me = lax.axis_index("req")
    per = rows // 128
    tiles = ns_ref[...].astype(F32)
    shape = tiles.shape
    lane = lax.broadcasted_iota(jnp.int32, shape, 1).astype(F32)
    sub = lax.broadcasted_iota(jnp.int32, shape, 0)
    moved = tiles != sub.astype(F32) * 128.0 + lane
    where_to = jnp.floor(tiles * (1.0 / rows))
    goes = jnp.max(jnp.where(moved, where_to, -1.0), axis=1, keepdims=True)
    src = jnp.max(jnp.where(goes == lane, (sub // per).astype(F32), -1.0), axis=0, keepdims=True)
    src = jnp.where(src < 0.0, lane[0:1], src)

    mine = ns_ref[pl.ds(me * per, per), :].astype(F32)
    row = jnp.concatenate([mine[i : i + 1] for i in range(per)], axis=1)
    col = col_form(row)
    base = (me * rows).astype(F32)
    rid = lax.broadcasted_iota(jnp.int32, (rows, 128), 0).astype(F32)
    rlane = lax.broadcasted_iota(jnp.int32, (rows, 128), 1).astype(F32)
    moved_col = col != rid + base
    order = jnp.zeros((rows, 128), F32)
    place = jnp.zeros((rows, 128), F32)
    for i in range(per):
        part = row[:, i * 128 : (i + 1) * 128]
        other = rlane + float(i * 128)
        moved_row = part != other[0:1] + base
        order = order + jnp.where(moved_row & (part < col), 1.0, 0.0)
        place = place + jnp.where(moved_row & (other < rid), 1.0, 0.0)
    order = jnp.sum(order, axis=1, keepdims=True)
    place = jnp.sum(place, axis=1, keepdims=True)
    out = float(rows)
    send = jnp.min(jnp.where(moved_col & (order == rlane), rid, out), axis=0, keepdims=True)
    send = jnp.minimum(send, out - 1.0)
    vac = jnp.min(jnp.where(moved_col & (place + float(MIG) == rlane), rid, out), axis=0, keepdims=True)
    idx = jnp.where(rlane[0:1] < float(MIG), send, vac)
    s8 = lax.broadcasted_iota(jnp.int32, (8, 128), 0)
    meta_ref[...] = jnp.where(s8 == 0, idx, jnp.where(s8 == 1, src, 0.0)).astype(jnp.int32)


def attn_kernel(
    tl_s, tab_s, plen_s, bkt_s,
    gain_ref, grp_ref, tlr_ref, ns_ref, hid_any, wq_any, wk_any, wv_any, pkv_any, tail_any,
    tail_out, send_ref, meta_ref, q16, tbias, mpart, lpart, opart,
    hid_v, wcat, pkv_v, buf, kvn, lhs, kcat, sco, prob, posb, plb, tlb, dtab,
    first_s, meta_s, s_in, s_tin, s_tout, s_meta,
):
    rows = hid_v.shape[0]
    nb = rows // 8
    groups = pkv_v.shape[1]
    pre = pkv_v.shape[2]
    nbuck = tab_s.shape[1]
    mig = send_ref.shape[0]
    span = bkt_s.shape[0]
    nblk = rows // RB
    loads = [
        pltpu.make_async_copy(hid_any, hid_v, s_in.at[0]),
        pltpu.make_async_copy(wq_any, wcat.at[:, 0:128], s_in.at[1]),
        pltpu.make_async_copy(wk_any, wcat.at[:, 128:256], s_in.at[2]),
        pltpu.make_async_copy(wv_any, wcat.at[:, 256:384], s_in.at[3]),
        pltpu.make_async_copy(pkv_any.at[0], pkv_v.at[0], s_in.at[4]),
        pltpu.make_async_copy(pkv_any.at[1], pkv_v.at[1], s_in.at[5]),
    ]
    for cp in loads:
        cp.start()

    def t_in(s, kv):
        sl = pl.ds(s * RB, RB)
        return pltpu.make_async_copy(tail_any.at[kv, sl], buf.at[kv, sl], s_tin.at[s, kv])

    def t_out(s, kv):
        sl = pl.ds(s * RB, RB)
        return pltpu.make_async_copy(buf.at[kv, sl], tail_out.at[kv, sl], s_tout.at[s, kv])

    @pl.loop(0, nblk)
    def _(s):
        t_in(s, 0).start()
        t_in(s, 1).start()

    for k in range(nbuck):
        first_s[k] = span

    @pl.loop(0, span, unroll=8)
    def _(i):
        d = span - 1 - i
        first_s[bkt_s[d]] = d

    nd = dtab.shape[2] // 128
    dist = [lax.broadcasted_iota(jnp.int32, (8, 128), 1) + c * 128 for c in range(nd)]
    d0 = [jnp.full((8, 128), tab_s[0, 0], F32) for _ in range(nd)]
    d1 = [jnp.full((8, 128), tab_s[1, 0], F32) for _ in range(nd)]
    for k in range(1, nbuck):
        for c in range(nd):
            ge = dist[c] >= first_s[k]
            d0[c] = jnp.where(ge, tab_s[0, k], d0[c])
            d1[c] = jnp.where(ge, tab_s[1, k], d1[c])
    for c in range(nd):
        dtab[0, :, c * 128 : (c + 1) * 128] = d0[c]
        dtab[1, :, c * 128 : (c + 1) * 128] = d1[c]

    migration_tables(ns_ref, meta_ref, rows)
    meta_copy = pltpu.make_async_copy(meta_ref, meta_s, s_meta)
    meta_copy.start()

    g = col_form(grp_ref[...])
    tl = col_form(tlr_ref[...])
    pln = jnp.zeros_like(g)
    for i in range(groups):
        pln = jnp.where(g == float(i), plen_s[i].astype(F32), pln)
    posb[...] = (pln + tl).astype(jnp.int32)
    plb[...] = pln.astype(jnp.int32)
    tlb[...] = tl.astype(jnp.int32)
    g2 = jnp.broadcast_to(g.reshape(nb, 1, 8, 128), (nb, 2, 8, 128)).reshape(2 * rows, 128)

    for cp in loads[:4]:
        cp.wait()
    h = hid_v[...].astype(F32)
    ms = jnp.mean(h * h, axis=-1, keepdims=True)
    n1 = (h * lax.rsqrt(ms + EPS) * gain_ref[...]).astype(BF16)
    qkv = jnp.dot(n1, wcat[...], preferred_element_type=F32).astype(BF16).astype(F32)
    q = qkv[:, 0:128]
    kvn[0] = qkv[:, 128:256]
    kvn[1] = qkv[:, 256:384]
    lane = lax.broadcasted_iota(jnp.int32, (nb, 2, 8, 128), 3)
    head = lax.broadcasted_iota(jnp.int32, (nb, 2, 8, 128), 1)
    qh = jnp.broadcast_to((q * 0.125).reshape(nb, 1, 8, 128), (nb, 2, 8, 128))
    qh = jnp.where((lane // 64) == head, qh, 0.0).reshape(2 * rows, 128)
    q16[...] = qh.astype(BF16)
    loads[4].wait()
    for i in range(groups):
        lhs[:, i * 128 : (i + 1) * 128] = jnp.where(g2 == float(i), qh, 0.0).astype(BF16)
        kcat[:, i * 128 : (i + 1) * 128] = pkv_v[0, i]
    sco[...] = lax.dot_general(lhs[...], kcat[...], (((1,), (1,)), ((), ())), preferred_element_type=F32)

    def take(tab, i):
        return jnp.take_along_axis(tab, i, axis=1, mode="promise_in_bounds")

    nch = pre // 128

    ln = lax.broadcasted_iota(jnp.int32, (8, 128), 1)
    sub = lax.broadcasted_iota(jnp.int32, (8, 128), 0)
    mine = (ln >> 6) == (sub & 1)

    def prompt_softmax(i):
        at = [i * UB + n for n in range(UB)]
        pos = [posb[pl.ds(b * 8, 8), :] for b in at]
        pb = [plb[pl.ds(b * 8, 8), :] for b in at]
        tb = [tlb[pl.ds(b * 8, 8), :] for b in at]
        raw = [
            [[sco[pl.ds(b * 16 + hh * 8, 8), c * 128 : (c + 1) * 128] for c in range(nch)] for hh in range(2)]
            for b in at
        ]
        tabs = [[dtab[hh, :, k * 128 : (k + 1) * 128] for k in range(nd)] for hh in range(2)]
        out = []
        for n in range(UB):
            low = pos[n] & 127
            gi = (low - ln) & 127
            blk = (pos[n] >> 7) - (ln > low).astype(jnp.int32)
            is_blk = [blk == k for k in range(nd)]
            td = tb[n] - (ln & 63)
            valid = (td >= 0) & mine
            td = jnp.maximum(td, 0)
            for hh in range(2):
                tail = jnp.where(valid, take(tabs[hh][0], td), NEG)
                gs = [take(tabs[hh][k], gi) for k in range(nd)]
                s = []
                for c in range(nch):
                    bias = gs[0]
                    for k in range(1, nd - c):
                        bias = jnp.where(is_blk[k + c], gs[k], bias)
                    s.append(jnp.where(ln + c * 128 < pb[n], raw[n][hh][c] + bias, NEG))
                mx = jnp.max(functools.reduce(jnp.maximum, s), axis=1, keepdims=True)
                e = [jnp.exp(v - mx) for v in s]
                tot = jnp.sum(functools.reduce(jnp.add, e), axis=1, keepdims=True)
                out.append((tail, mx, e, tot))
        for n in range(UB):
            for hh in range(2):
                tail, mx, e, tot = out[n * 2 + hh]
                rs = pl.ds(at[n] * 16 + hh * 8, 8)
                tbias[rs, :] = tail
                mpart[rs, :] = jnp.broadcast_to(mx, (8, 128))
                lpart[rs, :] = jnp.broadcast_to(tot, (8, 128))
            for c in range(nch):
                prob[pl.ds(at[n] * 16, 16), c * 128 : (c + 1) * 128] = jnp.concatenate(
                    [out[n * 2][2][c], out[n * 2 + 1][2][c]], axis=0
                ).astype(BF16)

    half = nb // UB // 2
    pl.loop(0, half)(prompt_softmax)

    sub16 = lax.broadcasted_iota(jnp.int32, (16, 128), 0)

    @pl.loop(0, nblk)
    def _(s):
        t_in(s, 0).wait()
        t_in(s, 1).wait()
        for i in range(RB):
            r = s * RB + i
            length = tl_s[r]
            base = pl.multiple_of((length >> 4) << 4, 16)
            for kv in range(2):
                w = buf[kv, r, pl.ds(base, 16), :].astype(F32)
                row = kvn[kv, pl.ds(r, 1), :]
                buf[kv, r, pl.ds(base, 16), :] = jnp.where(sub16 == length - base, row, w).astype(BF16)
        t_out(s, 0).start()
        t_out(s, 1).start()

    pl.loop(half, nb // UB)(prompt_softmax)
    loads[5].wait()
    acc = jnp.zeros((2 * rows, 128), F32)
    for i in range(0, groups, 2):
        rhs = jnp.concatenate([pkv_v[1, i], pkv_v[1, i + 1]], axis=1)
        o = jnp.dot(prob[...], rhs, preferred_element_type=F32)
        acc = jnp.where(g2 == float(i), o[:, 0:128], acc)
        acc = jnp.where(g2 == float(i + 1), o[:, 128:256], acc)
    opart[...] = acc

    meta_copy.wait()
    for m in range(mig):
        for kv in range(2):
            send_ref[m, kv] = buf[kv, meta_s[0, m]]

    @pl.loop(0, nblk)
    def _(s):
        t_out(s, 0).wait()
        t_out(s, 1).wait()


def attention_call(
    hidden_in, gain, wq, wk, wv, group_of, prompt_len, tail_len, bucket_of, table_t, new_slot, prompt_kv, tail_kv
):
    rows, width = hidden_in.shape
    smem = pl.BlockSpec(memory_space=pltpu.SMEM)
    vmem = pl.BlockSpec(memory_space=pltpu.VMEM)
    anym = pl.BlockSpec(memory_space=pl.ANY)
    _, groups, pre, wd = prompt_kv.shape
    tail_rows = tail_kv.shape[2]
    nd = -(-bucket_of.shape[0] // 128)
    nblk = rows // RB
    dma = pltpu.SemaphoreType.DMA
    return pl.pallas_call(
        attn_kernel,
        out_shape=(
            jax.ShapeDtypeStruct(tail_kv.shape, BF16),
            jax.ShapeDtypeStruct((MIG, 2, tail_rows, wd), BF16),
            jax.ShapeDtypeStruct((8, 128), jnp.int32),
            jax.ShapeDtypeStruct((2 * rows, wd), BF16),
        )
        + (jax.ShapeDtypeStruct((2 * rows, 128), F32),) * 4,
        in_specs=[smem] * 4 + [vmem] * 4 + [anym] * 6,
        out_specs=(anym,) + (vmem,) * 7,
        scratch_shapes=[
            pltpu.VMEM((rows, width), BF16),
            pltpu.VMEM((width, 3 * wd), BF16),
            pltpu.VMEM(prompt_kv.shape, BF16),
            pltpu.VMEM(tail_kv.shape, BF16),
            pltpu.VMEM((2, rows, wd), F32),
            pltpu.VMEM((2 * rows, groups * wd), BF16),
            pltpu.VMEM((pre, groups * wd), BF16),
            pltpu.VMEM((2 * rows, pre), F32),
            pltpu.VMEM((2 * rows, pre), BF16),
            pltpu.VMEM((rows, 128), jnp.int32),
            pltpu.VMEM((rows, 128), jnp.int32),
            pltpu.VMEM((rows, 128), jnp.int32),
            pltpu.VMEM((2, 8, nd * 128), F32),
            pltpu.SMEM((table_t.shape[1],), jnp.int32),
            pltpu.SMEM((8, 128), jnp.int32),
            dma((6,)),
            dma((nblk, 2)),
            dma((nblk, 2)),
            dma,
        ],
        compiler_params=pltpu.CompilerParams(vmem_limit_bytes=60 << 20),
        name="attention_tails",
    )(
        tail_len, table_t, prompt_len, bucket_of,
        gain.reshape(1, -1), group_of.reshape(1, -1), tail_len.reshape(1, -1), new_slot.reshape(-1, 128),
        hidden_in, wq, wk, wv, prompt_kv, tail_kv,
    )


MESH = pl.DeviceIdType.MESH
NCH = 2


def moe_kernel(
    meta_s,
    q16, tbias, mpart, lpart, opart, gain_ref, router_ref, ids_ref, tail_ref, kv_any, hid_any, wout_any, wg_any, wu_any, wd_any,
    mix, came, got,
    buf, head_v, hid_v, wout_v, wg_v, wu_v, wd_v,
    t1, t2, part, psib, psend, precv, stat, statr, dsend, drecv, xall, ypart, ysib, ysend, yrecv, rsend, rrecv, mvs, mvr, pickt, pick0, pick1,
    s_in, s_kv, s_t1, r_t1, s_t2, r_t2, s_ps, r_ps, s_px, r_px, s_st, r_st, s_d, r_d, s_gx, r_gx, s_gs, r_gs,
    s_ys, r_ys, s_yx, r_yx, s_r, r_r, s_mv, r_mv, s_ox, r_ox, s_os, r_os, s_cm, r_cm,
):
    r = lax.axis_index("req")
    t = lax.axis_index("tp")
    n_req = t1.shape[0]
    n_tp = mix.shape[0]
    n_x = n_tp // 2
    rows = hid_v.shape[0]
    width = wout_v.shape[1]
    crows = xall.shape[2]
    per = n_req // NCH
    cap = crows // per
    nslp = dsend.shape[0]
    capp = nslp // n_req
    c = lax.rem(t, 2)
    x = t // 2
    sib = x * 2 + 1 - c
    lanes = pl.ds(pl.multiple_of(t * 128, 128), 128)

    loads = [
        pltpu.make_async_copy(wout_any, wout_v, s_in.at[0]),
        pltpu.make_async_copy(hid_any.at[:, lanes], hid_v, s_in.at[1]),
        pltpu.make_async_copy(wg_any, wg_v, s_in.at[2]),
        pltpu.make_async_copy(wu_any, wu_v, s_in.at[3]),
        pltpu.make_async_copy(wd_any, wd_v, s_in.at[4]),
    ]
    nkv = rows // (TB * 8)

    def kv_load(i):
        sl = pl.ds(i * TB * 8, TB * 8)
        return pltpu.make_async_copy(kv_any.at[:, sl], buf.at[:, sl], s_kv.at[i])

    @pl.loop(0, nkv)
    def _(i):
        kv_load(i).start()

    for cp in loads:
        cp.start()

    def tp_copy(src, dst, ss, rs, peer):
        return pltpu.make_async_remote_copy(
            src_ref=src, dst_ref=dst, send_sem=ss, recv_sem=rs, device_id=(r, peer), device_id_type=MESH
        )

    def req_copy(src, dst, ss, rs, peer):
        return pltpu.make_async_remote_copy(
            src_ref=src, dst_ref=dst, send_sem=ss, recv_sem=rs, device_id=(peer, t), device_id_type=MESH
        )

    def xpeer(d):
        return lax.rem(x + d, n_x) * 2 + c

    def xfrom(d):
        return lax.rem(x + n_x - d, n_x) * 2 + c

    barrier = pltpu.get_barrier_semaphore()

    @pl.loop(1, n_tp)
    def _(d):
        pl.semaphore_signal(barrier, inc=1, device_id=(r, lax.rem(t + d, n_tp)), device_id_type=MESH)

    @pl.loop(1, n_req)
    def _(d):
        pl.semaphore_signal(barrier, inc=1, device_id=(lax.rem(r + d, n_req), t), device_id_type=MESH)

    sub16 = lax.broadcasted_iota(jnp.int32, (16, 128), 0)
    pair = lax.rem(sub16, 8) // 2
    lane4 = lax.broadcasted_iota(jnp.int32, (TB, 8, 128), 2)

    @pl.loop(0, nkv)
    def _(i):
        kv_load(i).wait()
        rs = pl.ds(pl.multiple_of(i * TB * 16, TB * 16), TB * 16)
        scs = []
        for n in range(TB):
            b = i * TB + n
            kb = buf[0, pl.ds(b * 8, 8)].reshape(512, 128)
            qb = q16[pl.ds(pl.multiple_of(b * 16, 16), 16), :]
            s4 = lax.dot_general(qb, kb, (((1,), (1,)), ((), ())), preferred_element_type=F32)
            sc = s4[:, 0:128]
            for j in range(1, 4):
                sc = jnp.where(pair == j, s4[:, j * 128 : (j + 1) * 128], sc)
            scs.append(sc)
        sc = jnp.concatenate(scs, axis=0) + tbias[rs, :]
        mp = mpart[rs, :]
        mx = jnp.maximum(jnp.max(sc, axis=1, keepdims=True), mp)
        e = jnp.exp(sc - mx)
        ap = jnp.exp(mp - mx)
        tot = jnp.sum(e, axis=1, keepdims=True) + lpart[rs, :] * ap
        os = []
        for n in range(TB):
            b = i * TB + n
            vb = buf[1, pl.ds(b * 8, 8)].reshape(512, 128)
            en = e[n * 16 : (n + 1) * 16]
            p4 = jnp.concatenate([jnp.where(pair == j, en, 0.0) for j in range(4)], axis=1).astype(BF16)
            os.append(jnp.dot(p4, vb, preferred_element_type=F32))
        o = (jnp.concatenate(os, axis=0) + opart[rs, :] * ap) / tot
        o = o.reshape(TB, 2, 8, 128)
        o = jnp.where(lane4 < 64, o[:, 0], o[:, 1]).reshape(TB * 8, 128)
        head_v[pl.ds(pl.multiple_of(i * TB * 8, TB * 8), TB * 8), :] = o.astype(BF16)

    head = head_v[...]
    loads[0].wait()
    for tt in range(n_tp):
        part[tt % 2, tt // 2] = jnp.dot(
            head, wout_v[:, tt * 128 : (tt + 1) * 128], preferred_element_type=F32
        ).astype(BF16)

    pl.semaphore_wait(barrier, n_tp - 1 + n_req - 1)

    def rs_sib(d, buf, dst, ss, rs):
        xx = lax.rem(x + d, n_x)
        return tp_copy(buf.at[1 - c, xx], dst.at[xx], ss.at[d], rs.at[d], sib)

    def rs_x(d, buf, dst, ss, rs):
        return tp_copy(buf.at[d], dst.at[d], ss.at[d], rs.at[d], xpeer(d))

    def rs_start(buf, bsib, ss1, rs1):
        for d in (2, 1, 3, 0):
            rs_sib(d, buf, bsib, ss1, rs1).start()

    def rs_send(buf, bsib, bsend, brecv, ss1, rs1, ss2, rs2):
        for d in (2, 1, 3):
            xx = lax.rem(x + d, n_x)
            rs_sib(d, buf, bsib, ss1, rs1).wait_recv()
            bsend[d] = (buf[c, xx].astype(F32) + bsib[xx].astype(F32)).astype(BF16)
            rs_x(d, bsend, brecv, ss2, rs2).start()

    def rs_total(buf, bsib, bsend, brecv, ss1, rs1, ss2, rs2):
        rs_sib(0, buf, bsib, ss1, rs1).wait_recv()
        tot = buf[c, x].astype(F32) + bsib[x].astype(F32)
        for d in (1, 3, 2):
            rs_x(d, bsend, brecv, ss2, rs2).wait_recv()
            tot = tot + brecv[d].astype(F32)
        return tot

    def rs_finish(buf, bsib, bsend, brecv, ss1, rs1, ss2, rs2):
        for d in (0, 1, 2, 3):
            rs_sib(d, buf, bsib, ss1, rs1).wait_send()
        for d in (1, 2, 3):
            rs_x(d, bsend, brecv, ss2, rs2).wait_send()

    def ag_x(d, buf, ss, rs):
        return tp_copy(buf.at[t], buf.at[t], ss.at[d], rs.at[d], xpeer(d))

    def ag_s(d, buf, ss, rs):
        who = xfrom(d)
        return tp_copy(buf.at[who], buf.at[who], ss.at[d], rs.at[d], sib)

    def ag_start(buf, ss1, rs1, ss2, rs2):
        for d in (2, 1, 3):
            ag_x(d, buf, ss1, rs1).start()
        ag_s(0, buf, ss2, rs2).start()

    def ag_left(buf, ss1, rs1, ss2, rs2):
        for d in (2, 1, 3):
            ag_x(d, buf, ss1, rs1).wait_send()

    def ag_pass(buf, ss1, rs1, ss2, rs2):
        for d in (1, 3, 2):
            who = xfrom(d)
            tp_copy(buf.at[who], buf.at[who], ss1.at[d], rs1.at[d], xpeer(d)).wait_recv()
            ag_s(d, buf, ss2, rs2).start()

    def ag_wait(buf, ss1, rs1, ss2, rs2):
        for d in (0, 1, 3, 2):
            mine = xfrom(d)
            other = lax.rem(x + n_x - d, n_x) * 2 + 1 - c
            tp_copy(buf.at[mine], buf.at[other], ss2.at[d], rs2.at[d], sib).wait_recv()

    def ag_finish(buf, ss1, rs1, ss2, rs2, left=False):
        if not left:
            ag_left(buf, ss1, rs1, ss2, rs2)
        for d in (0, 1, 2, 3):
            ag_s(d, buf, ss2, rs2).wait_send()

    attn_rs = (part, psib, psend, precv, s_ps, r_ps, s_px, r_px)
    rs_start(part, psib, s_ps, r_ps)
    rs_send(*attn_rs)

    def t1_copy(d):
        j = lax.rem(r + d, n_req)
        return req_copy(tail_ref.at[j], t1.at[r], s_t1.at[d], r_t1.at[d], j)

    lnf = lax.broadcasted_iota(jnp.int32, (rows, 128), 1).astype(F32)
    e0 = col_form(ids_ref[0:1, :])
    e1 = col_form(ids_ref[1:2, :])
    hit0 = lnf == e0
    hit1 = lnf == e1
    lower = lax.broadcasted_iota(jnp.int32, (rows, rows), 1) < lax.broadcasted_iota(jnp.int32, (rows, rows), 0)
    lower = lower.astype(F32).astype(BF16)
    o0 = hit0.astype(F32)
    o1 = hit1.astype(F32)
    cum0 = jnp.dot(lower, o0.astype(BF16), preferred_element_type=F32)
    cum1 = jnp.dot(lower, o1.astype(BF16), preferred_element_type=F32)
    tot0 = jnp.sum(o0, axis=0, keepdims=True)
    s0 = e0 * float(capp) + jnp.sum(jnp.where(hit0, cum0, 0.0), axis=1, keepdims=True)
    s1 = e1 * float(capp) + jnp.sum(jnp.where(hit1, cum1 + tot0, 0.0), axis=1, keepdims=True)
    row0 = jnp.transpose(s0)[0:1]
    row1 = jnp.transpose(s1)[0:1]
    sl = lax.broadcasted_iota(jnp.int32, (128, rows), 0).astype(F32)
    for k in range(nslp // 128):
        here = sl + float(k * 128)
        pickt[k * 128 : (k + 1) * 128, :] = ((here == row0) | (here == row1)).astype(F32).astype(BF16)
    loads[1].wait()
    resid = (hid_v[...].astype(F32) + rs_total(*attn_rs)).astype(BF16)

    dsend[...] = jnp.dot(pickt[...], resid, preferred_element_type=F32).astype(BF16)

    def block(j):
        return pl.ds(pl.multiple_of(j * capp, 16), capp)

    def d_copy(d):
        j = lax.rem(r + d, n_req)
        return req_copy(dsend.at[block(j)], drecv.at[block(r)], s_d.at[d], r_d.at[d], j)

    @pl.loop(1, n_req)
    def _(d):
        d_copy(d).start()

    drecv[block(r), :] = dsend[block(r), :]


    rf = resid.astype(F32)
    u = rf * gain_ref[:, lanes]
    lg = lax.dot_general(
        u.astype(BF16), router_ref[:, lanes], (((1,), (1,)), ((), ())), preferred_element_type=F32
    )
    n_e = lg.shape[1]
    ex = lnf[:, 0:n_e]
    diff = jnp.sum(
        jnp.where(ex == e0[:, 0:n_e], lg, 0.0) - jnp.where(ex == e1[:, 0:n_e], lg, 0.0), axis=1, keepdims=True
    )
    sq = jnp.sum(rf * rf, axis=1, keepdims=True)
    stat[...] = jnp.transpose(jnp.where(lnf == 0.0, sq, jnp.where(lnf == 1.0, diff, 0.0)))[0:8]

    def st_copy(d):
        return tp_copy(stat, statr.at[d], s_st.at[d], r_st.at[d], lax.rem(t + d, n_tp))

    for d in range(1, n_tp):
        st_copy(d).start()

    @pl.loop(1, n_req)
    def _(d):
        d_copy(d).wait_recv()

    def x_ag(h):
        return (xall.at[h], s_gx.at[h], r_gx.at[h], s_gs.at[h], r_gs.at[h])

    for h in range(NCH):
        xall[h, t] = jnp.concatenate(
            [drecv[j * capp : (j + 1) * capp, :].astype(F32)[0:cap] for j in range(h * per, (h + 1) * per)], axis=0
        ).astype(BF16)
        ag_start(*x_ag(h))

    @pl.loop(1, n_req)
    def _(d):
        t1_copy(d).start()

    t1[r] = tail_ref[r]

    tot = stat[...]
    for d in range(1, n_tp):
        st_copy(d).wait_recv()
        tot = tot + statr[d]
    tot = jnp.transpose(jnp.concatenate([tot, jnp.zeros((120, rows), F32)], axis=0))
    gate = jax.nn.sigmoid(tot[:, 1:2] * lax.rsqrt(tot[:, 0:1] * (1.0 / width) + EPS))

    for cp in loads[2:]:
        cp.wait()

    def ffn(h):
        xm = jnp.concatenate([xall[h, tt] for tt in range(n_tp)], axis=1).astype(F32)
        ms = jnp.mean(xm * xm, axis=-1, keepdims=True)
        nm = (xm * lax.rsqrt(ms + EPS) * gain_ref[...]).astype(BF16)
        gh = lax.dot_general(nm, wg_v[...], (((1,), (1,)), ((), ())), preferred_element_type=F32)
        uh = lax.dot_general(nm, wu_v[...], (((1,), (1,)), ((), ())), preferred_element_type=F32)
        act = (jax.nn.gelu(gh, approximate=True) * uh).astype(BF16)
        y = jnp.dot(act, wd_v[...], preferred_element_type=F32).astype(BF16)
        for tt in range(n_tp):
            ypart[h, tt % 2, tt // 2] = y[:, tt * 128 : (tt + 1) * 128]

    def y_rs(h):
        return (
            ypart.at[h], ysib.at[h], ysend.at[h], yrecv.at[h], s_ys.at[h], r_ys.at[h], s_yx.at[h], r_yx.at[h]
        )

    ag_pass(*x_ag(0))
    for h in range(NCH):
        ag_wait(*x_ag(h))
        ffn(h)
        rs_start(ypart.at[h], ysib.at[h], s_ys.at[h], r_ys.at[h])
        if h + 1 < NCH:
            ag_pass(*x_ag(h + 1))
        rs_send(*y_rs(h))

    @pl.loop(1, n_req)
    def _(d):
        t1_copy(d).wait_recv()

    @pl.loop(0, n_req)
    def _(j):
        t2[j] = t1[meta_s[1, j]]

    def t2_copy(d):
        j = lax.rem(r + d, n_req)
        return req_copy(t2.at[j], got.at[r], s_t2.at[d], r_t2.at[d], j)

    @pl.loop(1, n_req)
    def _(d):
        t2_copy(d).start()

    got[r] = t2[r]

    def r_copy(d):
        j = lax.rem(r + d, n_req)
        return req_copy(rsend.at[block(j)], rrecv.at[block(r)], s_r.at[d], r_r.at[d], j)

    pad = jnp.zeros((capp - cap, 128), F32)
    for h in range(NCH):
        tot = rs_total(*y_rs(h))
        for i in range(per):
            j = h * per + i
            rsend[j * capp : (j + 1) * capp, :] = jnp.concatenate(
                [tot[i * cap : (i + 1) * cap], pad], axis=0
            ).astype(BF16)

        @pl.loop(h * per, (h + 1) * per)
        def _(j):
            @pl.when(j != r)
            def _():
                r_copy(lax.rem(j + n_req - r, n_req)).start()

    rrecv[block(r), :] = rsend[block(r), :]

    for k in range(nslp // 128):
        here = lnf + float(k * 128)
        pick0[:, k * 128 : (k + 1) * 128] = (s0 == here).astype(F32).astype(BF16)
        pick1[:, k * 128 : (k + 1) * 128] = (s1 == here).astype(F32).astype(BF16)

    @pl.loop(1, n_req)
    def _(d):
        r_copy(d).wait_recv()

    p0 = jnp.dot(pick0[...], rrecv[...], preferred_element_type=F32)
    p1 = jnp.dot(pick1[...], rrecv[...], preferred_element_type=F32)
    mixed = (rf + gate * p0 + (1.0 - gate) * p1).astype(BF16)

    kk = lax.broadcasted_iota(jnp.int32, (16, rows), 0)
    rr = lax.broadcasted_iota(jnp.int32, (16, rows), 1)
    pick = jnp.zeros((16, rows), F32)
    for k in range(MIG):
        pick = jnp.where((kk == k) & (rr == meta_s[0, k]), 1.0, pick)
    mvs[...] = jnp.dot(pick.astype(BF16), mixed, preferred_element_type=F32).astype(BF16)

    def mv_copy(d):
        j = lax.rem(r + d, n_req)
        return req_copy(mvs, mvr.at[r], s_mv.at[d], r_mv.at[d], j)

    mix[t] = mixed
    o_ag = (mix, s_ox, r_ox, s_os, r_os)
    ag_start(*o_ag)

    @pl.loop(1, n_req)
    def _(d):
        mv_copy(d).start()

    mvr[r] = mvs[...]

    rs_finish(*attn_rs)
    for h in range(NCH):
        rs_finish(*y_rs(h))
        ag_finish(*x_ag(h), left=False)
    for d in range(1, n_tp):
        st_copy(d).wait_send()

    @pl.loop(1, n_req)
    def _(d):
        t1_copy(d).wait_send()
        d_copy(d).wait_send()
        t2_copy(d).wait_send()
        r_copy(d).wait_send()

    def cm_copy(d):
        return tp_copy(came.at[t], came.at[t], s_cm.at[d], r_cm.at[d], lax.rem(t + d, n_tp))

    @pl.loop(1, n_req)
    def _(d):
        mv_copy(d).wait_recv()

    came[t] = mvr[meta_s[1, r]]
    for d in range(1, n_tp):
        cm_copy(d).start()

    ag_pass(*o_ag)
    ag_wait(*o_ag)
    for d in range(1, n_tp):
        who = lax.rem(t + n_tp - d, n_tp)
        tp_copy(came.at[who], came.at[who], s_cm.at[d], r_cm.at[d], who).wait_recv()

    @pl.loop(1, n_req)
    def _(d):
        t2_copy(d).wait_recv()

    ag_finish(*o_ag)
    for d in range(1, n_tp):
        cm_copy(d).wait_send()

    @pl.loop(1, n_req)
    def _(d):
        mv_copy(d).wait_send()


def moe_call(n_req, n_tp, meta, parts, gain, router_t, ids_t, send_tail, tail, hidden, w_out, wg_t, wu_t, wd):
    rows, width = hidden.shape
    cap = 5 * rows * TOP // (4 * n_req)
    nsl = n_req * cap
    crows = nsl // NCH
    nslp = n_req * slot_stride(cap)
    chunk = send_tail.shape[1]
    smem = pl.BlockSpec(memory_space=pltpu.SMEM)
    vmem = pl.BlockSpec(memory_space=pltpu.VMEM)
    anym = pl.BlockSpec(memory_space=pl.ANY)
    dma = pltpu.SemaphoreType.DMA
    n_x = n_tp // 2

    def bf(*shape):
        return pltpu.VMEM(shape, BF16)

    return pl.pallas_call(
        moe_kernel,
        out_shape=(
            jax.ShapeDtypeStruct((n_tp, rows, 128), BF16),
            jax.ShapeDtypeStruct((n_tp, 16, 128), BF16),
            jax.ShapeDtypeStruct((n_req, chunk, 128), BF16),
        ),
        in_specs=[smem] + [vmem] * 9 + [anym] * 6,
        out_specs=(vmem, vmem, vmem),
        scratch_shapes=[
            bf(*tail.shape), bf(rows, 128), bf(rows, 128), bf(*w_out.shape), bf(*wg_t.shape), bf(*wu_t.shape), bf(*wd.shape),
            bf(n_req, chunk, 128), bf(n_req, chunk, 128),
            bf(2, n_x, rows, 128), bf(n_x, rows, 128), bf(n_x, rows, 128), bf(n_x, rows, 128),
            pltpu.VMEM((8, rows), F32), pltpu.VMEM((n_tp, 8, rows), F32),
            bf(nslp, 128), bf(nslp, 128), bf(NCH, n_tp, crows, 128),
            bf(NCH, 2, n_x, crows, 128), bf(NCH, n_x, crows, 128), bf(NCH, n_x, crows, 128), bf(NCH, n_x, crows, 128),
            bf(nslp, 128), bf(nslp, 128),
            bf(16, 128), bf(n_req, 16, 128), bf(nslp, rows), bf(rows, nslp), bf(rows, nslp),
        ]
        + [dma((5,))]
        + [dma((rows // (TB * 8),))]
        + [dma((n_req,))] * 4
        + [dma((n_x,))] * 4
        + [dma((n_tp,))] * 2
        + [dma((n_req,))] * 2
        + [dma((NCH, n_x))] * 8
        + [dma((n_req,))] * 4
        + [dma((n_x,))] * 4
        + [dma((n_tp,))] * 2,
        compiler_params=pltpu.CompilerParams(collective_id=0, has_side_effects=True, vmem_limit_bytes=56 << 20),
        name="moe_exchange",
    )(meta, *parts, gain.reshape(1, -1), router_t, ids_t, send_tail, tail, hidden, w_out, wg_t, wu_t, wd)


def place_kernel(meta_s, mix_ref, came_ref, got_ref, tail_in, out_ref, tail_out, sems):
    rows = tail_out.shape[1]

    def put(k, kv):
        return pltpu.make_async_copy(got_ref.at[k, kv], tail_out.at[kv, meta_s[0, MIG + k]], sems.at[k, kv])

    for k in range(MIG):
        for kv in range(2):

            @pl.when(meta_s[0, MIG + k] < rows)
            def _():
                put(k, kv).start()

    for tt in range(mix_ref.shape[0]):
        out_ref[:, tt * 128 : (tt + 1) * 128] = mix_ref[tt]
    sub = lax.broadcasted_iota(jnp.int32, (16, 128), 0)
    for k in range(MIG):
        slot = meta_s[0, MIG + k]

        @pl.when(slot < rows)
        def _():
            base = pl.multiple_of((slot >> 4) << 4, 16)
            for tt in range(mix_ref.shape[0]):
                cols = slice(tt * 128, (tt + 1) * 128)
                row = came_ref[tt].astype(F32)[k : k + 1, :]
                w = out_ref[pl.ds(base, 16), cols].astype(F32)
                out_ref[pl.ds(base, 16), cols] = jnp.where(sub == slot - base, row, w).astype(BF16)

    for k in range(MIG):
        for kv in range(2):

            @pl.when(meta_s[0, MIG + k] < rows)
            def _():
                put(k, kv).wait()


def place_call(meta, mix, came, got, tail):
    n_tp, rows, wd = mix.shape
    vmem = pl.BlockSpec(memory_space=pltpu.VMEM)
    return pl.pallas_call(
        place_kernel,
        out_shape=(
            jax.ShapeDtypeStruct((rows, n_tp * wd), BF16),
            jax.ShapeDtypeStruct(tail.shape, tail.dtype),
        ),
        in_specs=[pl.BlockSpec(memory_space=pltpu.SMEM), vmem, vmem, vmem, pl.BlockSpec(memory_space=pl.ANY)],
        out_specs=(vmem, pl.BlockSpec(memory_space=pl.ANY)),
        scratch_shapes=[pltpu.SemaphoreType.DMA((MIG, 2))],
        input_output_aliases={4: 1},
        name="place_rows",
    )(meta, mix, came, got, tail)


def body(
    hidden_in, prompt_kv, tail_kv, group_of, prompt_len, tail_len, bucket_of, bias_table, attn_gain, w_query, w_key,
    w_value, w_out, ffn_gain, router_weight, expert_ids, w_gate, w_up, w_down, new_slot,
):
    n_req = lax.axis_size("req")
    n_tp = lax.axis_size("tp")
    ids_t = expert_ids.T
    tail_new, send_tail, meta, *parts = attention_call(
        hidden_in, attn_gain, w_query, w_key, w_value, group_of, prompt_len, tail_len, bucket_of, bias_table.T,
        new_slot, prompt_kv, tail_kv,
    )
    pieces = send_tail.reshape(n_req, -1, send_tail.shape[-1])
    mix, came, got = moe_call(
        n_req, n_tp, meta, parts, ffn_gain, router_weight.T, ids_t, pieces, tail_new, hidden_in, w_out,
        w_gate[0].T, w_up[0].T, w_down[0],
    )
    return place_call(meta, mix, came, got.reshape(send_tail.shape), tail_new)


def solution(mesh):
    return jax.shard_map(
        body,
        mesh=mesh,
        in_specs=(
            P("req", None), P(None, "req", None, "tp"), P(None, "req", None, "tp"), P("req"), P("req"), P("req"), P(),
            P(None, "tp"), P(), P(None, "tp"), P(None, "tp"), P(None, "tp"), P("tp", None), P(), P(), P("req", None),
            P("req", None, "tp"), P("req", None, "tp"), P("req", "tp", None), P(),
        ),
        out_specs=(P("req", None), P(None, "req", None, "tp")),
        check_vma=False,
    )
```

```python
import functools

import jax
import jax.numpy as jnp
from jax import lax
from jax.experimental import pallas as pl
from jax.experimental.pallas import tpu as pltpu
from jax.sharding import PartitionSpec as P

F32 = jnp.float32
BF16 = jnp.bfloat16
EPS = 1e-06
NEG = -1e30
RB = 32
UB = 4
TB = 8
TOP = 2
MIG = 4


def slot_stride(cap):
    return -(-cap // 16) * 16


def col_form(row):
    n = row.shape[1]
    return jnp.transpose(jnp.broadcast_to(row.astype(F32), (128, n)))


def migration_tables(ns_ref, meta_ref, rows):
    me = lax.axis_index("req")
    per = rows // 128
    tiles = ns_ref[...].astype(F32)
    shape = tiles.shape
    lane = lax.broadcasted_iota(jnp.int32, shape, 1).astype(F32)
    sub = lax.broadcasted_iota(jnp.int32, shape, 0)
    moved = tiles != sub.astype(F32) * 128.0 + lane
    where_to = jnp.floor(tiles * (1.0 / rows))
    goes = jnp.max(jnp.where(moved, where_to, -1.0), axis=1, keepdims=True)
    src = jnp.max(jnp.where(goes == lane, (sub // per).astype(F32), -1.0), axis=0, keepdims=True)
    src = jnp.where(src < 0.0, lane[0:1], src)

    mine = ns_ref[pl.ds(me * per, per), :].astype(F32)
    row = jnp.concatenate([mine[i : i + 1] for i in range(per)], axis=1)
    col = col_form(row)
    base = (me * rows).astype(F32)
    rid = lax.broadcasted_iota(jnp.int32, (rows, 128), 0).astype(F32)
    rlane = lax.broadcasted_iota(jnp.int32, (rows, 128), 1).astype(F32)
    moved_col = col != rid + base
    order = jnp.zeros((rows, 128), F32)
    place = jnp.zeros((rows, 128), F32)
    for i in range(per):
        part = row[:, i * 128 : (i + 1) * 128]
        other = rlane + float(i * 128)
        moved_row = part != other[0:1] + base
        order = order + jnp.where(moved_row & (part < col), 1.0, 0.0)
        place = place + jnp.where(moved_row & (other < rid), 1.0, 0.0)
    order = jnp.sum(order, axis=1, keepdims=True)
    place = jnp.sum(place, axis=1, keepdims=True)
    out = float(rows)
    send = jnp.min(jnp.where(moved_col & (order == rlane), rid, out), axis=0, keepdims=True)
    send = jnp.minimum(send, out - 1.0)
    vac = jnp.min(jnp.where(moved_col & (place + float(MIG) == rlane), rid, out), axis=0, keepdims=True)
    idx = jnp.where(rlane[0:1] < float(MIG), send, vac)
    s8 = lax.broadcasted_iota(jnp.int32, (8, 128), 0)
    meta_ref[...] = jnp.where(s8 == 0, idx, jnp.where(s8 == 1, src, 0.0)).astype(jnp.int32)


def attn_kernel(
    tl_s, tab_s, plen_s, bkt_s,
    gain_ref, grp_ref, tlr_ref, ns_ref, hid_any, wq_any, wk_any, wv_any, pkv_any, tail_any,
    tail_out, send_ref, meta_ref, q16, tbias, mpart, lpart, opart,
    hid_v, wcat, pkv_v, buf, kvn, lhs, kcat, sco, prob, posb, plb, tlb, dtab,
    first_s, meta_s, s_in, s_tin, s_tout, s_meta,
):
    rows = hid_v.shape[0]
    nb = rows // 8
    groups = pkv_v.shape[1]
    pre = pkv_v.shape[2]
    nbuck = tab_s.shape[1]
    mig = send_ref.shape[0]
    span = bkt_s.shape[0]
    nblk = rows // RB
    loads = [
        pltpu.make_async_copy(hid_any, hid_v, s_in.at[0]),
        pltpu.make_async_copy(wq_any, wcat.at[:, 0:128], s_in.at[1]),
        pltpu.make_async_copy(wk_any, wcat.at[:, 128:256], s_in.at[2]),
        pltpu.make_async_copy(wv_any, wcat.at[:, 256:384], s_in.at[3]),
        pltpu.make_async_copy(pkv_any.at[0], pkv_v.at[0], s_in.at[4]),
        pltpu.make_async_copy(pkv_any.at[1], pkv_v.at[1], s_in.at[5]),
    ]
    for cp in loads:
        cp.start()

    def t_in(s, kv):
        sl = pl.ds(s * RB, RB)
        return pltpu.make_async_copy(tail_any.at[kv, sl], buf.at[kv, sl], s_tin.at[s, kv])

    def t_out(s, kv):
        sl = pl.ds(s * RB, RB)
        return pltpu.make_async_copy(buf.at[kv, sl], tail_out.at[kv, sl], s_tout.at[s, kv])

    @pl.loop(0, nblk)
    def _(s):
        t_in(s, 0).start()
        t_in(s, 1).start()

    for k in range(nbuck):
        first_s[k] = span

    @pl.loop(0, span, unroll=8)
    def _(i):
        d = span - 1 - i
        first_s[bkt_s[d]] = d

    nd = dtab.shape[2] // 128
    dist = [lax.broadcasted_iota(jnp.int32, (8, 128), 1) + c * 128 for c in range(nd)]
    d0 = [jnp.full((8, 128), tab_s[0, 0], F32) for _ in range(nd)]
    d1 = [jnp.full((8, 128), tab_s[1, 0], F32) for _ in range(nd)]
    for k in range(1, nbuck):
        for c in range(nd):
            ge = dist[c] >= first_s[k]
            d0[c] = jnp.where(ge, tab_s[0, k], d0[c])
            d1[c] = jnp.where(ge, tab_s[1, k], d1[c])
    for c in range(nd):
        dtab[0, :, c * 128 : (c + 1) * 128] = d0[c]
        dtab[1, :, c * 128 : (c + 1) * 128] = d1[c]

    migration_tables(ns_ref, meta_ref, rows)
    meta_copy = pltpu.make_async_copy(meta_ref, meta_s, s_meta)
    meta_copy.start()

    g = col_form(grp_ref[...])
    tl = col_form(tlr_ref[...])
    pln = jnp.zeros_like(g)
    for i in range(groups):
        pln = jnp.where(g == float(i), plen_s[i].astype(F32), pln)
    posb[...] = (pln + tl).astype(jnp.int32)
    plb[...] = pln.astype(jnp.int32)
    tlb[...] = tl.astype(jnp.int32)
    g2 = jnp.broadcast_to(g.reshape(nb, 1, 8, 128), (nb, 2, 8, 128)).reshape(2 * rows, 128)

    for cp in loads[:4]:
        cp.wait()
    h = hid_v[...].astype(F32)
    ms = jnp.mean(h * h, axis=-1, keepdims=True)
    n1 = (h * lax.rsqrt(ms + EPS) * gain_ref[...]).astype(BF16)
    qkv = jnp.dot(n1, wcat[...], preferred_element_type=F32).astype(BF16).astype(F32)
    q = qkv[:, 0:128]
    kvn[0] = qkv[:, 128:256]
    kvn[1] = qkv[:, 256:384]
    lane = lax.broadcasted_iota(jnp.int32, (nb, 2, 8, 128), 3)
    head = lax.broadcasted_iota(jnp.int32, (nb, 2, 8, 128), 1)
    qh = jnp.broadcast_to((q * 0.125).reshape(nb, 1, 8, 128), (nb, 2, 8, 128))
    qh = jnp.where((lane // 64) == head, qh, 0.0).reshape(2 * rows, 128)
    q16[...] = qh.astype(BF16)
    loads[4].wait()
    for i in range(groups):
        lhs[:, i * 128 : (i + 1) * 128] = jnp.where(g2 == float(i), qh, 0.0).astype(BF16)
        kcat[:, i * 128 : (i + 1) * 128] = pkv_v[0, i]
    sco[...] = lax.dot_general(lhs[...], kcat[...], (((1,), (1,)), ((), ())), preferred_element_type=F32)

    def take(tab, i):
        return jnp.take_along_axis(tab, i, axis=1, mode="promise_in_bounds")

    nch = pre // 128

    ln = lax.broadcasted_iota(jnp.int32, (8, 128), 1)
    sub = lax.broadcasted_iota(jnp.int32, (8, 128), 0)
    mine = (ln >> 6) == (sub & 1)

    def prompt_softmax(i):
        at = [i * UB + n for n in range(UB)]
        pos = [posb[pl.ds(b * 8, 8), :] for b in at]
        pb = [plb[pl.ds(b * 8, 8), :] for b in at]
        tb = [tlb[pl.ds(b * 8, 8), :] for b in at]
        raw = [
            [[sco[pl.ds(b * 16 + hh * 8, 8), c * 128 : (c + 1) * 128] for c in range(nch)] for hh in range(2)]
            for b in at
        ]
        tabs = [[dtab[hh, :, k * 128 : (k + 1) * 128] for k in range(nd)] for hh in range(2)]
        out = []
        for n in range(UB):
            low = pos[n] & 127
            gi = (low - ln) & 127
            blk = (pos[n] >> 7) - (ln > low).astype(jnp.int32)
            is_blk = [blk == k for k in range(nd)]
            td = tb[n] - (ln & 63)
            valid = (td >= 0) & mine
            td = jnp.maximum(td, 0)
            for hh in range(2):
                tail = jnp.where(valid, take(tabs[hh][0], td), NEG)
                gs = [take(tabs[hh][k], gi) for k in range(nd)]
                s = []
                for c in range(nch):
                    bias = gs[0]
                    for k in range(1, nd - c):
                        bias = jnp.where(is_blk[k + c], gs[k], bias)
                    s.append(jnp.where(ln + c * 128 < pb[n], raw[n][hh][c] + bias, NEG))
                mx = jnp.max(functools.reduce(jnp.maximum, s), axis=1, keepdims=True)
                e = [jnp.exp(v - mx) for v in s]
                tot = jnp.sum(functools.reduce(jnp.add, e), axis=1, keepdims=True)
                out.append((tail, mx, e, tot))
        for n in range(UB):
            for hh in range(2):
                tail, mx, e, tot = out[n * 2 + hh]
                rs = pl.ds(at[n] * 16 + hh * 8, 8)
                tbias[rs, :] = tail
                mpart[rs, :] = jnp.broadcast_to(mx, (8, 128))
                lpart[rs, :] = jnp.broadcast_to(tot, (8, 128))
            for c in range(nch):
                prob[pl.ds(at[n] * 16, 16), c * 128 : (c + 1) * 128] = jnp.concatenate(
                    [out[n * 2][2][c], out[n * 2 + 1][2][c]], axis=0
                ).astype(BF16)

    half = nb // UB // 2
    pl.loop(0, half)(prompt_softmax)

    sub16 = lax.broadcasted_iota(jnp.int32, (16, 128), 0)

    @pl.loop(0, nblk)
    def _(s):
        t_in(s, 0).wait()
        t_in(s, 1).wait()
        for i in range(RB):
            r = s * RB + i
            length = tl_s[r]
            base = pl.multiple_of((length >> 4) << 4, 16)
            for kv in range(2):
                w = buf[kv, r, pl.ds(base, 16), :].astype(F32)
                row = kvn[kv, pl.ds(r, 1), :]
                buf[kv, r, pl.ds(base, 16), :] = jnp.where(sub16 == length - base, row, w).astype(BF16)
        t_out(s, 0).start()
        t_out(s, 1).start()

    pl.loop(half, nb // UB)(prompt_softmax)
    loads[5].wait()
    acc = jnp.zeros((2 * rows, 128), F32)
    for i in range(0, groups, 2):
        rhs = jnp.concatenate([pkv_v[1, i], pkv_v[1, i + 1]], axis=1)
        o = jnp.dot(prob[...], rhs, preferred_element_type=F32)
        acc = jnp.where(g2 == float(i), o[:, 0:128], acc)
        acc = jnp.where(g2 == float(i + 1), o[:, 128:256], acc)
    opart[...] = acc

    meta_copy.wait()
    for m in range(mig):
        for kv in range(2):
            send_ref[m, kv] = buf[kv, meta_s[0, m]]

    @pl.loop(0, nblk)
    def _(s):
        t_out(s, 0).wait()
        t_out(s, 1).wait()


def attention_call(
    hidden_in, gain, wq, wk, wv, group_of, prompt_len, tail_len, bucket_of, table_t, new_slot, prompt_kv, tail_kv
):
    rows, width = hidden_in.shape
    smem = pl.BlockSpec(memory_space=pltpu.SMEM)
    vmem = pl.BlockSpec(memory_space=pltpu.VMEM)
    anym = pl.BlockSpec(memory_space=pl.ANY)
    _, groups, pre, wd = prompt_kv.shape
    tail_rows = tail_kv.shape[2]
    nd = -(-bucket_of.shape[0] // 128)
    nblk = rows // RB
    dma = pltpu.SemaphoreType.DMA
    return pl.pallas_call(
        attn_kernel,
        out_shape=(
            jax.ShapeDtypeStruct(tail_kv.shape, BF16),
            jax.ShapeDtypeStruct((MIG, 2, tail_rows, wd), BF16),
            jax.ShapeDtypeStruct((8, 128), jnp.int32),
            jax.ShapeDtypeStruct((2 * rows, wd), BF16),
        )
        + (jax.ShapeDtypeStruct((2 * rows, 128), F32),) * 4,
        in_specs=[smem] * 4 + [vmem] * 4 + [anym] * 6,
        out_specs=(anym,) + (vmem,) * 7,
        scratch_shapes=[
            pltpu.VMEM((rows, width), BF16),
            pltpu.VMEM((width, 3 * wd), BF16),
            pltpu.VMEM(prompt_kv.shape, BF16),
            pltpu.VMEM(tail_kv.shape, BF16),
            pltpu.VMEM((2, rows, wd), F32),
            pltpu.VMEM((2 * rows, groups * wd), BF16),
            pltpu.VMEM((pre, groups * wd), BF16),
            pltpu.VMEM((2 * rows, pre), F32),
            pltpu.VMEM((2 * rows, pre), BF16),
            pltpu.VMEM((rows, 128), jnp.int32),
            pltpu.VMEM((rows, 128), jnp.int32),
            pltpu.VMEM((rows, 128), jnp.int32),
            pltpu.VMEM((2, 8, nd * 128), F32),
            pltpu.SMEM((table_t.shape[1],), jnp.int32),
            pltpu.SMEM((8, 128), jnp.int32),
            dma((6,)),
            dma((nblk, 2)),
            dma((nblk, 2)),
            dma,
        ],
        compiler_params=pltpu.CompilerParams(vmem_limit_bytes=60 << 20),
        name="attention_tails",
    )(
        tail_len, table_t, prompt_len, bucket_of,
        gain.reshape(1, -1), group_of.reshape(1, -1), tail_len.reshape(1, -1), new_slot.reshape(-1, 128),
        hidden_in, wq, wk, wv, prompt_kv, tail_kv,
    )


MESH = pl.DeviceIdType.MESH
NCH = 2


def moe_kernel(
    meta_s,
    q16, tbias, mpart, lpart, opart, gain_ref, router_ref, ids_ref, tail_ref, kv_any, hid_any, wout_any, wg_any, wu_any, wd_any,
    mix, came, got,
    buf, head_v, hid_v, wout_v, wg_v, wu_v, wd_v,
    t1, t2, part, psib, psend, precv, stat, statr, dsend, drecv, xall, ypart, ysib, ysend, yrecv, rsend, rrecv, mvs, mvr, pickt, pick0, pick1,
    s_in, s_kv, s_t1, r_t1, s_t2, r_t2, s_ps, r_ps, s_px, r_px, s_st, r_st, s_d, r_d, s_gx, r_gx, s_gs, r_gs,
    s_ys, r_ys, s_yx, r_yx, s_r, r_r, s_mv, r_mv, s_ox, r_ox, s_os, r_os, s_cm, r_cm,
):
    r = lax.axis_index("req")
    t = lax.axis_index("tp")
    n_req = t1.shape[0]
    n_tp = mix.shape[0]
    n_x = n_tp // 2
    rows = hid_v.shape[0]
    width = wout_v.shape[1]
    crows = xall.shape[2]
    per = n_req // NCH
    cap = crows // per
    nslp = dsend.shape[0]
    capp = nslp // n_req
    c = lax.rem(t, 2)
    x = t // 2
    sib = x * 2 + 1 - c
    lanes = pl.ds(pl.multiple_of(t * 128, 128), 128)

    loads = [
        pltpu.make_async_copy(wout_any, wout_v, s_in.at[0]),
        pltpu.make_async_copy(hid_any.at[:, lanes], hid_v, s_in.at[1]),
        pltpu.make_async_copy(wg_any, wg_v, s_in.at[2]),
        pltpu.make_async_copy(wu_any, wu_v, s_in.at[3]),
        pltpu.make_async_copy(wd_any, wd_v, s_in.at[4]),
    ]
    nkv = rows // (TB * 8)

    def kv_load(i):
        sl = pl.ds(i * TB * 8, TB * 8)
        return pltpu.make_async_copy(kv_any.at[:, sl], buf.at[:, sl], s_kv.at[i])

    @pl.loop(0, nkv)
    def _(i):
        kv_load(i).start()

    for cp in loads:
        cp.start()

    def tp_copy(src, dst, ss, rs, peer):
        return pltpu.make_async_remote_copy(
            src_ref=src, dst_ref=dst, send_sem=ss, recv_sem=rs, device_id=(r, peer), device_id_type=MESH
        )

    def req_copy(src, dst, ss, rs, peer):
        return pltpu.make_async_remote_copy(
            src_ref=src, dst_ref=dst, send_sem=ss, recv_sem=rs, device_id=(peer, t), device_id_type=MESH
        )

    def xpeer(d):
        return lax.rem(x + d, n_x) * 2 + c

    def xfrom(d):
        return lax.rem(x + n_x - d, n_x) * 2 + c

    barrier = pltpu.get_barrier_semaphore()

    @pl.loop(1, n_tp)
    def _(d):
        pl.semaphore_signal(barrier, inc=1, device_id=(r, lax.rem(t + d, n_tp)), device_id_type=MESH)

    @pl.loop(1, n_req)
    def _(d):
        pl.semaphore_signal(barrier, inc=1, device_id=(lax.rem(r + d, n_req), t), device_id_type=MESH)

    sub16 = lax.broadcasted_iota(jnp.int32, (16, 128), 0)
    pair = lax.rem(sub16, 8) // 2
    lane4 = lax.broadcasted_iota(jnp.int32, (TB, 8, 128), 2)

    def tail_attention(i):
        kv_load(i).wait()
        rs = pl.ds(pl.multiple_of(i * TB * 16, TB * 16), TB * 16)
        scs = []
        for n in range(TB):
            b = i * TB + n
            kb = buf[0, pl.ds(b * 8, 8)].reshape(512, 128)
            qb = q16[pl.ds(pl.multiple_of(b * 16, 16), 16), :]
            s4 = lax.dot_general(qb, kb, (((1,), (1,)), ((), ())), preferred_element_type=F32)
            sc = s4[:, 0:128]
            for j in range(1, 4):
                sc = jnp.where(pair == j, s4[:, j * 128 : (j + 1) * 128], sc)
            scs.append(sc)
        sc = jnp.concatenate(scs, axis=0) + tbias[rs, :]
        mp = mpart[rs, :]
        mx = jnp.maximum(jnp.max(sc, axis=1, keepdims=True), mp)
        e = jnp.exp(sc - mx)
        ap = jnp.exp(mp - mx)
        tot = jnp.sum(e, axis=1, keepdims=True) + lpart[rs, :] * ap
        os = []
        for n in range(TB):
            b = i * TB + n
            vb = buf[1, pl.ds(b * 8, 8)].reshape(512, 128)
            en = e[n * 16 : (n + 1) * 16]
            p4 = jnp.concatenate([jnp.where(pair == j, en, 0.0) for j in range(4)], axis=1).astype(BF16)
            os.append(jnp.dot(p4, vb, preferred_element_type=F32))
        o = (jnp.concatenate(os, axis=0) + opart[rs, :] * ap) / tot
        o = o.reshape(TB, 2, 8, 128)
        o = jnp.where(lane4 < 64, o[:, 0], o[:, 1]).reshape(TB * 8, 128)
        head_v[pl.ds(pl.multiple_of(i * TB * 8, TB * 8), TB * 8), :] = o.astype(BF16)

    hrows = rows // 2

    def attn_part(h):
        head = head_v[h * hrows : (h + 1) * hrows, :]
        for tt in range(n_tp):
            part[h, tt % 2, tt // 2] = jnp.dot(
                head, wout_v[:, tt * 128 : (tt + 1) * 128], preferred_element_type=F32
            ).astype(BF16)

    pl.loop(0, nkv // 2)(tail_attention)
    loads[0].wait()
    attn_part(0)
    pl.semaphore_wait(barrier, n_tp - 1 + n_req - 1)

    def rs_sib(d, buf, dst, ss, rs):
        xx = lax.rem(x + d, n_x)
        return tp_copy(buf.at[1 - c, xx], dst.at[xx], ss.at[d], rs.at[d], sib)

    def rs_x(d, buf, dst, ss, rs):
        return tp_copy(buf.at[d], dst.at[d], ss.at[d], rs.at[d], xpeer(d))

    def rs_start(buf, bsib, ss1, rs1):
        for d in (2, 1, 3, 0):
            rs_sib(d, buf, bsib, ss1, rs1).start()

    def rs_send(buf, bsib, bsend, brecv, ss1, rs1, ss2, rs2):
        for d in (2, 1, 3):
            xx = lax.rem(x + d, n_x)
            rs_sib(d, buf, bsib, ss1, rs1).wait_recv()
            bsend[d] = (buf[c, xx].astype(F32) + bsib[xx].astype(F32)).astype(BF16)
            rs_x(d, bsend, brecv, ss2, rs2).start()

    def rs_total(buf, bsib, bsend, brecv, ss1, rs1, ss2, rs2):
        rs_sib(0, buf, bsib, ss1, rs1).wait_recv()
        tot = buf[c, x].astype(F32) + bsib[x].astype(F32)
        for d in (1, 3, 2):
            rs_x(d, bsend, brecv, ss2, rs2).wait_recv()
            tot = tot + brecv[d].astype(F32)
        return tot

    def rs_finish(buf, bsib, bsend, brecv, ss1, rs1, ss2, rs2):
        for d in (0, 1, 2, 3):
            rs_sib(d, buf, bsib, ss1, rs1).wait_send()
        for d in (1, 2, 3):
            rs_x(d, bsend, brecv, ss2, rs2).wait_send()

    def ag_x(d, buf, ss, rs):
        return tp_copy(buf.at[t], buf.at[t], ss.at[d], rs.at[d], xpeer(d))

    def ag_s(d, buf, ss, rs):
        who = xfrom(d)
        return tp_copy(buf.at[who], buf.at[who], ss.at[d], rs.at[d], sib)

    def ag_start(buf, ss1, rs1, ss2, rs2):
        for d in (2, 1, 3):
            ag_x(d, buf, ss1, rs1).start()
        ag_s(0, buf, ss2, rs2).start()

    def ag_left(buf, ss1, rs1, ss2, rs2):
        for d in (2, 1, 3):
            ag_x(d, buf, ss1, rs1).wait_send()

    def ag_pass(buf, ss1, rs1, ss2, rs2):
        for d in (1, 3, 2):
            who = xfrom(d)
            tp_copy(buf.at[who], buf.at[who], ss1.at[d], rs1.at[d], xpeer(d)).wait_recv()
            ag_s(d, buf, ss2, rs2).start()

    def ag_wait(buf, ss1, rs1, ss2, rs2):
        for d in (0, 1, 3, 2):
            mine = xfrom(d)
            other = lax.rem(x + n_x - d, n_x) * 2 + 1 - c
            tp_copy(buf.at[mine], buf.at[other], ss2.at[d], rs2.at[d], sib).wait_recv()

    def ag_finish(buf, ss1, rs1, ss2, rs2, left=False):
        if not left:
            ag_left(buf, ss1, rs1, ss2, rs2)
        for d in (0, 1, 2, 3):
            ag_s(d, buf, ss2, rs2).wait_send()

    def attn_rs(h):
        return (
            part.at[h], psib.at[h], psend.at[h], precv.at[h], s_ps.at[h], r_ps.at[h], s_px.at[h], r_px.at[h]
        )

    rs_start(part.at[0], psib.at[0], s_ps.at[0], r_ps.at[0])
    pl.loop(nkv // 2, nkv // 4 * 3)(tail_attention)
    rs_send(*attn_rs(0))
    pl.loop(nkv // 4 * 3, nkv)(tail_attention)
    attn_part(1)
    rs_start(part.at[1], psib.at[1], s_ps.at[1], r_ps.at[1])
    rs_send(*attn_rs(1))

    def t1_copy(d):
        j = lax.rem(r + d, n_req)
        return req_copy(tail_ref.at[j], t1.at[r], s_t1.at[d], r_t1.at[d], j)

    lnf = lax.broadcasted_iota(jnp.int32, (rows, 128), 1).astype(F32)
    e0 = col_form(ids_ref[0:1, :])
    e1 = col_form(ids_ref[1:2, :])
    hit0 = lnf == e0
    hit1 = lnf == e1
    lower = lax.broadcasted_iota(jnp.int32, (rows, rows), 1) < lax.broadcasted_iota(jnp.int32, (rows, rows), 0)
    lower = lower.astype(F32).astype(BF16)
    o0 = hit0.astype(F32)
    o1 = hit1.astype(F32)
    cum0 = jnp.dot(lower, o0.astype(BF16), preferred_element_type=F32)
    cum1 = jnp.dot(lower, o1.astype(BF16), preferred_element_type=F32)
    tot0 = jnp.sum(o0, axis=0, keepdims=True)
    s0 = e0 * float(capp) + jnp.sum(jnp.where(hit0, cum0, 0.0), axis=1, keepdims=True)
    s1 = e1 * float(capp) + jnp.sum(jnp.where(hit1, cum1 + tot0, 0.0), axis=1, keepdims=True)
    row0 = jnp.transpose(s0)[0:1]
    row1 = jnp.transpose(s1)[0:1]
    sl = lax.broadcasted_iota(jnp.int32, (128, rows), 0).astype(F32)
    for k in range(nslp // 128):
        here = sl + float(k * 128)
        pickt[k * 128 : (k + 1) * 128, :] = ((here == row0) | (here == row1)).astype(F32).astype(BF16)
    loads[1].wait()
    attn = jnp.concatenate([rs_total(*attn_rs(h)) for h in range(2)], axis=0)
    resid = (hid_v[...].astype(F32) + attn).astype(BF16)

    dsend[...] = jnp.dot(pickt[...], resid, preferred_element_type=F32).astype(BF16)

    def block(j):
        return pl.ds(pl.multiple_of(j * capp, 16), capp)

    def d_copy(d):
        j = lax.rem(r + d, n_req)
        return req_copy(dsend.at[block(j)], drecv.at[block(r)], s_d.at[d], r_d.at[d], j)

    @pl.loop(1, n_req)
    def _(d):
        d_copy(d).start()

    drecv[block(r), :] = dsend[block(r), :]


    rf = resid.astype(F32)
    u = rf * gain_ref[:, lanes]
    lg = lax.dot_general(
        u.astype(BF16), router_ref[:, lanes], (((1,), (1,)), ((), ())), preferred_element_type=F32
    )
    n_e = lg.shape[1]
    ex = lnf[:, 0:n_e]
    diff = jnp.sum(
        jnp.where(ex == e0[:, 0:n_e], lg, 0.0) - jnp.where(ex == e1[:, 0:n_e], lg, 0.0), axis=1, keepdims=True
    )
    sq = jnp.sum(rf * rf, axis=1, keepdims=True)
    stat[...] = jnp.transpose(jnp.where(lnf == 0.0, sq, jnp.where(lnf == 1.0, diff, 0.0)))[0:8]

    def st_copy(d):
        return tp_copy(stat, statr.at[d], s_st.at[d], r_st.at[d], lax.rem(t + d, n_tp))

    for d in range(1, n_tp):
        st_copy(d).start()

    @pl.loop(1, n_req)
    def _(d):
        d_copy(d).wait_recv()

    def x_ag(h):
        return (xall.at[h], s_gx.at[h], r_gx.at[h], s_gs.at[h], r_gs.at[h])

    for h in range(NCH):
        xall[h, t] = jnp.concatenate(
            [drecv[j * capp : (j + 1) * capp, :].astype(F32)[0:cap] for j in range(h * per, (h + 1) * per)], axis=0
        ).astype(BF16)
        ag_start(*x_ag(h))

    @pl.loop(1, n_req)
    def _(d):
        t1_copy(d).start()

    t1[r] = tail_ref[r]

    tot = stat[...]
    for d in range(1, n_tp):
        st_copy(d).wait_recv()
        tot = tot + statr[d]
    tot = jnp.transpose(jnp.concatenate([tot, jnp.zeros((120, rows), F32)], axis=0))
    gate = jax.nn.sigmoid(tot[:, 1:2] * lax.rsqrt(tot[:, 0:1] * (1.0 / width) + EPS))

    for cp in loads[2:]:
        cp.wait()

    def ffn(h):
        xm = jnp.concatenate([xall[h, tt] for tt in range(n_tp)], axis=1).astype(F32)
        ms = jnp.mean(xm * xm, axis=-1, keepdims=True)
        nm = (xm * lax.rsqrt(ms + EPS) * gain_ref[...]).astype(BF16)
        gh = lax.dot_general(nm, wg_v[...], (((1,), (1,)), ((), ())), preferred_element_type=F32)
        uh = lax.dot_general(nm, wu_v[...], (((1,), (1,)), ((), ())), preferred_element_type=F32)
        act = (jax.nn.gelu(gh, approximate=True) * uh).astype(BF16)
        y = jnp.dot(act, wd_v[...], preferred_element_type=F32).astype(BF16)
        for tt in range(n_tp):
            ypart[h, tt % 2, tt // 2] = y[:, tt * 128 : (tt + 1) * 128]

    def y_rs(h):
        return (
            ypart.at[h], ysib.at[h], ysend.at[h], yrecv.at[h], s_ys.at[h], r_ys.at[h], s_yx.at[h], r_yx.at[h]
        )

    ag_pass(*x_ag(0))
    for h in range(NCH):
        ag_wait(*x_ag(h))
        ffn(h)
        rs_start(ypart.at[h], ysib.at[h], s_ys.at[h], r_ys.at[h])
        if h + 1 < NCH:
            ag_pass(*x_ag(h + 1))
        rs_send(*y_rs(h))

    @pl.loop(1, n_req)
    def _(d):
        t1_copy(d).wait_recv()

    @pl.loop(0, n_req)
    def _(j):
        t2[j] = t1[meta_s[1, j]]

    def t2_copy(d):
        j = lax.rem(r + d, n_req)
        return req_copy(t2.at[j], got.at[r], s_t2.at[d], r_t2.at[d], j)

    @pl.loop(1, n_req)
    def _(d):
        t2_copy(d).start()

    got[r] = t2[r]

    def r_copy(d):
        j = lax.rem(r + d, n_req)
        return req_copy(rsend.at[block(j)], rrecv.at[block(r)], s_r.at[d], r_r.at[d], j)

    pad = jnp.zeros((capp - cap, 128), F32)
    for h in range(NCH):
        tot = rs_total(*y_rs(h))
        for i in range(per):
            j = h * per + i
            rsend[j * capp : (j + 1) * capp, :] = jnp.concatenate(
                [tot[i * cap : (i + 1) * cap], pad], axis=0
            ).astype(BF16)

        @pl.loop(h * per, (h + 1) * per)
        def _(j):
            @pl.when(j != r)
            def _():
                r_copy(lax.rem(j + n_req - r, n_req)).start()

    rrecv[block(r), :] = rsend[block(r), :]

    for k in range(nslp // 128):
        here = lnf + float(k * 128)
        pick0[:, k * 128 : (k + 1) * 128] = (s0 == here).astype(F32).astype(BF16)
        pick1[:, k * 128 : (k + 1) * 128] = (s1 == here).astype(F32).astype(BF16)

    @pl.loop(1, n_req)
    def _(d):
        r_copy(d).wait_recv()

    p0 = jnp.dot(pick0[...], rrecv[...], preferred_element_type=F32)
    p1 = jnp.dot(pick1[...], rrecv[...], preferred_element_type=F32)
    mixed = (rf + gate * p0 + (1.0 - gate) * p1).astype(BF16)

    kk = lax.broadcasted_iota(jnp.int32, (16, rows), 0)
    rr = lax.broadcasted_iota(jnp.int32, (16, rows), 1)
    pick = jnp.zeros((16, rows), F32)
    for k in range(MIG):
        pick = jnp.where((kk == k) & (rr == meta_s[0, k]), 1.0, pick)
    mvs[...] = jnp.dot(pick.astype(BF16), mixed, preferred_element_type=F32).astype(BF16)

    def mv_copy(d):
        j = lax.rem(r + d, n_req)
        return req_copy(mvs, mvr.at[r], s_mv.at[d], r_mv.at[d], j)

    mix[t] = mixed
    o_ag = (mix, s_ox, r_ox, s_os, r_os)
    ag_start(*o_ag)

    @pl.loop(1, n_req)
    def _(d):
        mv_copy(d).start()

    mvr[r] = mvs[...]

    for h in range(2):
        rs_finish(*attn_rs(h))
    for h in range(NCH):
        rs_finish(*y_rs(h))
        ag_finish(*x_ag(h), left=False)
    for d in range(1, n_tp):
        st_copy(d).wait_send()

    @pl.loop(1, n_req)
    def _(d):
        t1_copy(d).wait_send()
        d_copy(d).wait_send()
        t2_copy(d).wait_send()
        r_copy(d).wait_send()

    def cm_copy(d):
        return tp_copy(came.at[t], came.at[t], s_cm.at[d], r_cm.at[d], lax.rem(t + d, n_tp))

    @pl.loop(1, n_req)
    def _(d):
        mv_copy(d).wait_recv()

    came[t] = mvr[meta_s[1, r]]
    for d in range(1, n_tp):
        cm_copy(d).start()

    ag_pass(*o_ag)
    ag_wait(*o_ag)
    for d in range(1, n_tp):
        who = lax.rem(t + n_tp - d, n_tp)
        tp_copy(came.at[who], came.at[who], s_cm.at[d], r_cm.at[d], who).wait_recv()

    @pl.loop(1, n_req)
    def _(d):
        t2_copy(d).wait_recv()

    ag_finish(*o_ag)
    for d in range(1, n_tp):
        cm_copy(d).wait_send()

    @pl.loop(1, n_req)
    def _(d):
        mv_copy(d).wait_send()


def moe_call(n_req, n_tp, meta, parts, gain, router_t, ids_t, send_tail, tail, hidden, w_out, wg_t, wu_t, wd):
    rows, width = hidden.shape
    cap = 5 * rows * TOP // (4 * n_req)
    nsl = n_req * cap
    crows = nsl // NCH
    nslp = n_req * slot_stride(cap)
    chunk = send_tail.shape[1]
    smem = pl.BlockSpec(memory_space=pltpu.SMEM)
    vmem = pl.BlockSpec(memory_space=pltpu.VMEM)
    anym = pl.BlockSpec(memory_space=pl.ANY)
    dma = pltpu.SemaphoreType.DMA
    n_x = n_tp // 2

    def bf(*shape):
        return pltpu.VMEM(shape, BF16)

    return pl.pallas_call(
        moe_kernel,
        out_shape=(
            jax.ShapeDtypeStruct((n_tp, rows, 128), BF16),
            jax.ShapeDtypeStruct((n_tp, 16, 128), BF16),
            jax.ShapeDtypeStruct((n_req, chunk, 128), BF16),
        ),
        in_specs=[smem] + [vmem] * 9 + [anym] * 6,
        out_specs=(vmem, vmem, vmem),
        scratch_shapes=[
            bf(*tail.shape), bf(rows, 128), bf(rows, 128), bf(*w_out.shape), bf(*wg_t.shape), bf(*wu_t.shape), bf(*wd.shape),
            bf(n_req, chunk, 128), bf(n_req, chunk, 128),
            bf(2, 2, n_x, rows // 2, 128), bf(2, n_x, rows // 2, 128), bf(2, n_x, rows // 2, 128),
            bf(2, n_x, rows // 2, 128),
            pltpu.VMEM((8, rows), F32), pltpu.VMEM((n_tp, 8, rows), F32),
            bf(nslp, 128), bf(nslp, 128), bf(NCH, n_tp, crows, 128),
            bf(NCH, 2, n_x, crows, 128), bf(NCH, n_x, crows, 128), bf(NCH, n_x, crows, 128), bf(NCH, n_x, crows, 128),
            bf(nslp, 128), bf(nslp, 128),
            bf(16, 128), bf(n_req, 16, 128), bf(nslp, rows), bf(rows, nslp), bf(rows, nslp),
        ]
        + [dma((5,))]
        + [dma((rows // (TB * 8),))]
        + [dma((n_req,))] * 4
        + [dma((2, n_x))] * 4
        + [dma((n_tp,))] * 2
        + [dma((n_req,))] * 2
        + [dma((NCH, n_x))] * 8
        + [dma((n_req,))] * 4
        + [dma((n_x,))] * 4
        + [dma((n_tp,))] * 2,
        compiler_params=pltpu.CompilerParams(collective_id=0, has_side_effects=True, vmem_limit_bytes=56 << 20),
        name="moe_exchange",
    )(meta, *parts, gain.reshape(1, -1), router_t, ids_t, send_tail, tail, hidden, w_out, wg_t, wu_t, wd)


def place_kernel(meta_s, mix_ref, came_ref, got_ref, tail_in, out_ref, tail_out, sems):
    rows = tail_out.shape[1]

    def put(k, kv):
        return pltpu.make_async_copy(got_ref.at[k, kv], tail_out.at[kv, meta_s[0, MIG + k]], sems.at[k, kv])

    for k in range(MIG):
        for kv in range(2):

            @pl.when(meta_s[0, MIG + k] < rows)
            def _():
                put(k, kv).start()

    for tt in range(mix_ref.shape[0]):
        out_ref[:, tt * 128 : (tt + 1) * 128] = mix_ref[tt]
    sub = lax.broadcasted_iota(jnp.int32, (16, 128), 0)
    for k in range(MIG):
        slot = meta_s[0, MIG + k]

        @pl.when(slot < rows)
        def _():
            base = pl.multiple_of((slot >> 4) << 4, 16)
            for tt in range(mix_ref.shape[0]):
                cols = slice(tt * 128, (tt + 1) * 128)
                row = came_ref[tt].astype(F32)[k : k + 1, :]
                w = out_ref[pl.ds(base, 16), cols].astype(F32)
                out_ref[pl.ds(base, 16), cols] = jnp.where(sub == slot - base, row, w).astype(BF16)

    for k in range(MIG):
        for kv in range(2):

            @pl.when(meta_s[0, MIG + k] < rows)
            def _():
                put(k, kv).wait()


def place_call(meta, mix, came, got, tail):
    n_tp, rows, wd = mix.shape
    vmem = pl.BlockSpec(memory_space=pltpu.VMEM)
    return pl.pallas_call(
        place_kernel,
        out_shape=(
            jax.ShapeDtypeStruct((rows, n_tp * wd), BF16),
            jax.ShapeDtypeStruct(tail.shape, tail.dtype),
        ),
        in_specs=[pl.BlockSpec(memory_space=pltpu.SMEM), vmem, vmem, vmem, pl.BlockSpec(memory_space=pl.ANY)],
        out_specs=(vmem, pl.BlockSpec(memory_space=pl.ANY)),
        scratch_shapes=[pltpu.SemaphoreType.DMA((MIG, 2))],
        input_output_aliases={4: 1},
        name="place_rows",
    )(meta, mix, came, got, tail)


def body(
    hidden_in, prompt_kv, tail_kv, group_of, prompt_len, tail_len, bucket_of, bias_table, attn_gain, w_query, w_key,
    w_value, w_out, ffn_gain, router_weight, expert_ids, w_gate, w_up, w_down, new_slot,
):
    n_req = lax.axis_size("req")
    n_tp = lax.axis_size("tp")
    ids_t = expert_ids.T
    tail_new, send_tail, meta, *parts = attention_call(
        hidden_in, attn_gain, w_query, w_key, w_value, group_of, prompt_len, tail_len, bucket_of, bias_table.T,
        new_slot, prompt_kv, tail_kv,
    )
    pieces = send_tail.reshape(n_req, -1, send_tail.shape[-1])
    mix, came, got = moe_call(
        n_req, n_tp, meta, parts, ffn_gain, router_weight.T, ids_t, pieces, tail_new, hidden_in, w_out,
        w_gate[0].T, w_up[0].T, w_down[0],
    )
    return place_call(meta, mix, came, got.reshape(send_tail.shape), tail_new)


def solution(mesh):
    return jax.shard_map(
        body,
        mesh=mesh,
        in_specs=(
            P("req", None), P(None, "req", None, "tp"), P(None, "req", None, "tp"), P("req"), P("req"), P("req"), P(),
            P(None, "tp"), P(), P(None, "tp"), P(None, "tp"), P(None, "tp"), P("tp", None), P(), P(), P("req", None),
            P("req", None, "tp"), P("req", None, "tp"), P("req", "tp", None), P(),
        ),
        out_specs=(P("req", None), P(None, "req", None, "tp")),
        check_vma=False,
    )
```
